32 devices in a mesh: fsdp: 32 (over z, y, x, core).
Axes of the slice: x: 2, y: 2, z: 4, core: 2. Of those that a mesh axis runs over, the one named last changes fastest.
Arguments:
- layer_in: bfloat16 [2, 16384, 512], P(None, 'fsdp'), may hold values from -6 to 6
- out_grad: bfloat16 [2, 16384, 512], P(None, 'fsdp'), may hold values from -6 to 6
- lengths: int32 [2, 8], replicated, may hold values from 1024 to 8192, as said below
- group_order: int32 [2, 32], replicated, may hold values from 0 to 31, each once within a row
- w_query: bfloat16 [512, 512], P('fsdp'), may hold values from -0.25 to 0.25
- w_key: bfloat16 [512, 512], P('fsdp'), may hold values from -0.25 to 0.25
- w_value: bfloat16 [512, 512], P('fsdp'), may hold values from -0.25 to 0.25
- w_out: bfloat16 [512, 512], P('fsdp'), may hold values from -6 to 6
- w_in: bfloat16 [512, 2048], P('fsdp'), may hold values from -0.25 to 0.25
- w_back: bfloat16 [2048, 512], P('fsdp'), may hold values from -0.125 to 0.125
- norm_gain: bfloat16 [2, 512], P(None, 'fsdp'), may hold values from 0.5 to 1.5
- norm_shift: bfloat16 [2, 512], P(None, 'fsdp'), may hold values from -1.5 to 1.5
- ffn_bias_in: bfloat16 [2048], P('fsdp'), may hold values from -1.5 to 1.5
- ffn_bias_out: bfloat16 [512], P('fsdp'), may hold values from -1.5 to 1.5
Outputs:
- layer_out: bfloat16 [2, 16384, 512], P(None, 'fsdp')
- in_grad: float32 [2, 16384, 512], P(None, 'fsdp')
- grad_query: float32 [512, 512], P('fsdp')
- grad_key: float32 [512, 512], P('fsdp')
- grad_value: float32 [512, 512], P('fsdp')
- grad_out: float32 [512, 512], P('fsdp')
- grad_in: float32 [512, 2048], P('fsdp')
- grad_back: float32 [2048, 512], P('fsdp')
- grad_norm_gain: float32 [2, 512], P(None, 'fsdp')
- grad_norm_shift: float32 [2, 512], P(None, 'fsdp')
- grad_bias_in: float32 [2048], P('fsdp')
- grad_bias_out: float32 [512], P('fsdp')
The draws below stay inside these ranges and needn't reach their ends.
Inputs may be any that keep to these rules, and one draw needn't show every extreme that they name: `lengths`: every length is a multiple of 256; each row sums to 16384 and holds one length of exactly 8192. `group_order`: each row is a permutation of the groups of a micro-batch.
All inputs are finite; a program needn't handle non-finite values.
Results may differ from the reference program's by a relative error of at most 0.012.
Values may be sent and summed in bfloat16 or wider, within the bound.
No kernel may reach another device: no remote copies, remote signals or barrier semaphores. Data moves between devices by JAX's collectives and lax.ppermute only.
A program may use at most 448 MiB of HBM per device.

```python
import math
import jax
import jax.numpy as jnp
from jax import lax

D = 512
HEADS = 8
HEAD_DIM = 64
FF = 2048
BLOCK = 16
LEVELS = 9
MINLEN = 1024
MB = 2
GROUP = 512
UNIT = 256
MAXLEN = 8192
STREAM = 16384
NSEQ = 8
N_FSDP = 32


def draw_lengths(key, part):
    least = MINLEN // UNIT
    longest = MAXLEN // UNIT
    total_units = STREAM // UNIT
    others = NSEQ - 1
    spare = total_units - NSEQ * least - (longest - least)
    rows_out = []
    for micro_id in range(MB):
        sub_key = jax.random.fold_in(key, 11 + micro_id)
        first_key, second_key = jax.random.split(sub_key)
        shares = jax.random.randint(first_key, (others,), 1, 8)
        extra = spare * shares // jnp.sum(shares)
        leftover = spare - jnp.sum(extra)
        extra = extra + (jnp.arange(others) < leftover).astype(jnp.int32)
        units = jnp.concatenate([jnp.full((1,), longest, jnp.int32), (least + extra).astype(jnp.int32)])
        units = jax.random.permutation(second_key, units)
        rows_out.append(units * UNIT)
    return jnp.stack(rows_out).astype(jnp.int32)


def steps_of(rng, extent, pieces, low, largest):
    def one(dim, blocks):
        draws = jax.random.uniform(jax.random.fold_in(jax.random.fold_in(rng, 6), dim), (blocks,), jnp.float32, low / len(pieces), largest / len(pieces))
        return jnp.repeat(jnp.exp(draws), extent[dim] // blocks).reshape((-1,) + (1,) * (len(extent) - dim - 1))

    gain = one(*pieces[0])
    for cut in pieces[1:]:
        gain = gain * one(*cut)
    return gain


def gaussian(own_key, extent, scale, limit, cuts=(), held_as=jnp.bfloat16):
    gain = steps_of(own_key, extent, cuts, -0.22, 0.18) if cuts else 1.0
    values = jax.random.normal(own_key, extent, jnp.float32) * scale * gain
    return jnp.minimum(jnp.maximum(values, -limit), limit).astype(held_as)


def setup_inputs(seed: int = 0) -> dict:
    splits = jax.random.split(jax.random.key(seed), 15)
    return {
        "layer_in": gaussian(splits[0], (MB, STREAM, D), 1.0, 6.0, ((1, 32),)),
        "out_grad": gaussian(splits[1], (MB, STREAM, D), 1.0, 6.0, ((1, 32),)),
        "lengths": draw_lengths(jax.random.fold_in(splits[14], 71), 0),
        "group_order": jax.vmap(lambda own: jax.random.permutation(own, N_FSDP))(jax.random.split(splits[3], MB)).reshape((MB, N_FSDP)).astype(jnp.int32),
        "w_query": gaussian(splits[4], (D, D), D ** -0.5, 0.25, ((0, 32),)),
        "w_key": gaussian(splits[5], (D, D), D ** -0.5, 0.25, ((0, 32),)),
        "w_value": gaussian(splits[6], (D, D), D ** -0.5, 0.25, ((0, 32),)),
        "w_out": gaussian(splits[7], (D, D), 1 ** -0.5, 6.0, ((0, 32),)),
        "w_in": gaussian(splits[8], (D, FF), D ** -0.5, 0.25, ((0, 32),)),
        "w_back": gaussian(splits[9], (FF, D), FF ** -0.5, 0.125, ((0, 32),)),
        "norm_gain": jnp.clip(1.0 + 0.1 * jax.random.normal(splits[10], (2, D), jnp.float32), 0.5, 1.5).astype(jnp.bfloat16),
        "norm_shift": gaussian(splits[11], (2, D), 0.3, 1.5, ((1, 32),)),
        "ffn_bias_in": gaussian(splits[12], (FF,), 0.3, 1.5, ((0, 32),)),
        "ffn_bias_out": gaussian(splits[13], (D,), 0.3, 1.5, ((0, 32),)),
    }


HIGHEST = lax.Precision.HIGHEST
EPSILON = 1e-05

@jax.custom_vjp
def low(v):
    return lax.optimization_barrier(v.astype(jnp.bfloat16)).astype(jnp.float32)

@jax.custom_vjp
def low_back(v):
    return v

def low_keep(v):
    return (low(v), None)

def low_pass(kept, grad):
    return (grad,)

def back_keep(v):
    return (v, None)

def back_low(kept, grad):
    return (low(grad),)
low.defvjp(low_keep, low_pass)
low_back.defvjp(back_keep, back_low)

def norm_rows(values, gain_row, shift_row):
    centre = lax.optimization_barrier(jnp.mean(values, axis=-1, keepdims=True))
    centred = values - centre
    spread = lax.optimization_barrier(jnp.mean(centred * centred, axis=-1, keepdims=True))
    return centred * lax.rsqrt(spread + EPSILON) * gain_row + shift_row

def coarsen(values, factor):
    return lax.optimization_barrier(jnp.mean(values.reshape((values.shape[0] // factor, factor) + values.shape[1:]), axis=1))

def diagonal_terms(queries, keys_in, values_in, seq_ids):
    blocks = queries.shape[0] // BLOCK
    heads_n, head_width = (queries.shape[1], queries.shape[2])
    shape4 = (blocks, BLOCK, heads_n, head_width)
    scores = jnp.einsum('bqhe,bkhe->bqkh', queries.reshape(shape4), keys_in.reshape(shape4), precision=HIGHEST) / math.sqrt(head_width)
    seq_b = seq_ids.reshape(blocks, BLOCK)
    same_seq = (seq_b[:, :, None] == seq_b[:, None, :])[..., None]
    weights = jnp.where(same_seq, jnp.exp(scores), 0.0)
    numerator = jnp.einsum('bqkh,bkhe->bqhe', weights, values_in.reshape(shape4), precision=HIGHEST)
    denominator = lax.optimization_barrier(jnp.sum(weights, axis=2))
    return (numerator.reshape(blocks * BLOCK, heads_n, head_width), denominator.reshape(blocks * BLOCK, heads_n))

def sibling_terms(queries, keys_in, values_in, seq_ids, factor):
    pairs_n = queries.shape[0] // (2 * BLOCK)
    heads_n, head_width = (queries.shape[1], queries.shape[2])
    shape5 = (pairs_n, 2, BLOCK, heads_n, head_width)
    key_p = keys_in.reshape(shape5)[:, ::-1]
    value_p = values_in.reshape(shape5)[:, ::-1]
    seq_p = seq_ids.reshape(pairs_n, 2, BLOCK)
    seq_s = seq_p[:, ::-1]
    scores = jnp.einsum('bpqhe,bpkhe->bpqkh', queries.reshape(shape5), key_p, precision=HIGHEST) / math.sqrt(head_width)
    same_seq = (seq_p[:, :, :, None] == seq_s[:, :, None, :])[..., None]
    weights = jnp.where(same_seq, factor * jnp.exp(scores), 0.0)
    numerator = jnp.einsum('bpqkh,bpkhe->bpqhe', weights, value_p, precision=HIGHEST)
    denominator = lax.optimization_barrier(jnp.sum(weights, axis=3))
    total = pairs_n * 2 * BLOCK
    return (numerator.reshape(total, heads_n, head_width), denominator.reshape(total, heads_n))

def attention(queries, keys_in, values_in, seq_ids):
    numerator, denominator = diagonal_terms(queries, keys_in, values_in, seq_ids)
    for level_id in range(1, LEVELS + 1):
        factor = 2 ** (level_id - 1)
        coarse_q = coarsen(queries, factor)
        coarse_k = coarsen(keys_in, factor)
        coarse_v = coarsen(values_in, factor)
        if 2 * BLOCK * factor > GROUP:
            coarse_k = low(coarse_k)
            coarse_v = low(coarse_v)
        part_n, part_d = sibling_terms(coarse_q, coarse_k, coarse_v, seq_ids[::factor], float(factor))
        numerator = numerator + jnp.repeat(part_n, factor, axis=0)
        denominator = denominator + jnp.repeat(part_d, factor, axis=0)
    return numerator / denominator[..., None]

def block_forward(stream_x, seq_ids, params):
    w_q, w_k, w_v, w_o, w_up, w_down, gains, shifts, bias_up, bias_down = params
    tokens_n = stream_x.shape[0]
    shape3 = (tokens_n, HEADS, HEAD_DIM)
    normed = low(norm_rows(stream_x, gains[0], shifts[0]))
    queries = low_back(low(jnp.dot(normed, w_q, precision=HIGHEST)))
    keys_in = low_back(low(jnp.dot(normed, w_k, precision=HIGHEST)))
    values_in = low_back(low(jnp.dot(normed, w_v, precision=HIGHEST)))
    attended = attention(queries.reshape(shape3), keys_in.reshape(shape3), values_in.reshape(shape3), seq_ids)
    attended = low(attended.reshape(tokens_n, D))
    mixed_rows = stream_x + low_back(jnp.dot(attended, w_o, precision=HIGHEST))
    normed_two = low(norm_rows(mixed_rows, gains[1], shifts[1]))
    pre_act = low_back(jnp.dot(normed_two, w_up, precision=HIGHEST)) + bias_up
    hidden = low(jax.nn.gelu(pre_act, approximate=False))
    return mixed_rows + low_back(jnp.dot(hidden, w_down, precision=HIGHEST)) + bias_down

def to_stream(array, group_map):
    groups = array.reshape((N_FSDP, GROUP) + array.shape[1:])
    return jnp.zeros_like(groups).at[group_map].set(groups).reshape(array.shape)

def to_dealt(array, group_map):
    groups = array.reshape((N_FSDP, GROUP) + array.shape[1:])
    return groups[group_map].reshape(array.shape)

def seq_lookup(positions, seq_ends):
    return lax.optimization_barrier(jnp.sum((positions[:, None] >= seq_ends[None, :]).astype(jnp.int32), axis=1))

def reference(layer_in, out_grad, lengths, group_order, w_query, w_key, w_value, w_out, w_in, w_back, norm_gain, norm_shift, ffn_bias_in, ffn_bias_out):
    params = tuple((p_arr.astype(jnp.float32) for p_arr in (w_query, w_key, w_value, w_out, w_in, w_back, norm_gain, norm_shift, ffn_bias_in, ffn_bias_out)))
    inputs = layer_in.astype(jnp.float32)
    positions = jnp.arange(STREAM, dtype=jnp.int32)
    streams = [to_stream(inputs[micro_id], group_order[micro_id]) for micro_id in range(MB)]
    seq_list = [seq_lookup(positions, jnp.cumsum(lengths[micro_id], dtype=jnp.int32)) for micro_id in range(MB)]

    def forward(stream_list, param_list):
        return [block_forward(stream_list[micro_id], seq_list[micro_id], param_list) for micro_id in range(MB)]
    outputs, pullback = jax.vjp(forward, streams, params)
    cotangents = [to_stream(out_grad[micro_id].astype(jnp.float32), group_order[micro_id]) for micro_id in range(MB)]
    grad_streams, grad_params = pullback(cotangents)
    layer_out = jnp.stack([to_dealt(outputs[micro_id], group_order[micro_id]) for micro_id in range(MB)]).astype(jnp.bfloat16)
    in_grad = jnp.stack([to_dealt(grad_streams[micro_id], group_order[micro_id]) for micro_id in range(MB)])
    return (layer_out, in_grad, grad_params[0], grad_params[1], grad_params[2], grad_params[3], grad_params[4], grad_params[5], grad_params[6], grad_params[7], grad_params[8], grad_params[9])
```

```python
import math

import jax
import jax.numpy as jnp
import numpy as np
from jax import lax
from jax.experimental import pallas as pl
from jax.experimental.pallas import tpu as pltpu
from jax.sharding import PartitionSpec as P

HEADS = 8
HEAD_DIM = 64
BLOCK = 16
LEVELS = 9
EPSILON = 1e-05
OFF = -1e30
PAIRS = HEADS // 2
WIDE = 2 * HEAD_DIM
SCALE2 = math.log2(math.e) / math.sqrt(HEAD_DIM)
SCALE = 1.0 / math.sqrt(HEAD_DIM)
BF = jnp.bfloat16
F32 = jnp.float32
VMEM_LIMIT = 58 * 2**20
SIBS = 15


def coarse_offsets(length):
    offsets = {}
    row = 0
    for level_id in range(2, LEVELS + 1):
        factor = 2 ** (level_id - 1)
        offsets[factor] = row
        row += length // factor
    return offsets


def pool_matrix(length):
    matrix = np.zeros((length, length), np.float32)
    for factor, row in coarse_offsets(length).items():
        for i in range(length // factor):
            matrix[row + i, i * factor : (i + 1) * factor] = 1.0 / factor
    return matrix


def tile_bias(kind):
    rows = np.arange(128)
    keys = np.arange(256) % 128
    block_r = rows[:, None] // BLOCK
    block_k = keys[None, :] // BLOCK
    bias = np.full((128, 256), OFF, np.float32)
    if kind == "fine":
        bias[block_r // 2 == block_k // 2] = 0.0
    elif kind == "two":
        bias[block_r == (block_k ^ 1)] = 1.0
    elif kind == "four":
        bias[block_r == (block_k ^ 1)] = 2.0
    else:
        sibling = block_r == (block_k ^ 1)
        bias[sibling & (rows[:, None] < 64)] = 3.0
        if kind == "joined":
            bias[sibling & (rows[:, None] >= 64) & (rows[:, None] < 96)] = 4.0
    return bias


def sibling_select(mean):
    matrix = np.zeros((64, 256), np.float32)
    first = 0
    for level in range(4):
        span = 2**level
        per = BLOCK // span
        for j in range(BLOCK):
            row = (first + j // per) * BLOCK + (j % per) * span
            matrix[level * BLOCK + j, row : row + span] = 1.0 / span if mean else 1.0
        first += span
    return matrix


def pair_columns():
    matrix = np.zeros((HEADS * HEAD_DIM, 128), np.float32)
    for h in range(HEADS):
        col = 8 * (h // 2) + 2 * (h % 2)
        matrix[h * HEAD_DIM : (h + 1) * HEAD_DIM, col : col + 2] = 1.0
    return matrix


def minus_columns():
    matrix = np.zeros((PAIRS, 256, 128), np.float32)
    for p in range(PAIRS):
        matrix[p, :128, 8 * p : 8 * p + 2] = -1.0
        matrix[p, 128:, 8 * p + 2 : 8 * p + 4] = -1.0
    return matrix


def twin_columns():
    matrix = np.zeros((128, 128), np.float32)
    for i in range(64):
        matrix[2 * i : 2 * i + 2, 2 * i : 2 * i + 2] = 1.0
    return matrix


def mm(a, b):
    return lax.dot_general(a, b, (((1,), (0,)), ((), ())), preferred_element_type=F32)


def mm_nt(a, b):
    return lax.dot_general(a, b, (((1,), (1,)), ((), ())), preferred_element_type=F32)


def mm_tn(a, b):
    return lax.dot_general(a, b, (((0,), (0,)), ((), ())), preferred_element_type=F32)


def split(a):
    high = a.astype(BF)
    return high, (a - high.astype(F32)).astype(BF)


def mm_split(a, b):
    high, low = split(b)
    return mm(a, high) + mm(a, low)


def split_mm(a, b):
    high, low = split(a)
    return mm(high, b) + mm(low, b)


def head_masks():
    lane = lax.broadcasted_iota(jnp.int32, (1, WIDE), 1)
    first = (lane < HEAD_DIM).astype(F32)
    return first, 1.0 - first


def stacked(a, masks):
    return jnp.concatenate([a * masks[0].astype(a.dtype), a * masks[1].astype(a.dtype)], axis=0)


def unstacked(a, masks):
    half = a.shape[0] // 2
    return a[:half] * masks[0] + a[half:] * masks[1]


def head_ones(keys):
    row = lax.broadcasted_iota(jnp.int32, (2 * keys, WIDE), 0)
    lane = lax.broadcasted_iota(jnp.int32, (2 * keys, WIDE), 1)
    return ((row < keys) == (lane < HEAD_DIM)).astype(F32).astype(BF)


def even_columns(high, low):
    col = lax.broadcasted_iota(jnp.int32, high.shape, 1)
    return jnp.where(col % 2 == 0, high.astype(F32), low.astype(F32)).astype(BF)


def normalize(values):
    centre = jnp.mean(values, axis=-1, keepdims=True)
    centred = values - centre
    spread = jnp.mean(centred * centred, axis=-1, keepdims=True)
    inverse = lax.rsqrt(spread + EPSILON)
    return centred * inverse, inverse


def full(shape):
    return pl.BlockSpec(shape, lambda *ids: (0,) * len(shape))


def shape_of(shape, dtype):
    return jax.ShapeDtypeStruct(shape, dtype)


def params(grid_dims=1):
    return pltpu.CompilerParams(
        dimension_semantics=("arbitrary",) * grid_dims, vmem_limit_bytes=VMEM_LIMIT
    )


def bit_groups(devices):
    groups = []
    high = devices.bit_length() - 2
    while high >= 1:
        low = max(1, high - 1)
        groups.append(tuple(range(low, high + 1)))
        high = low - 1
    return groups


def offsets_of(group):
    return [sum(1 << b for i, b in enumerate(group) if k >> i & 1) for k in range(1 << len(group))]


def send(value, offset, devices):
    return lax.ppermute(value, "fsdp", [(i, i ^ offset) for i in range(devices)])


def staged_gather(block, devices):
    held = block[None]
    slots = [0]
    groups = bit_groups(devices)
    pieces = []
    for group_id, group in enumerate(groups):
        offsets = offsets_of(group)
        parts = [held] + [send(held, k, devices) for k in offsets[1:]]
        if group_id == len(groups) - 1:
            pieces = [(p, [s ^ k for s in slots]) for p, k in zip(parts, offsets)]
        else:
            held = jnp.concatenate(parts, axis=0)
            slots = [s ^ k for k in offsets for s in slots]
    return pieces + [(send(p, 1, devices), [s ^ 1 for s in sl]) for p, sl in pieces]


def add_parts(keep, received, outs_dtype, name):
    cuts = len(outs_dtype)
    count = keep.shape[0]
    part = count // cuts

    def body(*refs):
        ins = refs[: 1 + len(received)]
        outs = refs[1 + len(received) :]
        for c in range(cuts):
            for i in range(part):
                total = ins[0][c * part + i].astype(F32)
                for r in ins[1:]:
                    total = total + r[c * part + i].astype(F32)
                outs[c][i] = total.astype(outs[c].dtype)

    return pl.pallas_call(
        body,
        out_shape=[shape_of((part,) + keep.shape[1:], d) for d in outs_dtype],
        compiler_params=pltpu.CompilerParams(vmem_limit_bytes=VMEM_LIMIT),
        name=name,
    )(keep, *received)


def scatter_order(devices):
    order = [0]
    for group in bit_groups(devices)[::-1]:
        order = [s ^ k for s in order for k in offsets_of(group)]
    return order


def staged_scatter(keep, sent, devices, name):
    received = [send(sent, 1, devices)]
    held = keep
    for stage, group in enumerate(bit_groups(devices)[::-1]):
        offsets = offsets_of(group)
        outs = add_parts(held, received, [F32] + [BF] * (len(offsets) - 1), f"{name}_{stage}")
        held = outs[0]
        received = [send(o, k, devices) for o, k in zip(outs[1:], offsets[1:])]
    return held, received


def first_kernel(layout, me_ref, x_ref, *refs):
    pieces, (qkv_ref, norm_ref, w_ref, vec_ref, bias_ref, coarse_ref) = (
        refs[: len(layout["slots"])],
        refs[len(layout["slots"]) :],
    )
    rows, devices = layout["rows"], layout["devices"]
    me = me_ref[0]

    @pl.when(pl.program_id(0) == 0)
    def _():
        small = []
        order = []
        for ref, slots in zip(pieces, layout["slots"]):
            for i, s in enumerate(slots):
                if layout["direct"]:
                    at = pl.multiple_of((me ^ s) * rows, rows)
                    for part in range(3):
                        w_ref[pl.ds(at, rows), part * 512 : (part + 1) * 512] = ref[
                            i, part * rows : (part + 1) * rows, :
                        ]
                small.append(ref[i, layout["small"] : layout["small"] + 8, :].astype(F32)[:1])
                order.append(s)
        table = jnp.concatenate(small, axis=0)
        vec_ref[...], bias_ref[...] = spread_small(table, order, me, devices)

    x = x_ref[...].astype(F32)
    normal, _ = normalize(x)
    normed = (normal * vec_ref[0:1, :] + vec_ref[2:3, :]).astype(BF)
    norm_ref[...] = normed
    qkv = mm(normed, w_ref[...]).astype(BF)
    qkv_ref[...] = qkv
    width = qkv.shape[1]
    means = jnp.mean(qkv[:, width // 3 :].astype(F32).reshape(-1, 32, 2 * width // 3), axis=1)
    coarse_ref[...] = means.astype(BF).reshape(coarse_ref.shape)


def slot_numbers(order, shape, dim):
    index = lax.broadcasted_iota(jnp.int32, shape, dim)
    value = jnp.zeros(shape, jnp.int32)
    for bit in range(max(order).bit_length()):
        on = None
        mask = 0
        for k in range((len(order) - 1).bit_length()):
            if order[1 << k] >> bit & 1:
                mask |= 1 << k
        parity = jnp.zeros(shape, jnp.int32)
        for k in range((len(order) - 1).bit_length()):
            if mask >> k & 1:
                parity = parity ^ ((index >> k) & 1)
        value = value | (parity << bit)
    return value


def spread_small(table, order, me, devices):
    w = 512 // devices
    wide = 2048 // devices
    owner = slot_numbers(order, (devices, 512), 0) ^ me
    col = lax.broadcasted_iota(jnp.int32, (devices, 512), 1)
    mine = (col // w == owner).astype(F32)
    lane = lax.broadcasted_iota(jnp.int32, (devices, 128), 1)
    lane_t = lax.broadcasted_iota(jnp.int32, (128, 512), 0)
    col_t = lax.broadcasted_iota(jnp.int32, (128, 512), 1)
    match = (lane_t % w == col_t % w).astype(F32).astype(BF)
    head = table[:, :128]
    rows = []
    for p in range(5):
        own = (head * (lane // w == p).astype(F32)).astype(BF)
        rows.append(jnp.sum(mm(own, match) * mine, axis=0, keepdims=True))
    rows = rows + [jnp.zeros((1, 512), F32)] * 3
    owner_w = slot_numbers(order, (devices, 2048), 0) ^ me
    col_w = lax.broadcasted_iota(jnp.int32, (devices, 2048), 1)
    mine_w = (col_w // wide == owner_w).astype(F32)
    lane_w = lax.broadcasted_iota(jnp.int32, (128, 2048), 0)
    col_tw = lax.broadcasted_iota(jnp.int32, (128, 2048), 1)
    match_w = (lane_w == col_tw % wide).astype(F32).astype(BF)
    bias = jnp.sum(mm(table[:, 128:256].astype(BF), match_w) * mine_w, axis=0, keepdims=True)
    return jnp.concatenate(rows, axis=0), jnp.broadcast_to(bias, (8, 2048))


def local_kernel(
    flags_ref, qkv_ref, pool_ref, unpool_ref, bias_ref, num_ref, den_ref, coarse_ref, w_ref, vbar_ref,
    vals, num_c, den_c,
):
    apart = flags_ref[pl.program_id(0)]
    masks = head_masks()
    value = qkv_ref[:, 1024:1536].astype(F32)
    vbar = jnp.mean(value, axis=0, keepdims=True)
    vbar_ref[0] = jnp.broadcast_to(vbar, (8, 512))
    vals[...] = (value - vbar).astype(BF)
    coarse_ref[:, 0:1024] = mm(pool_ref[...], qkv_ref[:, 0:1024]).astype(BF)
    coarse_ref[:, 1024:1536] = mm(pool_ref[...], vals[...]).astype(BF)
    ones = head_ones(128)
    for t in range(8):
        rows = slice((t % 4) * 128, (t % 4) * 128 + 128)
        kind = 0 if t < 4 else (1, 1, 2, 3)[t - 4]
        if kind == 3:
            bias = jnp.where(apart > 0, bias_ref[4], bias_ref[3])
        else:
            bias = bias_ref[kind]
        for p in range(PAIRS):
            lanes = slice(p * WIDE, (p + 1) * WIDE)
            lanes_k = slice(512 + p * WIDE, 512 + (p + 1) * WIDE)
            if t < 4:
                q, k, v = qkv_ref[rows, lanes], qkv_ref[rows, lanes_k], vals[rows, lanes]
            else:
                q, k = coarse_ref[rows, lanes], coarse_ref[rows, lanes_k]
                v = coarse_ref[rows, 1024 + p * WIDE : 1024 + (p + 1) * WIDE]
            scores = mm_nt(q, stacked(k, masks))
            weights = jnp.exp2(scores * SCALE2 + bias).astype(BF)
            w_ref[0, t, :, p * 256 : (p + 1) * 256] = weights
            num = mm(weights, stacked(v, masks))
            den = mm(weights, ones)
            if t < 4:
                num_ref[rows, lanes] = num
                den_ref[rows, lanes] = den
            else:
                num_c[rows, lanes] = num
                den_c[rows, lanes] = den
    num_ref[...] += mm_split(unpool_ref[...], num_c[...])
    den_ref[...] += mm_split(unpool_ref[...], den_c[...])


def fill_slots(pieces, slots, target):
    for ref, sl in zip(pieces, slots):
        for i, s in enumerate(sl):
            target[s] = ref[i]


def middle_kernel(layout, ints_ref, x_ref, go_ref, num_ref, den_ref, vbar_ref, cq_ref, rb_ref, vec_ref, bias_ref,
                  sel_ref, unr_ref, sum_ref, cols_ref, *refs):
    count = len(layout["slots"])
    kv_pieces, weights = refs[:count], refs[count : count + layout["n_weights"]]
    (out_ref, hid_ref, gpre_ref, norm_ref, att_ref, gt_ref, gmix_ref, ghat_ref, ch_ref, cl_ref, pay_ref,
     kvr_ref, wr_ref, small_ref, sbias_ref) = refs[count + layout["n_weights"] : count + layout["n_weights"] + 15]
    kvs, buf, w_out, w_in, w_back = refs[count + layout["n_weights"] + 15 :]
    me = ints_ref[0]
    m = pl.program_id(0)
    rows = layout["rows"]

    @pl.when(m == 0)
    def _():
        fill_slots(kv_pieces, layout["slots"], kvs)
        buf[...] = jnp.zeros_like(buf)
        if layout["direct"]:
            for ref, sl in zip(weights, layout["wslots"]):
                for i, s in enumerate(sl):
                    d = me ^ s
                    w_back[pl.ds(pl.multiple_of(d * 4 * rows, 4 * rows), 4 * rows), :] = ref[i, 0 : 4 * rows, :]
                    at = pl.multiple_of(d * rows, rows)
                    for c in range(4):
                        w_in[pl.ds(at, rows), c * 512 : (c + 1) * 512] = ref[i, (4 + c) * rows : (5 + c) * rows, :]
                    w_out[pl.ds(at, rows), :] = ref[i, 8 * rows : 9 * rows, :]
        else:
            w_out[...] = weights[0][...]
            w_in[...] = weights[1][...]
            w_back[...] = weights[2][...]

    masks = head_masks()
    vbar = vbar_ref[0, 0:1, :]
    for b in range(SIBS):
        slot = ints_ref[layout["first_slot"] + m * SIBS + b]
        buf[b * BLOCK : (b + 1) * BLOCK, :] = kvs[slot, pl.ds(pl.multiple_of(m * BLOCK, BLOCK), BLOCK), :]
    remote = mm(sel_ref[...], buf[...])
    key_r = remote[:, 0:512].astype(BF)
    val_r = (remote[:, 512:1024].astype(BF).astype(F32) - vbar).astype(BF)
    kvr_ref[:, 0:512] = key_r
    kvr_ref[:, 512:1024] = val_r
    ones = head_ones(64)
    rb = rb_ref[0]
    nums = []
    dens = []
    for p in range(PAIRS):
        lanes = slice(p * WIDE, (p + 1) * WIDE)
        scores = mm_nt(cq_ref[:, lanes], stacked(key_r[:, lanes], masks))
        wr = jnp.exp2(scores * SCALE2 + rb).astype(BF)
        wr_ref[:, lanes] = wr
        nums.append(mm(wr, stacked(val_r[:, lanes], masks)))
        dens.append(mm(wr, ones))
    num = num_ref[...] + mm_split(unr_ref[...], jnp.concatenate(nums, axis=1))
    den = den_ref[...] + mm_split(unr_ref[...], jnp.concatenate(dens, axis=1))
    inverse_den = 1.0 / den
    centred_o = num * inverse_den
    attended = (centred_o + vbar).astype(BF)
    att_ref[...] = attended
    mixed = x_ref[...].astype(F32) + mm(attended, w_out[...])
    normal, inverse = normalize(mixed)
    normed = (normal * vec_ref[1:2, :] + vec_ref[3:4, :]).astype(BF)
    norm_ref[...] = normed
    top_b = go_ref[...]
    top = top_b.astype(F32)
    result = mixed + vec_ref[4:5, :]
    g_norm = jnp.zeros_like(mixed)
    for c in range(4):
        lanes = slice(c * 512, (c + 1) * 512)
        pre = mm(normed, w_in[:, lanes]) + bias_ref[0:1, lanes]
        cdf = 0.5 + 0.5 * lax.erf(pre * math.sqrt(0.5))
        hidden = (pre * cdf).astype(BF)
        hid_ref[:, lanes] = hidden
        slope = cdf + pre * (jnp.exp(-0.5 * pre * pre) * (1.0 / math.sqrt(2.0 * math.pi)))
        g_pre = mm_nt(top_b, w_back[lanes, :]) * slope
        sbias_ref[0, :, lanes] = jnp.broadcast_to(jnp.sum(g_pre, axis=0, keepdims=True), (8, 512))
        g_pre_b = g_pre.astype(BF)
        gpre_ref[:, lanes] = g_pre_b
        result = result + mm(hidden, w_back[lanes, :])
        g_norm = g_norm + mm_nt(g_pre_b, w_in[:, lanes])
    out_ref[...] = result.astype(BF)
    scaled = g_norm * vec_ref[1:2, :]
    g_mixed = top + (
        scaled
        - jnp.mean(scaled, axis=-1, keepdims=True)
        - normal * jnp.mean(scaled * normal, axis=-1, keepdims=True)
    ) * inverse
    gmix_ref[...] = g_mixed
    small_ref[0] = jnp.concatenate(
        [
            jnp.sum(g_norm * normal, axis=0, keepdims=True),
            jnp.sum(g_norm, axis=0, keepdims=True),
            jnp.sum(top, axis=0, keepdims=True),
            jnp.zeros((5, 512), F32),
        ],
        axis=0,
    )
    gt = g_mixed.astype(BF)
    gt_ref[...] = gt
    ghat = (mm_nt(gt, w_out[...]) * inverse_den).astype(BF)
    ghat_ref[...] = ghat
    dots = split_mm(ghat.astype(F32) * centred_o, cols_ref[...])
    dots_h, dots_l = split(dots)
    ch_ref[...] = dots_h
    cl_ref[...] = dots_l
    g_sum = mm(sum_ref[...], ghat).astype(BF)
    c_sum = mm(sum_ref[...], dots_h) + mm(sum_ref[...], dots_l)
    c_sum = c_sum + split_mm(g_sum.astype(F32) * vbar, cols_ref[...])
    c_h, c_l = split(c_sum)
    pay_ref[:, 0:512] = cq_ref[0:BLOCK, :]
    pay_ref[:, 512:1024] = g_sum
    pay_ref[:, 1024:1152] = even_columns(c_h, c_l)


def wide_grads_kernel(layout, me_ref, hid_ref, gpre_ref, norm_ref, att_ref, gt_ref, go_ref, *refs):
    rows = layout["rows"]
    if layout["direct"]:
        keep_ref, sent_ref, back, up, out = refs
    else:
        back, up, out = refs
    for c in range(4):
        lanes = slice(c * 512, (c + 1) * 512)
        back[lanes, :] = mm_tn(hid_ref[:, lanes], go_ref[...]).astype(BF)
        up[:, lanes] = mm_tn(norm_ref[...], gpre_ref[:, lanes]).astype(BF)
    out[...] = mm_tn(att_ref[...], gt_ref[...]).astype(BF)
    if layout["direct"]:
        me = me_ref[0]
        for half, ref in ((0, keep_ref), (1, sent_ref)):
            for i, s in enumerate(layout["order"]):
                d = me ^ (s ^ half)
                ref[i, 0 : 4 * rows, :] = back[pl.ds(pl.multiple_of(d * 4 * rows, 4 * rows), 4 * rows), :]
                at = pl.multiple_of(d * rows, rows)
                for c in range(4):
                    ref[i, (4 + c) * rows : (5 + c) * rows, :] = up[pl.ds(at, rows), c * 512 : (c + 1) * 512]
                ref[i, 8 * rows : 9 * rows, :] = out[pl.ds(at, rows), :]


def back_kernel(qkv_ref, coarse_ref, w_ref, ghat_ref, ch_ref, cl_ref, vbar_ref, wr_ref, kvr_ref, sum_ref, spread_ref,
                minus_ref, grad_ref, vals, gsum, ext_f, ext_c, gcoarse):
    masks = head_masks()
    vals[...] = (qkv_ref[:, 1024:1536].astype(F32) - vbar_ref[0, 0:1, :]).astype(BF)
    gsum[...] = mm(sum_ref[...], ghat_ref[...]).astype(BF)
    c_sum = mm(sum_ref[...], ch_ref[...]) + mm(sum_ref[...], cl_ref[...])
    c_h, c_l = split(c_sum)
    ext_c[...] = even_columns(c_h, c_l)
    ext_f[...] = even_columns(ch_ref[...], cl_ref[...])
    for t in range(8):
        rows = slice((t % 4) * 128, (t % 4) * 128 + 128)
        for p in range(PAIRS):
            lanes = slice(p * WIDE, (p + 1) * WIDE)
            lanes_k = slice(512 + p * WIDE, 512 + (p + 1) * WIDE)
            lanes_v = slice(1024 + p * WIDE, 1024 + (p + 1) * WIDE)
            if t < 4:
                q, k, v = qkv_ref[rows, lanes], qkv_ref[rows, lanes_k], vals[rows, lanes]
                g, ext = ghat_ref[rows, lanes], ext_f[rows, :]
            else:
                q, k, v = coarse_ref[rows, lanes], coarse_ref[rows, lanes_k], coarse_ref[rows, lanes_v]
                g, ext = gsum[rows, lanes], ext_c[rows, :]
            weights = w_ref[0, t, :, p * 256 : (p + 1) * 256]
            left = jnp.concatenate([g, ext], axis=1)
            right = jnp.concatenate([stacked(v, masks), minus_ref[p]], axis=1)
            gs = (weights.astype(F32) * mm_nt(left, right)).astype(BF)
            g_q = mm(gs, stacked(k, masks)) * SCALE
            g_k = unstacked(mm_tn(gs, q), masks) * SCALE
            g_v = unstacked(mm_tn(weights, g), masks)
            if t < 4:
                grad_ref[rows, lanes] = g_q
                grad_ref[rows, lanes_k] = g_k
                grad_ref[rows, lanes_v] = g_v
            else:
                gcoarse[rows, lanes] = g_q.astype(BF)
                gcoarse[rows, lanes_k] = g_k.astype(BF)
                gcoarse[rows, lanes_v] = g_v.astype(BF)
    far = slice(480, 512)
    for p in range(PAIRS):
        lanes = slice(p * WIDE, (p + 1) * WIDE)
        left = jnp.concatenate([gsum[far, lanes], ext_c[far, :]], axis=1)
        minus = jnp.concatenate([minus_ref[p, 0:64, :], minus_ref[p, 128:192, :]], axis=0)
        right = jnp.concatenate([stacked(kvr_ref[:, 512 + p * WIDE : 512 + (p + 1) * WIDE], masks), minus], axis=1)
        gs = (wr_ref[:, lanes].astype(F32) * mm_nt(left, right)).astype(BF)
        gcoarse[far, lanes] = (mm(gs, stacked(kvr_ref[:, lanes], masks)) * SCALE).astype(BF)
    grad_ref[...] += mm(spread_ref[...], gcoarse[...])


def last_kernel(layout, ints_ref, grad_ref, x_ref, gmix_ref, norm_ref, w_ref, vec_ref, ckv_ref, vbar_ref, rb_ref, sel_ref,
                sels_ref, spr_ref, cols_ref, twin_ref, small_ref, sbias_ref, *refs):
    count = len(layout["slots"])
    pieces = refs[:count]
    if layout["direct"]:
        ingrad_ref, keep_ref, sent_ref, slots_v, buf, gqkv, wgrad = refs[count:]
    else:
        ingrad_ref, wgrad, tail_ref, slots_v, buf, gqkv = refs[count:]
    me = ints_ref[0]
    rows = layout["rows"]
    devices = layout["devices"]
    masks = head_masks()
    fill_slots(pieces, layout["slots"], slots_v)
    buf[...] = jnp.zeros_like(buf)
    length = x_ref.shape[0] // 2
    lane = lax.broadcasted_iota(jnp.int32, (1, 128), 1)
    for m in range(2):
        vbar = vbar_ref[m, 0:1, :]
        for b in range(SIBS):
            slot = ints_ref[layout["first_slot"] + m * SIBS + b]
            buf[b * BLOCK : (b + 1) * BLOCK, :] = slots_v[slot, m * BLOCK : (m + 1) * BLOCK, :]
        q_r = mm(sel_ref[...], buf[:, 0:512]).astype(BF)
        g_r = mm(sels_ref[...], buf[:, 512:1024]).astype(BF)
        c_r = mm_split(sels_ref[...], mm(buf[:, 1024:1152], twin_ref[...]))
        c_r = c_r - split_mm(g_r.astype(F32) * vbar, cols_ref[...])
        c_h, c_l = split(c_r)
        ext = even_columns(c_h, c_l).astype(F32)
        rb = rb_ref[m]
        g_keys = []
        g_vals = []
        for p in range(PAIRS):
            lanes = slice(p * WIDE, (p + 1) * WIDE)
            lanes_v = slice(512 + p * WIDE, 512 + (p + 1) * WIDE)
            k = ckv_ref[m * 32 : (m + 1) * 32, lanes]
            v = ckv_ref[m * 32 : (m + 1) * 32, lanes_v]
            qq = stacked(q_r[:, lanes], masks)
            gg = stacked(g_r[:, lanes], masks)
            weights = jnp.exp2(mm_nt(k, qq) * SCALE2 + rb)
            ones_a = ((lane // 2) == 4 * p).astype(F32)
            ones_b = ((lane // 2) == 4 * p + 1).astype(F32)
            ext_p = jnp.concatenate([ext * ones_a, ext * ones_b], axis=0).astype(BF)
            left = jnp.concatenate([v, jnp.full((32, 128), -1.0, BF)], axis=1)
            gs = (weights * mm_nt(left, jnp.concatenate([gg, ext_p], axis=1))).astype(BF)
            g_keys.append(mm(gs, qq) * SCALE)
            g_vals.append(mm(weights.astype(BF), gg))
        extra = mm_split(spr_ref[...], jnp.concatenate(g_keys + g_vals, axis=1))
        part = slice(m * length, (m + 1) * length)
        gqkv[part, 0:512] = grad_ref[part, 0:512].astype(BF)
        gqkv[part, 512:1536] = (grad_ref[part, 512:1536] + extra).astype(BF)
    g_norm = mm_nt(gqkv[...], w_ref[...])
    normal, inverse = normalize(x_ref[...].astype(F32))
    scaled = g_norm * vec_ref[0:1, :]
    ingrad_ref[...] = gmix_ref[...] + (
        scaled
        - jnp.mean(scaled, axis=-1, keepdims=True)
        - normal * jnp.mean(scaled * normal, axis=-1, keepdims=True)
    ) * inverse
    for part in range(3):
        lanes = slice(part * 512, (part + 1) * 512)
        wgrad[:, lanes] = mm_tn(norm_ref[...], gqkv[:, lanes]).astype(BF)
    vectors = [
        jnp.sum(g_norm * normal, axis=0, keepdims=True),
        small_ref[0, 0:1, :] + small_ref[1, 0:1, :],
        jnp.sum(g_norm, axis=0, keepdims=True),
        small_ref[0, 1:2, :] + small_ref[1, 1:2, :],
        small_ref[0, 2:3, :] + small_ref[1, 2:3, :],
    ]
    bias = sbias_ref[0, 0:1, :] + sbias_ref[1, 0:1, :]
    halves = ((0, 0), (1, 1)) if layout["direct"] else ((None, None),)
    for half, _ in halves:
        order = list(layout["order"]) if half is not None else list(range(devices))
        owner = slot_numbers(order, (len(order), 1), 0)
        if half is not None:
            owner = (owner ^ half) ^ me
        tail = gather_small(vectors, bias, owner, devices)
        if half is None:
            tail_ref[...] = tail
            continue
        ref = (keep_ref, sent_ref)[half]
        for i, s in enumerate(order):
            at = pl.multiple_of((me ^ (s ^ half)) * rows, rows)
            for part in range(3):
                ref[i, part * rows : (part + 1) * rows, :] = wgrad[pl.ds(at, rows), part * 512 : (part + 1) * 512]
            ref[i, 3 * rows : 3 * rows + 8, 0:256] = jnp.broadcast_to(tail[i : i + 1, :], (8, 256)).astype(BF)
            ref[i, 3 * rows : 3 * rows + 8, 256:512] = jnp.zeros((8, 256), BF)


def gather_small(vectors, bias, owner, devices):
    w = 512 // devices
    wide = 2048 // devices
    count = owner.shape[0]
    col = lax.broadcasted_iota(jnp.int32, (count, 512), 1)
    mine = (col // w == owner).astype(F32)
    col_t = lax.broadcasted_iota(jnp.int32, (512, 128), 0)
    lane_t = lax.broadcasted_iota(jnp.int32, (512, 128), 1)
    total = jnp.zeros((count, 128), F32)
    for p, row in enumerate(vectors):
        place = ((lane_t // w == p) & (lane_t % w == col_t % w)).astype(F32).astype(BF)
        total = total + split_mm(row * mine, place)
    col_w = lax.broadcasted_iota(jnp.int32, (count, 2048), 1)
    mine_w = (col_w // wide == owner).astype(F32)
    col_tw = lax.broadcasted_iota(jnp.int32, (2048, 128), 0)
    lane_tw = lax.broadcasted_iota(jnp.int32, (2048, 128), 1)
    place_w = (lane_tw == col_tw % wide).astype(F32).astype(BF)
    return jnp.concatenate([total, split_mm(bias * mine_w, place_w)], axis=1)


def seq_lookup(positions, seq_ends):
    return jnp.sum((positions[..., None] >= seq_ends).astype(jnp.int32), axis=-1)


def remote_plan(lengths, group_order, position, devices, length):
    micro_n = lengths.shape[0]
    count = lengths.shape[1]
    upper = np.tril(np.ones((count, count), np.int32))
    seq_ends = jnp.sum(lengths[:, None, :] * upper[None], axis=2)
    device_ids = jnp.arange(devices, dtype=jnp.int32)
    level_q = np.full((32,), -1, np.int32)
    start_q = np.zeros((32,), np.int32)
    row = 0
    for level in range(4):
        factor = 32 << level
        for i in range(length // factor):
            level_q[row] = level
            start_q[row] = i * factor
            row += 1
    level_k = np.repeat(np.arange(4, dtype=np.int32), BLOCK)
    index_k = np.tile(np.arange(BLOCK, dtype=np.int32), 4)
    factor_k = 32 << level_k
    span_k = (1 << level_k) * length
    slots = []
    biases = []
    apart = []
    for m in range(micro_n):
        group_id = jnp.sum(jnp.where(device_ids == position, group_order[m], 0))
        siblings = []
        for level in range(4):
            first = ((group_id >> level) ^ 1) << level
            siblings += [first + i for i in range(1 << level)]
        siblings = jnp.stack(siblings)
        owner = jnp.sum(jnp.where(group_order[m][None, :] == siblings[:, None], device_ids[None, :], 0), axis=1)
        slots.append(owner ^ position)
        first_k = ((group_id >> level_k) ^ 1) * span_k
        seq_k = seq_lookup(first_k + index_k * factor_k, seq_ends[m])
        seq_q = seq_lookup(group_id * length + start_q, seq_ends[m])
        same = (seq_q[:, None] == seq_k[None, :]) & (level_q[:, None] == level_k[None, :])
        bias = jnp.where(same, (level_k + 5).astype(np.float32)[None, :], OFF)
        biases.append(jnp.concatenate([bias, bias], axis=1))
        halves = seq_lookup(group_id * length + np.array([0, length // 2], np.int32), seq_ends[m])
        apart.append((halves[0] != halves[1]).astype(jnp.int32))
    return jnp.concatenate(slots).astype(jnp.int32), jnp.stack(biases), jnp.stack(apart)


def exchange_order(stack, position, devices):
    rest = stack.shape[1:]
    for bit in range(devices.bit_length() - 1):
        cut = stack.reshape((devices >> (bit + 1), 2, 1 << bit) + rest)
        stack = jnp.where((position >> bit) & 1 > 0, cut[:, ::-1], cut).reshape((devices,) + rest)
    return stack


def reordered(stack, order):
    return jnp.concatenate([stack[int(i) : int(i) + 1] for i in order], axis=0)


def natural(pieces, position, devices):
    order = [s for _, sl in pieces for s in sl]
    stack = jnp.concatenate([p for p, _ in pieces], axis=0)
    return exchange_order(reordered(stack, np.argsort(np.array(order))), position, devices)


def on_device(
    layer_in,
    out_grad,
    lengths,
    group_order,
    w_query,
    w_key,
    w_value,
    w_out,
    w_in,
    w_back,
    norm_gain,
    norm_shift,
    ffn_bias_in,
    ffn_bias_out,
):
    devices = lax.axis_size("fsdp")
    position = lax.axis_index("fsdp")
    micro_n, length, width = layer_in.shape
    hidden_n = w_in.shape[1]
    tokens = micro_n * length
    rows = w_query.shape[0]
    direct = rows % 16 == 0
    me = jnp.reshape(position, (1,)).astype(jnp.int32)
    x = layer_in.reshape(tokens, width)
    top = out_grad.reshape(tokens, width)

    small_rows = -(-3 * rows // 8) * 8
    tail = jnp.concatenate(
        [
            norm_gain.reshape(-1),
            norm_shift.reshape(-1),
            ffn_bias_out,
            jnp.zeros((128 - 5 * rows,), BF),
            ffn_bias_in,
            jnp.zeros((384 - ffn_bias_in.shape[0],), BF),
        ]
    )
    packed = jnp.concatenate([w_query, w_key, w_value], axis=0)
    if small_rows > 3 * rows:
        packed = jnp.concatenate([packed, jnp.zeros((small_rows - 3 * rows, width), BF)], axis=0)
    packed = jnp.concatenate([packed, jnp.broadcast_to(tail[None, :], (8, width))], axis=0)
    pieces_q = staged_gather(packed, devices)
    packed_w = jnp.concatenate(
        [w_back] + [w_in[:, c * width : (c + 1) * width] for c in range(hidden_n // width)] + [w_out], axis=0
    )
    pieces_w = staged_gather(packed_w, devices)

    slots, remote_bias, apart = remote_plan(lengths, group_order, position, devices, length)
    ints = jnp.concatenate([me, slots])

    layout = {
        "rows": rows,
        "devices": devices,
        "direct": direct,
        "small": small_rows,
        "slots": [sl for _, sl in pieces_q],
        "first_slot": 1,
        "order": scatter_order(devices),
    }
    n_pieces = len(pieces_q)
    arrays_q = [p for p, _ in pieces_q]
    if direct:
        w_spec = full((width, 3 * width))
    block_rows = 256
    grid = tokens // block_rows
    scalar = pl.BlockSpec(memory_space=pltpu.SMEM)
    smalls_w = [] if direct else [natural(pieces_q, position, devices)]
    if direct:
        body = lambda *refs: first_kernel(layout, *refs)
    else:
        w_all = jnp.concatenate(
            [smalls_w[0][:, part * rows : (part + 1) * rows].reshape(width, width) for part in range(3)], axis=1
        )

        def body(me_ref, x_ref, *refs):
            ins, given, outs = refs[:n_pieces], refs[n_pieces], refs[n_pieces + 1 :]

            @pl.when(pl.program_id(0) == 0)
            def _():
                outs[2][...] = given[...]

            first_kernel(layout, me_ref, x_ref, *ins, *outs)

    qkv, normed, w_qkv, vectors, bias_row, coarse_kv = pl.pallas_call(
        body,
        grid=(grid,),
        in_specs=[scalar, pl.BlockSpec((block_rows, width), lambda i: (i, 0))]
        + [full(a.shape) for a in arrays_q]
        + ([] if direct else [full((width, 3 * width))]),
        out_specs=[
            pl.BlockSpec((block_rows, 3 * width), lambda i: (i, 0)),
            pl.BlockSpec((block_rows, width), lambda i: (i, 0)),
            full((width, 3 * width)),
            full((8, width)),
            full((8, hidden_n)),
            pl.BlockSpec((1, block_rows // 32, 2 * width), lambda i: (i, 0, 0)),
        ],
        out_shape=[
            shape_of((tokens, 3 * width), BF),
            shape_of((tokens, width), BF),
            shape_of((width, 3 * width), BF),
            shape_of((8, width), F32),
            shape_of((8, hidden_n), F32),
            shape_of((grid, block_rows // 32, 2 * width), BF),
        ],
        compiler_params=params(),
        name="norm_qkv",
    )(me, x, *arrays_q, *([] if direct else [w_all]))

    pieces_kv = staged_gather(coarse_kv.reshape(micro_n * BLOCK, 2 * width), devices)

    pool = pool_matrix(length)
    held = (pool > 0).astype(np.float32)
    tile_biases = np.stack([tile_bias(k) for k in ("fine", "two", "four", "joined", "apart")])
    per_micro = lambda r, c: pl.BlockSpec((r, c), lambda i: (i, 0))
    num, den, coarse, weights, vbar = pl.pallas_call(
        local_kernel,
        grid=(micro_n,),
        in_specs=[scalar, per_micro(length, 3 * width), full((length, length)), full((length, length)), full(tile_biases.shape)],
        out_specs=[
            per_micro(length, width),
            per_micro(length, width),
            per_micro(length, 3 * width),
            pl.BlockSpec((1, 8, 128, 256 * PAIRS), lambda i: (i, 0, 0, 0)),
            pl.BlockSpec((1, 8, width), lambda i: (i, 0, 0)),
        ],
        out_shape=[
            shape_of((tokens, width), F32),
            shape_of((tokens, width), F32),
            shape_of((tokens, 3 * width), BF),
            shape_of((micro_n, 8, 128, 256 * PAIRS), BF),
            shape_of((micro_n, 8, width), F32),
        ],
        scratch_shapes=[
            pltpu.VMEM((length, width), BF),
            pltpu.VMEM((length, width), F32),
            pltpu.VMEM((length, width), F32),
        ],
        compiler_params=params(),
        name="local_forward",
    )(apart, qkv, jnp.asarray(pool, BF), jnp.asarray(held.T, BF), jnp.asarray(tile_biases))

    coarse3 = coarse.reshape(micro_n, length, 3 * width)[:, length - 32 :, :]
    coarse_q = coarse3[:, :, :width].reshape(micro_n * 32, width)
    coarse_own = coarse3[:, :, width:].reshape(micro_n * 32, 2 * width)

    arrays_kv = [p for p, _ in pieces_kv]
    if direct:
        weights_in = [p for p, _ in pieces_w]
    else:
        nat = natural(pieces_w, position, devices)
        weights_in = [
            nat[:, 8 * rows : 9 * rows].reshape(width, width),
            jnp.concatenate([nat[:, (4 + c) * rows : (5 + c) * rows].reshape(width, width) for c in range(4)], axis=1),
            nat[:, : 4 * rows].reshape(hidden_n, width),
        ]
    layout_m = dict(layout, slots=[sl for _, sl in pieces_kv], wslots=[sl for _, sl in pieces_w], n_weights=len(weights_in))
    sel = jnp.asarray(sibling_select(True), BF)
    sel_sum = jnp.asarray(sibling_select(False), BF)
    unpool_r = jnp.asarray(held[length - 32 :].T, BF)
    sum_32 = jnp.asarray(held[length - 32 : length - 32 + BLOCK], BF)
    cols = jnp.asarray(pair_columns(), BF)
    outs_m = [
        ((tokens, width), BF, per_micro(length, width)),
        ((tokens, hidden_n), BF, per_micro(length, hidden_n)),
        ((tokens, hidden_n), BF, per_micro(length, hidden_n)),
        ((tokens, width), BF, per_micro(length, width)),
        ((tokens, width), BF, per_micro(length, width)),
        ((tokens, width), BF, per_micro(length, width)),
        ((tokens, width), F32, per_micro(length, width)),
        ((tokens, width), BF, per_micro(length, width)),
        ((tokens, 128), BF, per_micro(length, 128)),
        ((tokens, 128), BF, per_micro(length, 128)),
        ((micro_n * BLOCK, 2 * width + 128), BF, per_micro(BLOCK, 2 * width + 128)),
        ((micro_n * 64, 2 * width), BF, per_micro(64, 2 * width)),
        ((micro_n * 32, width), BF, per_micro(32, width)),
        ((micro_n, 8, width), F32, pl.BlockSpec((1, 8, width), lambda i: (i, 0, 0))),
        ((micro_n, 8, hidden_n), F32, pl.BlockSpec((1, 8, hidden_n), lambda i: (i, 0, 0))),
    ]
    (layer_out, hidden, g_pre, normed_two, attended, gt, g_mixed, ghat, dots_h, dots_l, payload, far_kv, far_w,
     small_sums, bias_sums) = pl.pallas_call(
        lambda *refs: middle_kernel(layout_m, *refs),
        grid=(micro_n,),
        in_specs=[
            scalar,
            per_micro(length, width),
            per_micro(length, width),
            per_micro(length, width),
            per_micro(length, width),
            pl.BlockSpec((1, 8, width), lambda i: (i, 0, 0)),
            per_micro(32, width),
            pl.BlockSpec((1, 32, 128), lambda i: (i, 0, 0)),
            full((8, width)),
            full((8, hidden_n)),
            full((64, 256)),
            full((length, 32)),
            full((BLOCK, length)),
            full((width, 128)),
        ]
        + [full(a.shape) for a in arrays_kv]
        + [full(a.shape) for a in weights_in],
        out_specs=[o[2] for o in outs_m],
        out_shape=[shape_of(o[0], o[1]) for o in outs_m],
        scratch_shapes=[
            pltpu.VMEM((devices, micro_n * BLOCK, 2 * width), BF),
            pltpu.VMEM((256, 2 * width), BF),
            pltpu.VMEM((width, width), BF),
            pltpu.VMEM((width, hidden_n), BF),
            pltpu.VMEM((hidden_n, width), BF),
        ],
        compiler_params=params(),
        name="middle",
    )(ints, x, top, num, den, vbar, coarse_q, remote_bias, vectors, bias_row, sel, unpool_r, sum_32, cols,
      *arrays_kv, *weights_in)

    pieces_g = staged_gather(payload, devices)

    order = layout["order"]
    half = devices // 2
    wide_in = (me, hidden, g_pre, normed_two, attended, gt, top)
    plain = [shape_of((hidden_n, width), BF), shape_of((width, hidden_n), BF), shape_of((width, width), BF)]
    if direct:
        keep_w, sent_w = pl.pallas_call(
            lambda *refs: wide_grads_kernel(layout, *refs),
            in_specs=[scalar] + [pl.BlockSpec(memory_space=pltpu.VMEM)] * 6,
            out_shape=[shape_of((half, 9 * rows, width), BF)] * 2,
            scratch_shapes=[pltpu.VMEM(s.shape, s.dtype) for s in plain],
            compiler_params=pltpu.CompilerParams(vmem_limit_bytes=VMEM_LIMIT),
            name="wide_grads",
        )(*wide_in)
    else:
        g_back, g_in, g_out = pl.pallas_call(
            lambda *refs: wide_grads_kernel(layout, *refs),
            in_specs=[scalar] + [pl.BlockSpec(memory_space=pltpu.VMEM)] * 6,
            out_shape=plain,
            compiler_params=pltpu.CompilerParams(vmem_limit_bytes=VMEM_LIMIT),
            name="wide_grads",
        )(*wide_in)
        stack = jnp.concatenate(
            [g_back.reshape(devices, 4 * rows, width)]
            + [g_in[:, c * width : (c + 1) * width].reshape(devices, rows, width) for c in range(4)]
            + [g_out.reshape(devices, rows, width)],
            axis=1,
        )
        chosen = np.array(order, np.int32)
        stack = exchange_order(stack, position, devices)
        keep_w, sent_w = reordered(stack, chosen), reordered(stack, chosen ^ 1)
    held_w, received_w = staged_scatter(keep_w, sent_w, devices, "add_wide")

    (grads,) = pl.pallas_call(
        back_kernel,
        grid=(micro_n,),
        in_specs=[
            per_micro(length, 3 * width),
            per_micro(length, 3 * width),
            pl.BlockSpec((1, 8, 128, 256 * PAIRS), lambda i: (i, 0, 0, 0)),
            per_micro(length, width),
            per_micro(length, 128),
            per_micro(length, 128),
            pl.BlockSpec((1, 8, width), lambda i: (i, 0, 0)),
            per_micro(32, width),
            per_micro(64, 2 * width),
            full((length, length)),
            full((length, length)),
            full((PAIRS, 256, 128)),
        ],
        out_specs=[per_micro(length, 3 * width)],
        out_shape=[shape_of((tokens, 3 * width), F32)],
        scratch_shapes=[
            pltpu.VMEM((length, width), BF),
            pltpu.VMEM((length, width), BF),
            pltpu.VMEM((length, 128), BF),
            pltpu.VMEM((length, 128), BF),
            pltpu.VMEM((length, 3 * width), BF),
        ],
        compiler_params=params(),
        name="local_backward",
    )(qkv, coarse, weights, ghat, dots_h, dots_l, vbar, far_w, far_kv, jnp.asarray(held, BF), jnp.asarray(pool.T, BF),
      jnp.asarray(minus_columns(), BF))

    arrays_g = [p for p, _ in pieces_g]
    layout_l = dict(layout, slots=[sl for _, sl in pieces_g])
    in_vmem = pl.BlockSpec(memory_space=pltpu.VMEM)
    last_in = (ints, grads, x, g_mixed, normed, w_qkv, vectors, coarse_own, vbar, remote_bias, sel, sel_sum,
               jnp.asarray(pool[length - 32 :].T, BF), cols, jnp.asarray(twin_columns(), BF), small_sums, bias_sums,
               *arrays_g)
    scratch = [
        pltpu.VMEM((devices, micro_n * BLOCK, 2 * width + 128), BF),
        pltpu.VMEM((256, 2 * width + 128), BF),
        pltpu.VMEM((tokens, 3 * width), BF),
    ]
    if direct:
        in_grad, keep_q, sent_q = pl.pallas_call(
            lambda *refs: last_kernel(layout_l, *refs),
            in_specs=[scalar] + [in_vmem] * (len(last_in) - 1),
            out_shape=[shape_of((tokens, width), F32)] + [shape_of((half, 3 * rows + 8, width), BF)] * 2,
            scratch_shapes=scratch + [pltpu.VMEM((width, 3 * width), BF)],
            compiler_params=pltpu.CompilerParams(vmem_limit_bytes=VMEM_LIMIT),
            name="qkv_grads",
        )(*last_in)
    else:
        in_grad, g_qkv, tails = pl.pallas_call(
            lambda *refs: last_kernel(layout_l, *refs),
            in_specs=[scalar] + [in_vmem] * (len(last_in) - 1),
            out_shape=[shape_of((tokens, width), F32), shape_of((width, 3 * width), BF), shape_of((devices, 256), F32)],
            scratch_shapes=scratch,
            compiler_params=pltpu.CompilerParams(vmem_limit_bytes=VMEM_LIMIT),
            name="qkv_grads",
        )(*last_in)
        stack = jnp.concatenate(
            [g_qkv[:, c * width : (c + 1) * width].reshape(devices, rows, width) for c in range(3)]
            + [jnp.broadcast_to(jnp.pad(tails, ((0, 0), (0, 256)))[:, None, :], (devices, 8, width)).astype(BF)],
            axis=1,
        )
        chosen = np.array(order, np.int32)
        stack = exchange_order(stack, position, devices)
        keep_q, sent_q = reordered(stack, chosen), reordered(stack, chosen ^ 1)
    held_q, received_q = staged_scatter(keep_q, sent_q, devices, "add_qkv")
    (sum_w,) = add_parts(held_w, received_w, [F32], "add_wide_last")
    (sum_q,) = add_parts(held_q, received_q, [F32], "add_qkv_last")
    sum_w, sum_q = sum_w[0], sum_q[0]
    small = sum_q[3 * rows]
    wide = hidden_n // devices
    return (
        layer_out.reshape(micro_n, length, width),
        in_grad.reshape(micro_n, length, width),
        sum_q[:rows],
        sum_q[rows : 2 * rows],
        sum_q[2 * rows : 3 * rows],
        sum_w[8 * rows : 9 * rows],
        jnp.concatenate([sum_w[(4 + c) * rows : (5 + c) * rows] for c in range(4)], axis=1),
        sum_w[: 4 * rows],
        small[: 2 * rows].reshape(2, rows),
        small[2 * rows : 4 * rows].reshape(2, rows),
        small[128 : 128 + wide],
        small[4 * rows : 5 * rows],
    )


def solution(mesh):
    placed = (
        P(None, "fsdp", None),
        P(None, "fsdp", None),
        P(),
        P(),
        P("fsdp", None),
        P("fsdp", None),
        P("fsdp", None),
        P("fsdp", None),
        P("fsdp", None),
        P("fsdp", None),
        P(None, "fsdp"),
        P(None, "fsdp"),
        P("fsdp"),
        P("fsdp"),
    )
    return jax.shard_map(
        on_device,
        mesh=mesh,
        in_specs=placed,
        out_specs=(
            P(None, "fsdp", None),
            P(None, "fsdp", None),
            P("fsdp", None),
            P("fsdp", None),
            P("fsdp", None),
            P("fsdp", None),
            P("fsdp", None),
            P("fsdp", None),
            P(None, "fsdp"),
            P(None, "fsdp"),
            P("fsdp"),
            P("fsdp"),
        ),
        check_vma=False,
    )
```

```python
import math

import jax
import jax.numpy as jnp
import numpy as np
from jax import lax
from jax.experimental import pallas as pl
from jax.experimental.pallas import tpu as pltpu
from jax.sharding import PartitionSpec as P

HEADS = 8
HEAD_DIM = 64
BLOCK = 16
LEVELS = 9
EPSILON = 1e-05
OFF = -1e30
PAIRS = HEADS // 2
WIDE = 2 * HEAD_DIM
SCALE2 = math.log2(math.e) / math.sqrt(HEAD_DIM)
SCALE = 1.0 / math.sqrt(HEAD_DIM)
BF = jnp.bfloat16
F32 = jnp.float32
SIBS = 15


def iota(shape, dim):
    return lax.broadcasted_iota(jnp.int32, shape, dim)


def ones_where(condition, value=1.0):
    return jnp.where(condition, value, 0.0).astype(BF)


def coarse_places(index, length):
    shift = jnp.zeros_like(index)
    start = jnp.zeros_like(index)
    row = 0
    for level_id in range(2, LEVELS + 1):
        shift = shift + (index >= row).astype(jnp.int32)
        start = jnp.where(index >= row, row, start)
        row += length >> (level_id - 1)
    return shift, jnp.where(index >= row, length, index - start)


def members(length, first, count, by_rows):
    shape = (count, length) if by_rows else (length, count)
    narrow = (count, 1) if by_rows else (1, count)
    shift, place = coarse_places(iota(narrow, 0 if by_rows else 1) + first, length)
    covers = (iota(shape, 1 if by_rows else 0) >> shift) == place
    return covers, jnp.exp2(-shift.astype(F32))


def mean_rows(length, first, count):
    covers, share = members(length, first, count, True)
    return ones_where(covers, share)


def sum_rows(length, first, count):
    return ones_where(members(length, first, count, True)[0])


def share_columns(length, first, count):
    covers, share = members(length, first, count, False)
    return ones_where(covers, share)


def copy_columns(length, first, count):
    return ones_where(members(length, first, count, False)[0])


def tile_bias(kind, limit=0):
    row = iota((128, 256), 0)
    key = iota((128, 256), 1) & 127
    block_r, block_k = row // BLOCK, key // BLOCK
    sibling = block_r == (block_k ^ 1)
    if kind == 0:
        return jnp.where(block_r // 2 == block_k // 2, 0.0, OFF)
    if kind < 3:
        return jnp.where(sibling, float(kind), OFF)
    last = jnp.where(row < limit, 4.0, OFF)
    return jnp.where(sibling, jnp.where(row < 64, 3.0, last), OFF)


def sibling_rows(mean):
    row = iota((64, 256), 0)
    level, k = row // BLOCK, row % BLOCK
    span = jnp.left_shift(1, level)
    block = span - 1 + (k >> (4 - level))
    inside = k & ((BLOCK >> level) - 1)
    offset = iota((64, 256), 1) - (block * BLOCK + (inside << level))
    chosen = (offset >= 0) & (offset < span)
    return ones_where(chosen, 1.0 / span.astype(F32)) if mean else ones_where(chosen)


def head_columns():
    head = iota((512, 128), 0) // HEAD_DIM
    return ones_where(iota((512, 128), 1) // 2 == 4 * (head // 2) + head % 2)


def minus_columns(pair, keys):
    second = (iota((2 * keys, 128), 0) >= keys).astype(jnp.int32)
    return ones_where(iota((2 * keys, 128), 1) // 2 == 4 * pair + second, -1.0)


def twin_columns():
    return ones_where(iota((128, 128), 0) // 2 == iota((128, 128), 1) // 2)


def mm(a, b):
    return lax.dot_general(a, b, (((1,), (0,)), ((), ())), preferred_element_type=F32)


def mm_nt(a, b):
    return lax.dot_general(a, b, (((1,), (1,)), ((), ())), preferred_element_type=F32)


def mm_tn(a, b):
    return lax.dot_general(a, b, (((0,), (0,)), ((), ())), preferred_element_type=F32)


def split(a):
    high = a.astype(BF)
    return high, (a - high.astype(F32)).astype(BF)


def mm_split(a, b):
    high, low = split(b)
    return mm(a, high) + mm(a, low)


def split_mm(a, b):
    high, low = split(a)
    return mm(high, b) + mm(low, b)


def head_masks():
    lane = lax.broadcasted_iota(jnp.int32, (1, WIDE), 1)
    first = (lane < HEAD_DIM).astype(F32)
    return first, 1.0 - first


def stacked(a, masks):
    return jnp.concatenate([a * masks[0].astype(a.dtype), a * masks[1].astype(a.dtype)], axis=0)


def unstacked(a, masks):
    half = a.shape[0] // 2
    return a[:half] * masks[0] + a[half:] * masks[1]


def head_ones(keys):
    row = lax.broadcasted_iota(jnp.int32, (2 * keys, WIDE), 0)
    lane = lax.broadcasted_iota(jnp.int32, (2 * keys, WIDE), 1)
    return ((row < keys) == (lane < HEAD_DIM)).astype(F32).astype(BF)


def even_columns(high, low):
    col = lax.broadcasted_iota(jnp.int32, high.shape, 1)
    return jnp.where(col % 2 == 0, high.astype(F32), low.astype(F32)).astype(BF)


def normalize(values):
    centre = jnp.mean(values, axis=-1, keepdims=True)
    centred = values - centre
    spread = jnp.mean(centred * centred, axis=-1, keepdims=True)
    inverse = lax.rsqrt(spread + EPSILON)
    return centred * inverse, inverse


def shape_of(shape, dtype):
    return jax.ShapeDtypeStruct(shape, dtype)


def call(body, name, outs, ins, scalars=0, scratch=(), mib=8, us=2.0, after=()):
    vmem = pl.BlockSpec(memory_space=pltpu.VMEM)
    smem = pl.BlockSpec(memory_space=pltpu.SMEM)
    count, late = len(ins), len(after)

    def kernel(*refs):
        body(*refs[:count], *refs[count + late :])

    return pl.pallas_call(
        kernel,
        in_specs=[smem] * scalars + [vmem] * (count - scalars) + [pl.BlockSpec(memory_space=pl.ANY)] * late,
        out_specs=[pl.BlockSpec(memory_space=pltpu.VMEM)] * len(outs),
        out_shape=[shape_of(shape, dtype) for shape, dtype in outs],
        scratch_shapes=[pltpu.VMEM(shape, dtype) for shape, dtype in scratch],
        compiler_params=pltpu.CompilerParams(vmem_limit_bytes=int(mib * 2**20)),
        cost_estimate=pl.CostEstimate(flops=int(us * 1.1e9), transcendentals=0, bytes_accessed=1024),
        name=name,
    )(*ins, *after)


def bit_groups(devices):
    groups = []
    high = devices.bit_length() - 2
    while high >= 1:
        low = max(1, high - 1)
        groups.append(tuple(range(low, high + 1)))
        high = low - 1
    return groups


def offsets_of(group):
    return [sum(1 << b for i, b in enumerate(group) if k >> i & 1) for k in range(1 << len(group))]


def send(value, offset, devices):
    return lax.ppermute(value, "fsdp", [(i, i ^ offset) for i in range(devices)])


def joined(parts):
    return parts[0] if len(parts) == 1 else jnp.concatenate(parts, axis=0)


def follow(values, *earlier):
    return lax.optimization_barrier((values, earlier))[0] if earlier else values


def staged_gather(block, devices, between=(), marks=None):
    between = list(between) + [()] * len(bit_groups(devices))
    held = block[None]
    slots = [0]
    groups = bit_groups(devices)
    pieces = []
    for group_id, group in enumerate(groups):
        offsets = offsets_of(group)
        parts = [held] + [send(held, k, devices) for k in offsets[1:]]
        parts = follow(parts, *between[group_id])
        if group_id == len(groups) - 1:
            pieces = [(p, [s ^ k for s in slots]) for p, k in zip(parts, offsets)]
        else:
            held = joined(parts)
            slots = [s ^ k for k in offsets for s in slots]
            if marks is not None:
                marks.append(held)
    return pieces + [(send(p, 1, devices), [s ^ 1 for s in sl]) for p, sl in pieces]


def crossed_gather(block, cut, devices, marks, earlier):
    groups = bit_groups(devices)
    parts = [block[None]]
    slots = [0]
    for group in groups[:-1]:
        held = joined(parts)
        offsets = offsets_of(group)
        parts = [held] + [send(held, k, devices) for k in offsets[1:]]
        slots = [s ^ k for k in offsets for s in slots]
    parts = follow(parts, *earlier)
    halves = []
    for rows, order in ((slice(0, cut), groups[-1]), (slice(cut, None), groups[-1][::-1])):
        held, own = joined([p[:, rows] for p in parts]), slots
        for bit in order[:-1]:
            held = joined([held, send(held, 1 << bit, devices)])
            own = own + [s ^ (1 << bit) for s in own]
        marks.append(held)
        last = 1 << order[-1]
        halves.append([(held, own), (send(held, last, devices), [s ^ last for s in own])])
    first, second = follow([[p for p, _ in pieces] for pieces in halves], halves[0][1][0], halves[1][1][0])
    return [
        pieces + [(send(p, 1, devices), [s ^ 1 for s in sl]) for p, (_, sl) in zip(held, pieces)]
        for held, pieces in zip((first, second), halves)
    ]


def add_parts(keep, received, outs_dtype, name, after=()):
    cuts = len(outs_dtype)
    part = keep.shape[0] // cuts

    def body(*refs):
        ins = refs[: 1 + len(received)]
        outs = refs[1 + len(received) :]
        for c in range(cuts):
            for i in range(part):
                total = ins[0][c * part + i].astype(F32)
                for r in ins[1:]:
                    total = total + r[c * part + i].astype(F32)
                outs[c][i] = total.astype(outs[c].dtype)

    return call(body, name, [((part,) + keep.shape[1:], d) for d in outs_dtype], (keep, *received), mib=4, us=1.5, after=after)


def scatter_order(devices):
    order = [0]
    for group in bit_groups(devices)[::-1]:
        order = [s ^ k for s in order for k in offsets_of(group)]
    return order


def scatter_step(held, received, group, devices, name, after=()):
    offsets = offsets_of(group)
    outs = add_parts(held, received, [F32] + [BF] * (len(offsets) - 1), name, after)
    return outs[0], [send(o, k, devices) for o, k in zip(outs[1:], offsets[1:])]


def pack_kernel(rows, wq_ref, wk_ref, wv_ref, wo_ref, wi_ref, wb_ref, gain_ref, shift_ref, bi_ref, bo_ref, first_ref, second_ref):
    for part, ref in enumerate((wq_ref, wk_ref, wv_ref)):
        first_ref[part * rows : (part + 1) * rows, :] = ref[...]
    tail = jnp.zeros((1, 512), F32)
    for ref, at in ((gain_ref, 0), (shift_ref, 2 * rows), (bo_ref, 4 * rows), (bi_ref, 128)):
        for r in range(ref.shape[0]):
            count = ref.shape[1]
            index = lax.broadcasted_iota(jnp.int32, (count, 512), 0)
            lane = lax.broadcasted_iota(jnp.int32, (count, 512), 1)
            place = (lane == index + (at + r * count)).astype(F32).astype(BF)
            tail = tail + mm(ref[r : r + 1, :], place)
    first_ref[3 * rows : 3 * rows + 8, :] = jnp.broadcast_to(tail, (8, 512)).astype(BF)
    second_ref[0 : 4 * rows, :] = wb_ref[...]
    second_ref[4 * rows : 5 * rows, :] = wo_ref[...]
    for c in range(4):
        second_ref[(5 + c) * rows : (6 + c) * rows, :] = wi_ref[:, c * 512 : (c + 1) * 512]


def first_kernel(layout, ints_ref, x_ref, *refs):
    count = len(layout["slots"])
    pieces, refs = refs[:count], refs[count:]
    if not layout["direct"]:
        given, refs = refs[0], refs[1:]
    qkv_ref, norm_ref, w_ref, vec_ref, bias_ref, coarse_ref = refs
    rows, devices = layout["rows"], layout["devices"]
    me = ints_ref[0]
    small = []
    order = []
    if not layout["direct"]:
        w_ref[...] = given[...]
    for ref, slots in zip(pieces, layout["slots"]):
        for i, s in enumerate(slots):
            if layout["direct"]:
                at = pl.multiple_of((me ^ s) * rows, rows)
                for part in range(3):
                    w_ref[pl.ds(at, rows), part * 512 : (part + 1) * 512] = ref[i, part * rows : (part + 1) * rows, :]
            small.append(ref[i, layout["small"] : layout["small"] + 8, :].astype(F32)[:1])
            order.append(s)
    table = jnp.concatenate(small, axis=0)
    vec_ref[...], bias_ref[...] = spread_small(table, order, me, devices)
    for r in range(4):
        part = slice(r * 256, (r + 1) * 256)
        normal, _ = normalize(x_ref[part, :].astype(F32))
        normed = (normal * vec_ref[0:1, :] + vec_ref[2:3, :]).astype(BF)
        norm_ref[part, :] = normed
        qkv = mm(normed, w_ref[...]).astype(BF)
        qkv_ref[part, :] = qkv
        means = jnp.mean(qkv[:, 512:1536].astype(F32).reshape(8, 32, 1024), axis=1)
        coarse_ref[r * 8 : (r + 1) * 8, :] = means.astype(BF)


def slot_numbers(order, shape, dim):
    index = lax.broadcasted_iota(jnp.int32, shape, dim)
    value = jnp.zeros(shape, jnp.int32)
    for bit in range(max(order).bit_length()):
        on = None
        mask = 0
        for k in range((len(order) - 1).bit_length()):
            if order[1 << k] >> bit & 1:
                mask |= 1 << k
        parity = jnp.zeros(shape, jnp.int32)
        for k in range((len(order) - 1).bit_length()):
            if mask >> k & 1:
                parity = parity ^ ((index >> k) & 1)
        value = value | (parity << bit)
    return value


def spread_small(table, order, me, devices):
    w = 512 // devices
    wide = 2048 // devices
    owner = slot_numbers(order, (devices, 512), 0) ^ me
    col = lax.broadcasted_iota(jnp.int32, (devices, 512), 1)
    mine = (col // w == owner).astype(F32)
    lane = lax.broadcasted_iota(jnp.int32, (devices, 128), 1)
    lane_t = lax.broadcasted_iota(jnp.int32, (128, 512), 0)
    col_t = lax.broadcasted_iota(jnp.int32, (128, 512), 1)
    match = (lane_t % w == col_t % w).astype(F32).astype(BF)
    head = table[:, :128]
    rows = []
    for p in range(5):
        own = (head * (lane // w == p).astype(F32)).astype(BF)
        rows.append(jnp.sum(mm(own, match) * mine, axis=0, keepdims=True))
    rows = rows + [jnp.zeros((1, 512), F32)] * 3
    owner_w = slot_numbers(order, (devices, 2048), 0) ^ me
    col_w = lax.broadcasted_iota(jnp.int32, (devices, 2048), 1)
    mine_w = (col_w // wide == owner_w).astype(F32)
    lane_w = lax.broadcasted_iota(jnp.int32, (128, 2048), 0)
    col_tw = lax.broadcasted_iota(jnp.int32, (128, 2048), 1)
    match_w = (lane_w == col_tw % wide).astype(F32).astype(BF)
    bias = jnp.sum(mm(table[:, 128:256].astype(BF), match_w) * mine_w, axis=0, keepdims=True)
    return jnp.concatenate(rows, axis=0), jnp.broadcast_to(bias, (8, 2048))


def local_kernel(
    m, flag_at, ints_ref, qkv_ref, num_ref, den_ref, coarse_ref, w_ref, vbar_ref, vals, num_c, den_c, ones, matrix, biases,
):
    limit = jnp.where(ints_ref[flag_at + m] > 0, 64, 96)
    masks = head_masks()
    ones[...] = head_ones(128)
    length = num_ref.shape[0]
    base = m * length
    whole = slice(base, base + length)
    value = qkv_ref[whole, 1024:1536].astype(F32)
    vbar = jnp.mean(value, axis=0, keepdims=True)
    vbar_ref[...] = jnp.broadcast_to(vbar, (8, 512))
    vals[...] = (value - vbar).astype(BF)
    matrix[...] = mean_rows(length, 0, length)
    for kind in range(4):
        biases[kind] = tile_bias(kind, limit)
    coarse_ref[:, 0:1024] = mm(matrix[...], qkv_ref[whole, 0:1024]).astype(BF)
    coarse_ref[:, 1024:1536] = mm(matrix[...], vals[...]).astype(BF)
    for t in range(8):
        rows = slice((t % 4) * 128, (t % 4) * 128 + 128)
        far = slice(base + (t % 4) * 128, base + (t % 4) * 128 + 128)
        kind = 0 if t < 4 else (1, 1, 2, 3)[t - 4]
        bias = biases[kind]
        for p in range(PAIRS):
            lanes = slice(p * WIDE, (p + 1) * WIDE)
            lanes_k = slice(512 + p * WIDE, 512 + (p + 1) * WIDE)
            if t < 4:
                q, k, v = qkv_ref[far, lanes], qkv_ref[far, lanes_k], vals[rows, lanes]
            else:
                q, k = coarse_ref[rows, lanes], coarse_ref[rows, lanes_k]
                v = coarse_ref[rows, 1024 + p * WIDE : 1024 + (p + 1) * WIDE]
            scores = mm_nt(q, stacked(k, masks))
            weights = jnp.exp2(scores * SCALE2 + bias).astype(BF)
            w_ref[t, :, p * 256 : (p + 1) * 256] = weights
            both = mm(weights, jnp.concatenate([stacked(v, masks), ones[...]], axis=1))
            if t < 4:
                num_ref[rows, lanes] = both[:, :WIDE]
                den_ref[rows, lanes] = both[:, WIDE:]
            else:
                num_c[rows, lanes] = both[:, :WIDE]
                den_c[rows, lanes] = both[:, WIDE:]
    matrix[...] = copy_columns(length, 0, length)
    num_ref[...] += mm_split(matrix[...], num_c[...])
    den_ref[...] += mm_split(matrix[...], den_c[...])


def fill_slots(pieces, slots, target):
    for ref, sl in zip(pieces, slots):
        for i, s in enumerate(sl):
            target[s] = ref[i]


def take_siblings(layout, ints_ref, m, source, buf):
    for b in range(SIBS):
        if layout["direct"]:
            slot = ints_ref[layout["first_slot"] + m * SIBS + b]
            block = source[slot, m * BLOCK : (m + 1) * BLOCK, :]
        else:
            block = source[m * SIBS + b]
        buf[b * BLOCK : (b + 1) * BLOCK, :] = block


def middle_kernel(layout, ints_ref, x_ref, go_ref, rb_ref, vec_ref, bias_ref, *refs):
    local, refs = (refs[0:4], refs[4:8]), refs[8:]
    count = len(layout["slots"])
    kv_pieces, weights = refs[:count], refs[count : count + layout["n_weights"]]
    (out_ref, hid_ref, gpre_ref, norm_ref, att_ref, gt_ref, gmix_ref, ghat_ref, ch_ref, cl_ref, pay_ref,
     kvr_ref, wr_ref, small_ref, sbias_ref) = refs[count + layout["n_weights"] : count + layout["n_weights"] + 15]
    scratch = refs[count + layout["n_weights"] + 15 :]
    kvs, (buf, w_out, w_in, w_back) = scratch[0], scratch[-4:]
    me = ints_ref[0]
    rows = layout["rows"]
    length = local[0][0].shape[0]
    buf[...] = jnp.zeros_like(buf)
    if layout["direct"]:
        fill_slots(kv_pieces, layout["slots"], kvs)
        for ref, sl in zip(weights, layout["wslots"]):
            for i, s in enumerate(sl):
                d = me ^ s
                at = pl.multiple_of(d * rows, rows)
                if ref.shape[1] == 5 * rows:
                    w_back[pl.ds(pl.multiple_of(d * 4 * rows, 4 * rows), 4 * rows), :] = ref[i, 0 : 4 * rows, :]
                    w_out[pl.ds(at, rows), :] = ref[i, 4 * rows : 5 * rows, :]
                else:
                    for c in range(4):
                        w_in[pl.ds(at, rows), c * 512 : (c + 1) * 512] = ref[i, c * rows : (c + 1) * rows, :]
    else:
        w_out[...] = weights[0][...]
        w_in[...] = weights[1][...]
        w_back[...] = weights[2][...]

    masks = head_masks()
    ones = head_ones(64)
    select = sibling_rows(True)
    spread = copy_columns(length, length - 32, 32)
    sums = sum_rows(length, length - 32, BLOCK)
    columns = head_columns()
    for m in range(2):
        part = slice(m * length, (m + 1) * length)
        num_ref, den_ref, vbar_ref, coarse_ref = local[m]
        vbar = vbar_ref[0:1, :]
        far_q = coarse_ref[length - 32 : length, 0:512]
        take_siblings(layout, ints_ref, m, kvs if layout["direct"] else kv_pieces[0], buf)
        remote = mm(select, buf[...])
        key_r = remote[:, 0:512].astype(BF)
        val_r = (remote[:, 512:1024].astype(BF).astype(F32) - vbar).astype(BF)
        kvr_ref[m * 64 : (m + 1) * 64, 0:512] = key_r
        kvr_ref[m * 64 : (m + 1) * 64, 512:1024] = val_r
        rb = rb_ref[m]
        nums = []
        dens = []
        for p in range(PAIRS):
            lanes = slice(p * WIDE, (p + 1) * WIDE)
            scores = mm_nt(far_q[:, lanes], stacked(key_r[:, lanes], masks))
            wr = jnp.exp2(scores * SCALE2 + rb).astype(BF)
            wr_ref[m * 32 : (m + 1) * 32, lanes] = wr
            both = mm(wr, jnp.concatenate([stacked(val_r[:, lanes], masks), ones], axis=1))
            nums.append(both[:, :WIDE])
            dens.append(both[:, WIDE:])
        num = num_ref[...] + mm_split(spread, jnp.concatenate(nums, axis=1))
        den = den_ref[...] + mm_split(spread, jnp.concatenate(dens, axis=1))
        inverse_den = 1.0 / den
        centred_o = num * inverse_den
        attended = (centred_o + vbar).astype(BF)
        att_ref[part, :] = attended
        mixed = x_ref[part, :].astype(F32) + mm(attended, w_out[...])
        normal, inverse = normalize(mixed)
        normed = (normal * vec_ref[1:2, :] + vec_ref[3:4, :]).astype(BF)
        norm_ref[part, :] = normed
        top_b = go_ref[part, :]
        top = top_b.astype(F32)
        result = mixed + vec_ref[4:5, :]
        g_norm = jnp.zeros_like(mixed)
        for c in range(4):
            lanes = slice(c * 512, (c + 1) * 512)
            pre = mm(normed, w_in[:, lanes]) + bias_ref[0:1, lanes]
            cdf = 0.5 + 0.5 * lax.erf(pre * math.sqrt(0.5))
            hidden = (pre * cdf).astype(BF)
            hid_ref[part, lanes] = hidden
            slope = cdf + pre * (jnp.exp(-0.5 * pre * pre) * (1.0 / math.sqrt(2.0 * math.pi)))
            g_pre = mm_nt(top_b, w_back[lanes, :]) * slope
            sbias_ref[m, :, lanes] = jnp.broadcast_to(jnp.sum(g_pre, axis=0, keepdims=True), (8, 512))
            g_pre_b = g_pre.astype(BF)
            gpre_ref[part, lanes] = g_pre_b
            result = result + mm(hidden, w_back[lanes, :])
            g_norm = g_norm + mm_nt(g_pre_b, w_in[:, lanes])
        out_ref[part, :] = result.astype(BF)
        scaled = g_norm * vec_ref[1:2, :]
        g_mixed = top + (
            scaled
            - jnp.mean(scaled, axis=-1, keepdims=True)
            - normal * jnp.mean(scaled * normal, axis=-1, keepdims=True)
        ) * inverse
        gmix_ref[part, :] = g_mixed
        small_ref[m] = jnp.concatenate(
            [
                jnp.sum(g_norm * normal, axis=0, keepdims=True),
                jnp.sum(g_norm, axis=0, keepdims=True),
                jnp.sum(top, axis=0, keepdims=True),
                jnp.zeros((5, 512), F32),
            ],
            axis=0,
        )
        gt = g_mixed.astype(BF)
        gt_ref[part, :] = gt
        ghat = (mm_nt(gt, w_out[...]) * inverse_den).astype(BF)
        ghat_ref[part, :] = ghat
        dots = split_mm(ghat.astype(F32) * centred_o, columns)
        dots_h, dots_l = split(dots)
        ch_ref[part, :] = dots_h
        cl_ref[part, :] = dots_l
        g_sum = mm(sums, ghat).astype(BF)
        c_sum = mm(sums, dots_h) + mm(sums, dots_l)
        c_sum = c_sum + split_mm(g_sum.astype(F32) * vbar, columns)
        c_h, c_l = split(c_sum)
        pay = slice(m * BLOCK, (m + 1) * BLOCK)
        pay_ref[pay, 0:512] = far_q[0:BLOCK, :]
        pay_ref[pay, 512:1024] = g_sum
        pay_ref[pay, 1024:1152] = even_columns(c_h, c_l)


def wide_grads_kernel(layout, me_ref, hid_ref, gpre_ref, norm_ref, att_ref, gt_ref, go_ref, *refs):
    rows = layout["rows"]
    if layout["direct"]:
        keep_ref, sent_ref, back, up, out = refs
    else:
        back, up, out = refs
    for c in range(4):
        lanes = slice(c * 512, (c + 1) * 512)
        back[lanes, :] = mm_tn(hid_ref[:, lanes], go_ref[...]).astype(BF)
        up[:, lanes] = mm_tn(norm_ref[...], gpre_ref[:, lanes]).astype(BF)
    out[...] = mm_tn(att_ref[...], gt_ref[...]).astype(BF)
    if layout["direct"]:
        me = me_ref[0]
        for half, ref in ((0, keep_ref), (1, sent_ref)):
            for i, s in enumerate(layout["order"]):
                d = me ^ (s ^ half)
                ref[i, 0 : 4 * rows, :] = back[pl.ds(pl.multiple_of(d * 4 * rows, 4 * rows), 4 * rows), :]
                at = pl.multiple_of(d * rows, rows)
                for c in range(4):
                    ref[i, (4 + c) * rows : (5 + c) * rows, :] = up[pl.ds(at, rows), c * 512 : (c + 1) * 512]
                ref[i, 8 * rows : 9 * rows, :] = out[pl.ds(at, rows), :]


def back_kernel(m, qkv_ref, coarse_ref, w_ref, ghat_ref, ch_ref, cl_ref, vbar_ref, wr_ref, kvr_ref, grad_ref,
                vals, gsum, ext_f, ext_c, gcoarse, matrix, minus_ref):
    masks = head_masks()
    length = vals.shape[0]
    base = m * length
    whole = slice(base, base + length)
    vals[...] = (qkv_ref[whole, 1024:1536].astype(F32) - vbar_ref[0:1, :]).astype(BF)
    matrix[...] = sum_rows(length, 0, length)
    for p in range(PAIRS):
        minus_ref[p] = minus_columns(p, 128)
    gsum[...] = mm(matrix[...], ghat_ref[whole, :]).astype(BF)
    c_sum = mm(matrix[...], ch_ref[whole, :]) + mm(matrix[...], cl_ref[whole, :])
    c_h, c_l = split(c_sum)
    ext_c[...] = even_columns(c_h, c_l)
    ext_f[...] = even_columns(ch_ref[whole, :], cl_ref[whole, :])
    zero = jnp.zeros((128, WIDE), BF)
    for t in range(8):
        rows = slice((t % 4) * 128, (t % 4) * 128 + 128)
        far = slice(base + (t % 4) * 128, base + (t % 4) * 128 + 128)
        for p in range(PAIRS):
            lanes = slice(p * WIDE, (p + 1) * WIDE)
            lanes_k = slice(512 + p * WIDE, 512 + (p + 1) * WIDE)
            lanes_v = slice(1024 + p * WIDE, 1024 + (p + 1) * WIDE)
            if t < 4:
                q, k, v = qkv_ref[far, lanes], qkv_ref[far, lanes_k], vals[rows, lanes]
                g, ext = ghat_ref[far, lanes], ext_f[rows, :]
            else:
                q, k, v = coarse_ref[rows, lanes], coarse_ref[rows, lanes_k], coarse_ref[rows, lanes_v]
                g, ext = gsum[rows, lanes], ext_c[rows, :]
            weights = w_ref[t, :, p * 256 : (p + 1) * 256]
            left = jnp.concatenate([g, ext], axis=1)
            right = jnp.concatenate([stacked(v, masks), minus_ref[p]], axis=1)
            gs = (weights.astype(F32) * mm_nt(left, right)).astype(BF)
            g_q = mm(gs, stacked(k, masks)) * SCALE
            g_kv = mm_tn(
                jnp.concatenate([gs, weights], axis=0),
                jnp.concatenate([jnp.concatenate([q, zero], axis=1), jnp.concatenate([zero, g], axis=1)], axis=0),
            )
            g_k = unstacked(g_kv[:, :WIDE], masks) * SCALE
            g_v = unstacked(g_kv[:, WIDE:], masks)
            if t < 4:
                grad_ref[rows, lanes] = g_q
                grad_ref[rows, lanes_k] = g_k
                grad_ref[rows, lanes_v] = g_v
            else:
                gcoarse[rows, lanes] = g_q.astype(BF)
                gcoarse[rows, lanes_k] = g_k.astype(BF)
                gcoarse[rows, lanes_v] = g_v.astype(BF)
    far = slice(480, 512)
    for p in range(PAIRS):
        lanes = slice(p * WIDE, (p + 1) * WIDE)
        left = jnp.concatenate([gsum[far, lanes], ext_c[far, :]], axis=1)
        minus = minus_columns(p, 64)
        part = slice(m * 64, (m + 1) * 64)
        right = jnp.concatenate([stacked(kvr_ref[part, 512 + p * WIDE : 512 + (p + 1) * WIDE], masks), minus], axis=1)
        gs = (wr_ref[m * 32 : (m + 1) * 32, lanes].astype(F32) * mm_nt(left, right)).astype(BF)
        gcoarse[far, lanes] = (mm(gs, stacked(kvr_ref[part, lanes], masks)) * SCALE).astype(BF)
    matrix[...] = share_columns(length, 0, length)
    grad_ref[...] += mm(matrix[...], gcoarse[...])


def last_kernel(layout, ints_ref, x_ref, gmix_ref, norm_ref, w_ref, vec_ref, rb_ref, small_ref, sbias_ref, *refs):
    local, refs = (refs[0:3], refs[3:6]), refs[6:]
    count = len(layout["slots"])
    pieces = refs[:count]
    if layout["direct"]:
        ingrad_ref, keep_ref, sent_ref, slots_v, buf, gqkv, wgrad = refs[count:]
    else:
        ingrad_ref, wgrad, tail_ref, buf, gqkv = refs[count:]
    me = ints_ref[0]
    rows = layout["rows"]
    devices = layout["devices"]
    masks = head_masks()
    if layout["direct"]:
        fill_slots(pieces, layout["slots"], slots_v)
    buf[...] = jnp.zeros_like(buf)
    length = x_ref.shape[0] // 2
    lane = lax.broadcasted_iota(jnp.int32, (1, 128), 1)
    select, select_sum = sibling_rows(True), sibling_rows(False)
    spread = share_columns(length, length - 32, 32)
    columns, twins = head_columns(), twin_columns()
    for m in range(2):
        grad_ref, coarse_ref, vbar_ref = local[m]
        vbar = vbar_ref[0:1, :]
        take_siblings(layout, ints_ref, m, slots_v if layout["direct"] else pieces[0], buf)
        q_r = mm(select, buf[:, 0:512]).astype(BF)
        g_r = mm(select_sum, buf[:, 512:1024]).astype(BF)
        c_r = mm_split(select_sum, mm(buf[:, 1024:1152], twins))
        c_r = c_r - split_mm(g_r.astype(F32) * vbar, columns)
        c_h, c_l = split(c_r)
        ext = even_columns(c_h, c_l).astype(F32)
        rb = rb_ref[m]
        g_keys = []
        g_vals = []
        for p in range(PAIRS):
            lanes = slice(p * WIDE, (p + 1) * WIDE)
            k = coarse_ref[length - 32 : length, 512 + p * WIDE : 512 + (p + 1) * WIDE]
            v = coarse_ref[length - 32 : length, 1024 + p * WIDE : 1024 + (p + 1) * WIDE]
            qq = stacked(q_r[:, lanes], masks)
            gg = stacked(g_r[:, lanes], masks)
            weights = jnp.exp2(mm_nt(k, qq) * SCALE2 + rb)
            ones_a = ((lane // 2) == 4 * p).astype(F32)
            ones_b = ((lane // 2) == 4 * p + 1).astype(F32)
            ext_p = jnp.concatenate([ext * ones_a, ext * ones_b], axis=0).astype(BF)
            left = jnp.concatenate([v, jnp.full((32, 128), -1.0, BF)], axis=1)
            gs = (weights * mm_nt(left, jnp.concatenate([gg, ext_p], axis=1))).astype(BF)
            g_keys.append(mm(gs, qq) * SCALE)
            g_vals.append(mm(weights.astype(BF), gg))
        extra = mm_split(spread, jnp.concatenate(g_keys + g_vals, axis=1))
        part = slice(m * length, (m + 1) * length)
        gqkv[part, 0:512] = grad_ref[:, 0:512].astype(BF)
        gqkv[part, 512:1536] = (grad_ref[:, 512:1536] + extra).astype(BF)
    g_norm = mm_nt(gqkv[...], w_ref[...])
    normal, inverse = normalize(x_ref[...].astype(F32))
    scaled = g_norm * vec_ref[0:1, :]
    ingrad_ref[...] = gmix_ref[...] + (
        scaled
        - jnp.mean(scaled, axis=-1, keepdims=True)
        - normal * jnp.mean(scaled * normal, axis=-1, keepdims=True)
    ) * inverse
    for part in range(3):
        lanes = slice(part * 512, (part + 1) * 512)
        wgrad[:, lanes] = mm_tn(norm_ref[...], gqkv[:, lanes]).astype(BF)
    vectors = [
        jnp.sum(g_norm * normal, axis=0, keepdims=True),
        small_ref[0, 0:1, :] + small_ref[1, 0:1, :],
        jnp.sum(g_norm, axis=0, keepdims=True),
        small_ref[0, 1:2, :] + small_ref[1, 1:2, :],
        small_ref[0, 2:3, :] + small_ref[1, 2:3, :],
    ]
    bias = sbias_ref[0, 0:1, :] + sbias_ref[1, 0:1, :]
    halves = ((0, 0), (1, 1)) if layout["direct"] else ((None, None),)
    for half, _ in halves:
        order = list(layout["order"]) if half is not None else list(range(devices))
        owner = slot_numbers(order, (len(order), 1), 0)
        if half is not None:
            owner = (owner ^ half) ^ me
        tail = gather_small(vectors, bias, owner, devices)
        if half is None:
            tail_ref[...] = tail
            continue
        ref = (keep_ref, sent_ref)[half]
        for i, s in enumerate(order):
            at = pl.multiple_of((me ^ (s ^ half)) * rows, rows)
            for part in range(3):
                ref[i, part * rows : (part + 1) * rows, :] = wgrad[pl.ds(at, rows), part * 512 : (part + 1) * 512]
            ref[i, 3 * rows : 3 * rows + 8, 0:256] = jnp.broadcast_to(tail[i : i + 1, :], (8, 256)).astype(BF)
            ref[i, 3 * rows : 3 * rows + 8, 256:512] = jnp.zeros((8, 256), BF)


def gather_small(vectors, bias, owner, devices):
    w = 512 // devices
    wide = 2048 // devices
    count = owner.shape[0]
    col = lax.broadcasted_iota(jnp.int32, (count, 512), 1)
    mine = (col // w == owner).astype(F32)
    col_t = lax.broadcasted_iota(jnp.int32, (512, 128), 0)
    lane_t = lax.broadcasted_iota(jnp.int32, (512, 128), 1)
    total = jnp.zeros((count, 128), F32)
    for p, row in enumerate(vectors):
        place = ((lane_t // w == p) & (lane_t % w == col_t % w)).astype(F32).astype(BF)
        total = total + split_mm(row * mine, place)
    col_w = lax.broadcasted_iota(jnp.int32, (count, 2048), 1)
    mine_w = (col_w // wide == owner).astype(F32)
    col_tw = lax.broadcasted_iota(jnp.int32, (2048, 128), 0)
    lane_tw = lax.broadcasted_iota(jnp.int32, (2048, 128), 1)
    place_w = (lane_tw == col_tw % wide).astype(F32).astype(BF)
    return jnp.concatenate([total, split_mm(bias * mine_w, place_w)], axis=1)


def total_of(refs, rows):
    total = refs[0][0, rows, :].astype(F32)
    for r in refs[1:]:
        total = total + r[0, rows, :].astype(F32)
    return total


def finish_wide_kernel(rows, *refs):
    ins, (back_ref, in_ref, out_ref) = refs[:-3], refs[-3:]
    back_ref[...] = total_of(ins, slice(0, 4 * rows))
    for c in range(4):
        in_ref[:, c * 512 : (c + 1) * 512] = total_of(ins, slice((4 + c) * rows, (5 + c) * rows))
    out_ref[...] = total_of(ins, slice(8 * rows, 9 * rows))


def finish_qkv_kernel(rows, *refs):
    ins, (q_ref, k_ref, v_ref, gain_ref, shift_ref, bi_ref, bo_ref) = refs[:-7], refs[-7:]
    for part, ref in enumerate((q_ref, k_ref, v_ref)):
        ref[...] = total_of(ins, slice(part * rows, (part + 1) * rows))
    tail = total_of(ins, slice(3 * rows, 3 * rows + 8))[0:1]
    for r in range(2):
        gain_ref[r : r + 1, :] = tail[:, r * rows : (r + 1) * rows]
        shift_ref[r : r + 1, :] = tail[:, (2 + r) * rows : (3 + r) * rows]
    bo_ref[...] = tail[:, 4 * rows : 5 * rows]
    bi_ref[...] = tail[:, 128 : 128 + bi_ref.shape[1]]


def remote_plan(lengths, group_order, position, devices, length):
    count = lengths.shape[1]
    lower = np.tril(np.ones((count, count), np.int32))
    seq_ends = jnp.sum(lengths[:, None, :] * lower[None], axis=2)
    device_ids = np.arange(devices, dtype=np.int32)
    group_id = jnp.sum(jnp.where(device_ids == position, group_order, 0), axis=1)[:, None]
    level_s = np.repeat(np.arange(4, dtype=np.int32), [1, 2, 4, 8])
    index_s = np.concatenate([np.arange(1 << level, dtype=np.int32) for level in range(4)])
    siblings = (((group_id >> level_s) ^ 1) << level_s) + index_s
    owner = jnp.sum(jnp.where(group_order[:, None, :] == siblings[:, :, None], device_ids, 0), axis=2)
    level_q = np.full((32,), -1, np.int32)
    start_q = np.zeros((32,), np.int32)
    row = 0
    for level in range(4):
        for i in range(length // (32 << level)):
            level_q[row] = level
            start_q[row] = i * (32 << level)
            row += 1
    level_k = np.tile(np.repeat(np.arange(4, dtype=np.int32), BLOCK), 2)
    start_k = np.tile(np.arange(BLOCK, dtype=np.int32), 8) * (32 << level_k)
    first_k = (((group_id >> level_k) ^ 1) << level_k) * length
    starts = np.concatenate([start_q, np.array([0, length // 2], np.int32)])
    places = jnp.concatenate([first_k + start_k, group_id * length + starts], axis=1)
    seq = jnp.sum((places[:, :, None] >= seq_ends[:, None, :]).astype(jnp.int32), axis=2)
    same = (seq[:, 128:160, None] == seq[:, None, :128]) & (level_q[:, None] == level_k[None, :])
    bias = jnp.where(same, (level_k + 5).astype(np.float32), OFF)
    apart = (seq[:, 160] != seq[:, 161]).astype(jnp.int32)
    ints = jnp.concatenate([jnp.reshape(position, (1,)), (owner ^ position).reshape(-1), apart]).astype(jnp.int32)
    return ints, bias


def exchange_order(stack, position, devices):
    rest = stack.shape[1:]
    for bit in range(devices.bit_length() - 1):
        cut = stack.reshape((devices >> (bit + 1), 2, 1 << bit) + rest)
        stack = jnp.where((position >> bit) & 1 > 0, cut[:, ::-1], cut).reshape((devices,) + rest)
    return stack


def reordered(stack, order):
    return jnp.concatenate([stack[int(i) : int(i) + 1] for i in order], axis=0)


def natural(pieces, position, devices):
    order = [s for _, sl in pieces for s in sl]
    stack = jnp.concatenate([p for p, _ in pieces], axis=0)
    return exchange_order(reordered(stack, np.argsort(np.array(order))), position, devices)


def picked(pieces, ints, micro_n):
    order = [s for _, sl in pieces for s in sl]
    stack = reordered(jnp.concatenate([p for p, _ in pieces], axis=0), np.argsort(np.array(order)))
    blocks = []
    for m in range(micro_n):
        for b in range(SIBS):
            block = lax.dynamic_slice_in_dim(stack, ints[1 + m * SIBS + b], 1, axis=0)
            blocks.append(block[:, m * BLOCK : (m + 1) * BLOCK])
    return jnp.concatenate(blocks, axis=0)


def on_device(
    layer_in,
    out_grad,
    lengths,
    group_order,
    w_query,
    w_key,
    w_value,
    w_out,
    w_in,
    w_back,
    norm_gain,
    norm_shift,
    ffn_bias_in,
    ffn_bias_out,
):
    devices = lax.axis_size("fsdp")
    position = lax.axis_index("fsdp")
    micro_n, length, width = layer_in.shape
    hidden_n = w_in.shape[1]
    tokens = micro_n * length
    rows = w_query.shape[0]
    half = devices // 2
    direct = rows % 16 == 0
    x = layer_in.reshape(tokens, width)
    top = out_grad.reshape(tokens, width)

    small_rows = -(-3 * rows // 8) * 8
    biases = (ffn_bias_in.reshape(1, -1), ffn_bias_out.reshape(1, -1))
    if direct:
        shards = (w_query, w_key, w_value, w_out, w_in, w_back, norm_gain, norm_shift, *biases)
        packed, packed_w = pl.pallas_call(
            lambda *refs: pack_kernel(rows, *refs),
            grid=(1,),
            in_specs=[pl.BlockSpec(a.shape, lambda i: (0, 0)) for a in shards],
            out_specs=[pl.BlockSpec(memory_space=pltpu.VMEM)] * 2,
            out_shape=[shape_of((3 * rows + 8, width), BF), shape_of((9 * rows, width), BF)],
            name="pack",
        )(*shards)
    else:
        tail = jnp.concatenate(
            [
                norm_gain.reshape(-1),
                norm_shift.reshape(-1),
                ffn_bias_out,
                jnp.zeros((128 - 5 * rows,), BF),
                ffn_bias_in,
                jnp.zeros((384 - ffn_bias_in.shape[0],), BF),
            ]
        )
        packed = jnp.concatenate(
            [
                w_query,
                w_key,
                w_value,
                jnp.zeros((small_rows - 3 * rows, width), BF),
                jnp.broadcast_to(tail[None, :], (8, width)),
            ],
            axis=0,
        )
        packed_w = jnp.concatenate(
            [w_back, w_out] + [w_in[:, c * width : (c + 1) * width] for c in range(hidden_n // width)], axis=0
        )
    marks_q, marks_w = [], []
    pieces_q = staged_gather(packed, devices, marks=marks_q)
    packed_w, lengths, group_order = follow((packed_w, lengths, group_order), marks_q[0])
    pieces_bo, pieces_in = crossed_gather(packed_w, 5 * rows, devices, marks_w, [p for p, _ in pieces_q[:4]])
    ints, remote_bias = remote_plan(lengths, group_order, position, devices, length)

    layout = {
        "rows": rows,
        "devices": devices,
        "direct": direct,
        "small": small_rows,
        "slots": [sl for _, sl in pieces_q],
        "first_slot": 1,
        "order": scatter_order(devices),
    }
    flag_at = 1 + micro_n * SIBS
    arrays_q = [p for p, _ in pieces_q]
    if not direct:
        nat = natural(pieces_q, position, devices)
        arrays_q.append(
            jnp.concatenate([nat[:, part * rows : (part + 1) * rows].reshape(width, width) for part in range(3)], axis=1)
        )
    me = jnp.reshape(position, (1,)).astype(jnp.int32)
    qkv, normed, w_qkv, vectors, bias_row, coarse_kv = call(
        lambda *refs: first_kernel(layout, *refs),
        "norm_qkv",
        [
            ((tokens, 3 * width), BF),
            ((tokens, width), BF),
            ((width, 3 * width), BF),
            ((8, width), F32),
            ((8, hidden_n), F32),
            ((micro_n * BLOCK, 2 * width), BF),
        ],
        (ints, x, *arrays_q),
        scalars=1,
        mib=12,
        us=5.0,
    )

    local = [
        call(
            lambda *refs, m=m: local_kernel(m, flag_at, *refs),
            f"local_forward_{m}",
            [
                ((length, width), F32),
                ((length, width), F32),
                ((length, 3 * width), BF),
                ((8, 128, 256 * PAIRS), BF),
                ((8, width), F32),
            ],
            (ints, qkv),
            scalars=1,
            scratch=[
                ((length, width), BF),
                ((length, width), F32),
                ((length, width), F32),
                ((256, WIDE), BF),
                ((length, length), BF),
                ((4, 128, 256), F32),
            ],
            mib=12,
            us=4.0,
            after=marks_w if m == 0 else (),
        )
        for m in range(micro_n)
    ]

    pieces_kv = staged_gather(coarse_kv, devices, [(local[0][4], *marks_w), (local[1][4],)])
    arrays_kv = [p for p, _ in pieces_kv] if direct else [picked(pieces_kv, ints, micro_n)]
    if direct:
        weights_in = [p for p, _ in pieces_bo + pieces_in]
    else:
        nat_bo, nat_in = natural(pieces_bo, position, devices), natural(pieces_in, position, devices)
        weights_in = [
            nat_bo[:, 4 * rows :].reshape(width, width),
            jnp.concatenate([nat_in[:, c * rows : (c + 1) * rows].reshape(width, width) for c in range(4)], axis=1),
            nat_bo[:, : 4 * rows].reshape(hidden_n, width),
        ]
    layout_m = dict(
        layout,
        slots=[sl for _, sl in pieces_kv][: len(arrays_kv)],
        wslots=[sl for _, sl in pieces_bo + pieces_in],
        n_weights=len(weights_in),
    )
    per_local = [a for num, den, coarse, _, vbar in local for a in (num, den, vbar, coarse)]
    (layer_out, hidden, g_pre, normed_two, attended, gt, g_mixed, ghat, dots_h, dots_l, payload, far_kv, far_w,
     small_sums, bias_sums) = call(
        lambda *refs: middle_kernel(layout_m, *refs),
        "middle",
        [
            ((tokens, width), BF),
            ((tokens, hidden_n), BF),
            ((tokens, hidden_n), BF),
            ((tokens, width), BF),
            ((tokens, width), BF),
            ((tokens, width), BF),
            ((tokens, width), F32),
            ((tokens, width), BF),
            ((tokens, 128), BF),
            ((tokens, 128), BF),
            ((micro_n * BLOCK, 2 * width + 128), BF),
            ((micro_n * 64, 2 * width), BF),
            ((micro_n * 32, width), BF),
            ((micro_n, 8, width), F32),
            ((micro_n, 8, hidden_n), F32),
        ],
        (ints, x, top, remote_bias, vectors, bias_row, *per_local, *arrays_kv, *weights_in),
        scalars=1,
        scratch=[((devices, micro_n * BLOCK, 2 * width), BF)] * direct
        + [
            ((256, 2 * width), BF),
            ((width, width), BF),
            ((width, hidden_n), BF),
            ((hidden_n, width), BF),
        ],
        mib=22,
        us=20.0,
    )

    order = layout["order"]
    wide_in = (me, hidden, g_pre, normed_two, attended, gt, top)
    plain = [((hidden_n, width), BF), ((width, hidden_n), BF), ((width, width), BF)]
    if direct:
        keep_w, sent_w = call(
            lambda *refs: wide_grads_kernel(layout, *refs),
            "wide_grads",
            [((half, 9 * rows, width), BF)] * 2,
            wide_in,
            scalars=1,
            scratch=plain,
            mib=14,
            us=8.0,
        )
    else:
        g_back, g_in, g_out = call(
            lambda *refs: wide_grads_kernel(layout, *refs), "wide_grads", plain, wide_in, scalars=1, mib=14, us=8.0
        )
        stack = jnp.concatenate(
            [g_back.reshape(devices, 4 * rows, width)]
            + [g_in[:, c * width : (c + 1) * width].reshape(devices, rows, width) for c in range(4)]
            + [g_out.reshape(devices, rows, width)],
            axis=1,
        )
        chosen = np.array(order, np.int32)
        stack = exchange_order(stack, position, devices)
        keep_w, sent_w = reordered(stack, chosen), reordered(stack, chosen ^ 1)
    stages = bit_groups(devices)[::-1]
    received_w = [send(sent_w, 1, devices)]

    def local_backward(m, after):
        return call(
            lambda *refs: back_kernel(m, *refs),
            f"local_backward_{m}",
            [((length, 3 * width), F32)],
            (qkv, local[m][2], local[m][3], ghat, dots_h, dots_l, local[m][4], far_w, far_kv),
            scratch=[
                ((length, width), BF),
                ((length, width), BF),
                ((length, 128), BF),
                ((length, 128), BF),
                ((length, 3 * width), BF),
                ((length, length), BF),
                ((PAIRS, 256, 128), BF),
            ],
            mib=12,
            us=8.0,
            after=after,
        )[0]

    grads = [local_backward(0, ())]
    pieces_g = staged_gather(payload, devices, [(keep_w,), (grads[0],)])
    held_w, received_w = scatter_step(keep_w, received_w, stages[0], devices, "add_wide_0", (grads[0],))
    arrivals = [p for p, _ in pieces_g]
    grads.append(local_backward(1, (held_w, *arrivals)))

    arrays_g = [p for p, _ in pieces_g] if direct else [picked(pieces_g, ints, micro_n)]
    layout_l = dict(layout, slots=[sl for _, sl in pieces_g][: len(arrays_g)])
    per_local = [a for m in range(micro_n) for a in (grads[m], local[m][2], local[m][4])]
    last_in = (ints, x, g_mixed, normed, w_qkv, vectors, remote_bias, small_sums, bias_sums, *per_local, *arrays_g)
    scratch = [((devices, micro_n * BLOCK, 2 * width + 128), BF)] * direct + [
        ((256, 2 * width + 128), BF),
        ((tokens, 3 * width), BF),
    ]
    mib = 19
    if direct:
        in_grad, keep_q, sent_q = call(
            lambda *refs: last_kernel(layout_l, *refs),
            "qkv_grads",
            [((tokens, width), F32)] + [((half, 3 * rows + 8, width), BF)] * 2,
            last_in,
            scalars=1,
            scratch=scratch + [((width, 3 * width), BF)],
            mib=mib,
            us=10.0,
        )
    else:
        in_grad, g_qkv, tails = call(
            lambda *refs: last_kernel(layout_l, *refs),
            "qkv_grads",
            [((tokens, width), F32), ((width, 3 * width), BF), ((devices, 256), F32)],
            last_in,
            scalars=1,
            scratch=scratch,
            mib=mib,
            us=10.0,
        )
        stack = jnp.concatenate(
            [g_qkv[:, c * width : (c + 1) * width].reshape(devices, rows, width) for c in range(3)]
            + [jnp.broadcast_to(jnp.pad(tails, ((0, 0), (0, 256)))[:, None, :], (devices, 8, width)).astype(BF)],
            axis=1,
        )
        chosen = np.array(order, np.int32)
        stack = exchange_order(stack, position, devices)
        keep_q, sent_q = reordered(stack, chosen), reordered(stack, chosen ^ 1)
    for stage, group in enumerate(stages):
        if stage == 0:
            held_w, received_w = scatter_step(held_w, received_w, stages[1], devices, "add_wide_1", (keep_q,))
            held_q, received_q = keep_q, [send(follow(sent_q, held_w), 1, devices)]
        elif stage + 1 < len(stages):
            held_w, received_w = scatter_step(held_w, received_w, stages[stage + 1], devices, f"add_wide_{stage + 1}", (held_q,))
        held_q, received_q = scatter_step(held_q, received_q, group, devices, f"add_qkv_{stage}")
    g_back, g_in, g_out = call(
        lambda *refs: finish_wide_kernel(rows, *refs),
        "finish_wide",
        [((4 * rows, width), F32), ((rows, hidden_n), F32), ((rows, width), F32)],
        (held_w, *received_w),
        mib=4,
        us=1.0,
    )
    g_query, g_key, g_value, g_gain, g_shift, g_bias_in, g_bias_out = call(
        lambda *refs: finish_qkv_kernel(rows, *refs),
        "finish_qkv",
        [((rows, width), F32)] * 3
        + [((2, rows), F32)] * 2
        + [((1, hidden_n // devices), F32), ((1, rows), F32)],
        (held_q, *received_q),
        mib=4,
        us=1.0,
    )
    return (
        layer_out.reshape(micro_n, length, width),
        in_grad.reshape(micro_n, length, width),
        g_query,
        g_key,
        g_value,
        g_out,
        g_in,
        g_back,
        g_gain,
        g_shift,
        g_bias_in.reshape(-1),
        g_bias_out.reshape(-1),
    )


def solution(mesh):
    placed = (
        P(None, "fsdp", None),
        P(None, "fsdp", None),
        P(),
        P(),
        P("fsdp", None),
        P("fsdp", None),
        P("fsdp", None),
        P("fsdp", None),
        P("fsdp", None),
        P("fsdp", None),
        P(None, "fsdp"),
        P(None, "fsdp"),
        P("fsdp"),
        P("fsdp"),
    )
    return jax.shard_map(
        on_device,
        mesh=mesh,
        in_specs=placed,
        out_specs=(
            P(None, "fsdp", None),
            P(None, "fsdp", None),
            P("fsdp", None),
            P("fsdp", None),
            P("fsdp", None),
            P("fsdp", None),
            P("fsdp", None),
            P("fsdp", None),
            P(None, "fsdp"),
            P(None, "fsdp"),
            P("fsdp"),
            P("fsdp"),
        ),
        check_vma=False,
    )
```

```python
import math

import jax
import jax.numpy as jnp
import numpy as np
from jax import lax
from jax.experimental import pallas as pl
from jax.experimental.pallas import tpu as pltpu
from jax.sharding import PartitionSpec as P

HEADS = 8
HEAD_DIM = 64
BLOCK = 16
LEVELS = 9
EPSILON = 1e-05
OFF = -1e30
PAIRS = HEADS // 2
WIDE = 2 * HEAD_DIM
SCALE2 = math.log2(math.e) / math.sqrt(HEAD_DIM)
SCALE = 1.0 / math.sqrt(HEAD_DIM)
BF = jnp.bfloat16
F32 = jnp.float32
SIBS = 15
STEP = 512
CHUNK = 1024


def iota(shape, dim):
    return lax.broadcasted_iota(jnp.int32, shape, dim)


def ones_where(condition, value=1.0):
    return jnp.where(condition, value, 0.0).astype(BF)


def coarse_places(index, length):
    shift = jnp.zeros_like(index)
    start = jnp.zeros_like(index)
    row = 0
    for level_id in range(2, LEVELS + 1):
        shift = shift + (index >= row).astype(jnp.int32)
        start = jnp.where(index >= row, row, start)
        row += length >> (level_id - 1)
    return shift, jnp.where(index >= row, length, index - start)


def members(length, first, count, by_rows):
    shape = (count, length) if by_rows else (length, count)
    narrow = (count, 1) if by_rows else (1, count)
    shift, place = coarse_places(iota(narrow, 0 if by_rows else 1) + first, length)
    covers = (iota(shape, 1 if by_rows else 0) >> shift) == place
    return covers, jnp.exp2(-shift.astype(F32))


def mean_rows(length, first, count):
    covers, share = members(length, first, count, True)
    return ones_where(covers, share)


def sum_rows(length, first, count):
    return ones_where(members(length, first, count, True)[0])


def share_columns(length, first, count):
    covers, share = members(length, first, count, False)
    return ones_where(covers, share)


def copy_columns(length, first, count):
    return ones_where(members(length, first, count, False)[0])


def tile_bias(kind, limit=0):
    row = iota((128, 256), 0)
    key = iota((128, 256), 1) & 127
    block_r, block_k = row // BLOCK, key // BLOCK
    sibling = block_r == (block_k ^ 1)
    if kind == 0:
        return jnp.where(block_r // 2 == block_k // 2, 0.0, OFF)
    if kind < 3:
        return jnp.where(sibling, float(kind), OFF)
    last = jnp.where(row < limit, 4.0, OFF)
    return jnp.where(sibling, jnp.where(row < 64, 3.0, last), OFF)


def sibling_rows(mean):
    row = iota((64, 256), 0)
    level, k = row // BLOCK, row % BLOCK
    span = jnp.left_shift(1, level)
    block = span - 1 + (k >> (4 - level))
    inside = k & ((BLOCK >> level) - 1)
    offset = iota((64, 256), 1) - (block * BLOCK + (inside << level))
    chosen = (offset >= 0) & (offset < span)
    return ones_where(chosen, 1.0 / span.astype(F32)) if mean else ones_where(chosen)


def head_columns():
    head = iota((512, 128), 0) // HEAD_DIM
    return ones_where(iota((512, 128), 1) // 2 == 4 * (head // 2) + head % 2)


def minus_columns(pair, keys):
    second = (iota((2 * keys, 128), 0) >= keys).astype(jnp.int32)
    return ones_where(iota((2 * keys, 128), 1) // 2 == 4 * pair + second, -1.0)


def twin_columns():
    return ones_where(iota((128, 128), 0) // 2 == iota((128, 128), 1) // 2)


def mm(a, b):
    return lax.dot_general(a, b, (((1,), (0,)), ((), ())), preferred_element_type=F32)


def mm_nt(a, b):
    return lax.dot_general(a, b, (((1,), (1,)), ((), ())), preferred_element_type=F32)


def mm_tn(a, b):
    return lax.dot_general(a, b, (((0,), (0,)), ((), ())), preferred_element_type=F32)


def split(a):
    high = a.astype(BF)
    return high, (a - high.astype(F32)).astype(BF)


def mm_split(a, b):
    high, low = split(b)
    return mm(a, high) + mm(a, low)


def split_mm(a, b):
    high, low = split(a)
    return mm(high, b) + mm(low, b)


def head_masks():
    lane = lax.broadcasted_iota(jnp.int32, (1, WIDE), 1)
    first = (lane < HEAD_DIM).astype(F32)
    return first, 1.0 - first


def stacked(a, masks):
    return jnp.concatenate([a * masks[0].astype(a.dtype), a * masks[1].astype(a.dtype)], axis=0)


def unstacked(a, masks):
    half = a.shape[0] // 2
    return a[:half] * masks[0] + a[half:] * masks[1]


def head_ones(keys):
    row = lax.broadcasted_iota(jnp.int32, (2 * keys, WIDE), 0)
    lane = lax.broadcasted_iota(jnp.int32, (2 * keys, WIDE), 1)
    return ((row < keys) == (lane < HEAD_DIM)).astype(F32).astype(BF)


def even_columns(high, low):
    col = lax.broadcasted_iota(jnp.int32, high.shape, 1)
    return jnp.where(col % 2 == 0, high.astype(F32), low.astype(F32)).astype(BF)


def normalize(values):
    centre = jnp.mean(values, axis=-1, keepdims=True)
    centred = values - centre
    spread = jnp.mean(centred * centred, axis=-1, keepdims=True)
    inverse = lax.rsqrt(spread + EPSILON)
    return centred * inverse, inverse


def shape_of(shape, dtype):
    return jax.ShapeDtypeStruct(shape, dtype)


def call(body, name, outs, ins, scalars=0, scratch=(), mib=8, us=2.0, after=()):
    vmem = pl.BlockSpec(memory_space=pltpu.VMEM)
    smem = pl.BlockSpec(memory_space=pltpu.SMEM)
    count, late = len(ins), len(after)

    def kernel(*refs):
        body(*refs[:count], *refs[count + late :])

    return pl.pallas_call(
        kernel,
        in_specs=[smem] * scalars + [vmem] * (count - scalars) + [pl.BlockSpec(memory_space=pl.ANY)] * late,
        out_specs=[pl.BlockSpec(memory_space=pltpu.VMEM)] * len(outs),
        out_shape=[shape_of(shape, dtype) for shape, dtype in outs],
        scratch_shapes=[pltpu.VMEM(shape, dtype) for shape, dtype in scratch],
        compiler_params=pltpu.CompilerParams(vmem_limit_bytes=int(mib * 2**20)),
        cost_estimate=pl.CostEstimate(flops=int(us * 1.1e9), transcendentals=0, bytes_accessed=1024),
        name=name,
    )(*ins, *after)


def bit_groups(devices):
    groups = []
    high = devices.bit_length() - 2
    while high >= 1:
        low = max(1, high - 1)
        groups.append(tuple(range(low, high + 1)))
        high = low - 1
    return groups


def offsets_of(group):
    return [sum(1 << b for i, b in enumerate(group) if k >> i & 1) for k in range(1 << len(group))]


def send(value, offset, devices):
    return lax.ppermute(value, "fsdp", [(i, i ^ offset) for i in range(devices)])


def joined(parts):
    return parts[0] if len(parts) == 1 else jnp.concatenate(parts, axis=0)


def follow(values, *earlier):
    return lax.optimization_barrier((values, earlier))[0] if earlier else values


def first_sends(block, devices):
    held = block[None]
    return [held] + [send(held, k, devices) for k in offsets_of(bit_groups(devices)[0])[1:]]


def staged_gather(block, devices, between=(), marks=None, begun=None):
    between = list(between) + [()] * len(bit_groups(devices))
    held = block[None]
    slots = [0]
    groups = bit_groups(devices)
    for group_id, group in enumerate(groups):
        offsets = offsets_of(group)
        parts = begun if begun and group_id == 0 else [held] + [send(held, k, devices) for k in offsets[1:]]
        parts = follow(parts, *between[group_id])
        if group_id < len(groups) - 1:
            held = joined(parts)
            slots = [s ^ k for k in offsets for s in slots]
            if marks is not None:
                marks.append(held)
    return [(p, [s ^ k for s in slots]) for p, k in zip(parts, offsets)]


def core_gather(pieces, devices, after=()):
    held = follow([p for p, _ in pieces], *after)
    return pieces + [(send(p, 1, devices), [s ^ 1 for s in sl]) for p, (_, sl) in zip(held, pieces)]


def crossed_gather(block, cut, devices, marks, earlier):
    groups = bit_groups(devices)
    parts = [block[None]]
    slots = [0]
    for group in groups[:-1]:
        held = joined(parts)
        offsets = offsets_of(group)
        parts = [held] + [send(held, k, devices) for k in offsets[1:]]
        slots = [s ^ k for k in offsets for s in slots]
    parts = follow(parts, *earlier)
    halves = []
    for rows, order in ((slice(0, cut), groups[-1]), (slice(cut, None), groups[-1][::-1])):
        held, own = joined([p[:, rows] for p in parts]), slots
        for bit in order[:-1]:
            held = joined([held, send(held, 1 << bit, devices)])
            own = own + [s ^ (1 << bit) for s in own]
        marks.append(held)
        last = 1 << order[-1]
        halves.append([(held, own), (send(held, last, devices), [s ^ last for s in own])])
    first, second = follow([[p for p, _ in pieces] for pieces in halves], halves[0][1][0], halves[1][1][0])
    return [
        pieces + [(send(p, 1, devices), [s ^ 1 for s in sl]) for p, (_, sl) in zip(held, pieces)]
        for held, pieces in zip((first, second), halves)
    ]


def add_parts(keeps, received, outs_dtype, name, after=()):
    cuts = len(outs_dtype)
    part = keeps[0].shape[0] // cuts
    count = len(keeps)
    sizes = [k.shape[1] for k in keeps]
    ins = [a for arrays in (keeps, *received) for a in arrays]

    def body(*refs):
        outs = refs[len(ins) :]
        for c in range(cuts):
            for i in range(part):
                row = 0
                for j, size in enumerate(sizes):
                    total = refs[j][c * part + i].astype(F32)
                    for r in refs[count + j : len(ins) : count]:
                        total = total + r[c * part + i].astype(F32)
                    outs[c][i, row : row + size] = total.astype(outs[c].dtype)
                    row += size

    shape = (part, sum(sizes)) + keeps[0].shape[2:]
    return call(body, name, [(shape, d) for d in outs_dtype], ins, mib=4, us=1.5, after=after)


def scatter_order(devices):
    order = [0]
    for group in bit_groups(devices)[::-1]:
        order = [s ^ k for s in order for k in offsets_of(group)]
    return order


def scatter_step(held, received, group, devices, name, after=()):
    offsets = offsets_of(group)
    outs = add_parts(held, received, [F32] + [BF] * (len(offsets) - 1), name, after)
    return outs[:1], [[send(o, k, devices)] for o, k in zip(outs[1:], offsets[1:])]


def pack_kernel(rows, wq_ref, wk_ref, wv_ref, wo_ref, wi_ref, wb_ref, gain_ref, shift_ref, bi_ref, bo_ref, first_ref, second_ref):
    for part, ref in enumerate((wq_ref, wk_ref, wv_ref)):
        first_ref[part * rows : (part + 1) * rows, :] = ref[...]
    tail = jnp.zeros((1, 512), F32)
    for ref, at in ((gain_ref, 0), (shift_ref, 2 * rows), (bo_ref, 4 * rows), (bi_ref, 128)):
        for r in range(ref.shape[0]):
            count = ref.shape[1]
            index = lax.broadcasted_iota(jnp.int32, (count, 512), 0)
            lane = lax.broadcasted_iota(jnp.int32, (count, 512), 1)
            place = (lane == index + (at + r * count)).astype(F32).astype(BF)
            tail = tail + mm(ref[r : r + 1, :], place)
    first_ref[3 * rows : 3 * rows + 8, :] = jnp.broadcast_to(tail, (8, 512)).astype(BF)
    second_ref[0 : 4 * rows, :] = wb_ref[...]
    second_ref[4 * rows : 5 * rows, :] = wo_ref[...]
    for c in range(4):
        second_ref[(5 + c) * rows : (6 + c) * rows, :] = wi_ref[:, c * 512 : (c + 1) * 512]


def first_kernel(layout, ints_ref, x_ref, *refs):
    count = len(layout["slots"])
    pieces, refs = refs[:count], refs[count:]
    if not layout["direct"]:
        given, refs = refs[0], refs[1:]
    qkv_ref, norm_ref, w_ref, vec_ref, bias_ref, coarse_ref = refs
    rows, devices = layout["rows"], layout["devices"]
    me = ints_ref[0]
    small = []
    order = []
    if not layout["direct"]:
        w_ref[...] = given[...]
    for ref, slots in zip(pieces, layout["slots"]):
        for i, s in enumerate(slots):
            if layout["direct"]:
                at = pl.multiple_of((me ^ s) * rows, rows)
                for part in range(3):
                    w_ref[pl.ds(at, rows), part * 512 : (part + 1) * 512] = ref[i, part * rows : (part + 1) * rows, :]
            small.append(ref[i, layout["small"] : layout["small"] + 8, :].astype(F32)[:1])
            order.append(s)
    table = jnp.concatenate(small, axis=0)
    vec_ref[...], bias_ref[...] = spread_small(table, order, me, devices)
    for r in range(4):
        part = slice(r * 256, (r + 1) * 256)
        normal, _ = normalize(x_ref[part, :].astype(F32))
        normed = (normal * vec_ref[0:1, :] + vec_ref[2:3, :]).astype(BF)
        norm_ref[part, :] = normed
        qkv = mm(normed, w_ref[...]).astype(BF)
        qkv_ref[part, :] = qkv
        means = jnp.mean(qkv[:, 512:1536].astype(F32).reshape(8, 32, 1024), axis=1)
        coarse_ref[r * 8 : (r + 1) * 8, :] = means.astype(BF)


def slot_numbers(order, shape, dim):
    index = lax.broadcasted_iota(jnp.int32, shape, dim)
    value = jnp.zeros(shape, jnp.int32)
    for bit in range(max(order).bit_length()):
        on = None
        mask = 0
        for k in range((len(order) - 1).bit_length()):
            if order[1 << k] >> bit & 1:
                mask |= 1 << k
        parity = jnp.zeros(shape, jnp.int32)
        for k in range((len(order) - 1).bit_length()):
            if mask >> k & 1:
                parity = parity ^ ((index >> k) & 1)
        value = value | (parity << bit)
    return value


def spread_small(table, order, me, devices):
    w = 512 // devices
    wide = 2048 // devices
    owner = slot_numbers(order, (devices, 512), 0) ^ me
    col = lax.broadcasted_iota(jnp.int32, (devices, 512), 1)
    mine = (col // w == owner).astype(F32)
    lane = lax.broadcasted_iota(jnp.int32, (devices, 128), 1)
    lane_t = lax.broadcasted_iota(jnp.int32, (128, 512), 0)
    col_t = lax.broadcasted_iota(jnp.int32, (128, 512), 1)
    match = (lane_t % w == col_t % w).astype(F32).astype(BF)
    head = table[:, :128]
    rows = []
    for p in range(5):
        own = (head * (lane // w == p).astype(F32)).astype(BF)
        rows.append(jnp.sum(mm(own, match) * mine, axis=0, keepdims=True))
    rows = rows + [jnp.zeros((1, 512), F32)] * 3
    owner_w = slot_numbers(order, (devices, 2048), 0) ^ me
    col_w = lax.broadcasted_iota(jnp.int32, (devices, 2048), 1)
    mine_w = (col_w // wide == owner_w).astype(F32)
    lane_w = lax.broadcasted_iota(jnp.int32, (128, 2048), 0)
    col_tw = lax.broadcasted_iota(jnp.int32, (128, 2048), 1)
    match_w = (lane_w == col_tw % wide).astype(F32).astype(BF)
    bias = jnp.sum(mm(table[:, 128:256].astype(BF), match_w) * mine_w, axis=0, keepdims=True)
    return jnp.concatenate(rows, axis=0), jnp.broadcast_to(bias, (8, 2048))


def local_kernel(
    m, flag_at, ints_ref, qkv_ref, num_ref, den_ref, coarse_ref, w_ref, vbar_ref, vals, num_c, den_c, ones, matrix, biases,
):
    limit = jnp.where(ints_ref[flag_at + m] > 0, 64, 96)
    masks = head_masks()
    ones[...] = head_ones(128)
    length = num_ref.shape[0]
    base = m * length
    whole = slice(base, base + length)
    value = qkv_ref[whole, 1024:1536].astype(F32)
    vbar = jnp.mean(value, axis=0, keepdims=True)
    vbar_ref[...] = jnp.broadcast_to(vbar, (8, 512))
    vals[...] = (value - vbar).astype(BF)
    matrix[...] = mean_rows(length, 0, length)
    for kind in range(4):
        biases[kind] = tile_bias(kind, limit)
    coarse_ref[:, 0:1024] = mm(matrix[...], qkv_ref[whole, 0:1024]).astype(BF)
    coarse_ref[:, 1024:1536] = mm(matrix[...], vals[...]).astype(BF)
    for t in range(8):
        rows = slice((t % 4) * 128, (t % 4) * 128 + 128)
        far = slice(base + (t % 4) * 128, base + (t % 4) * 128 + 128)
        kind = 0 if t < 4 else (1, 1, 2, 3)[t - 4]
        bias = biases[kind]
        for p in range(PAIRS):
            lanes = slice(p * WIDE, (p + 1) * WIDE)
            lanes_k = slice(512 + p * WIDE, 512 + (p + 1) * WIDE)
            if t < 4:
                q, k, v = qkv_ref[far, lanes], qkv_ref[far, lanes_k], vals[rows, lanes]
            else:
                q, k = coarse_ref[rows, lanes], coarse_ref[rows, lanes_k]
                v = coarse_ref[rows, 1024 + p * WIDE : 1024 + (p + 1) * WIDE]
            scores = mm_nt(q, stacked(k, masks))
            weights = jnp.exp2(scores * SCALE2 + bias).astype(BF)
            w_ref[t, :, p * 256 : (p + 1) * 256] = weights
            both = mm(weights, jnp.concatenate([stacked(v, masks), ones[...]], axis=1))
            if t < 4:
                num_ref[rows, lanes] = both[:, :WIDE]
                den_ref[rows, lanes] = both[:, WIDE:]
            else:
                num_c[rows, lanes] = both[:, :WIDE]
                den_c[rows, lanes] = both[:, WIDE:]
    matrix[...] = copy_columns(length, 0, length)
    num_ref[...] += mm_split(matrix[...], num_c[...])
    den_ref[...] += mm_split(matrix[...], den_c[...])


def fill_slots(pieces, slots, target):
    for ref, sl in zip(pieces, slots):
        for i, s in enumerate(sl):
            target[s] = ref[i]


def take_siblings(layout, ints_ref, m, source, buf):
    for b in range(SIBS):
        if layout["direct"]:
            slot = ints_ref[layout["first_slot"] + m * SIBS + b]
            block = source[slot, m * BLOCK : (m + 1) * BLOCK, :]
        else:
            block = source[m * SIBS + b]
        buf[b * BLOCK : (b + 1) * BLOCK, :] = block


def middle_kernel(layout, ints_ref, x_ref, go_ref, rb_ref, vec_ref, bias_ref, *refs):
    local, refs = (refs[0:4], refs[4:8]), refs[8:]
    count = len(layout["slots"])
    kv_pieces, weights = refs[:count], refs[count : count + layout["n_weights"]]
    (out_ref, hid_ref, gpre_ref, norm_ref, att_ref, gt_ref, gmix_ref, ghat_ref, ch_ref, cl_ref, pay_ref,
     kvr_ref, wr_ref, small_ref, sbias_ref) = refs[count + layout["n_weights"] : count + layout["n_weights"] + 15]
    scratch = refs[count + layout["n_weights"] + 15 :]
    kvs, (buf, w_out, w_in, w_back, far_num, far_den) = scratch[0], scratch[-6:]
    me = ints_ref[0]
    rows = layout["rows"]
    length = local[0][0].shape[0]
    buf[...] = jnp.zeros_like(buf)
    if layout["direct"]:
        fill_slots(kv_pieces, layout["slots"], kvs)
        for ref, sl in zip(weights, layout["wslots"]):
            for i, s in enumerate(sl):
                d = me ^ s
                at = pl.multiple_of(d * rows, rows)
                if ref.shape[1] == 5 * rows:
                    w_back[pl.ds(pl.multiple_of(d * 4 * rows, 4 * rows), 4 * rows), :] = ref[i, 0 : 4 * rows, :]
                    w_out[pl.ds(at, rows), :] = ref[i, 4 * rows : 5 * rows, :]
                else:
                    for c in range(4):
                        w_in[pl.ds(at, rows), c * 512 : (c + 1) * 512] = ref[i, c * rows : (c + 1) * rows, :]
    else:
        w_out[...] = weights[0][...]
        w_in[...] = weights[1][...]
        w_back[...] = weights[2][...]

    masks = head_masks()
    ones = head_ones(64)
    select = sibling_rows(True)
    spread = copy_columns(length, length - 32, 32)
    sums = sum_rows(length, length - 32, BLOCK)
    columns = head_columns()
    for m in range(2):
        num_ref, den_ref, vbar_ref, coarse_ref = local[m]
        vbar = vbar_ref[0:1, :]
        far_q = coarse_ref[length - 32 : length, 0:512]
        take_siblings(layout, ints_ref, m, kvs if layout["direct"] else kv_pieces[0], buf)
        remote = mm(select, buf[...])
        key_r = remote[:, 0:512].astype(BF)
        val_r = (remote[:, 512:1024].astype(BF).astype(F32) - vbar).astype(BF)
        kvr_ref[m * 64 : (m + 1) * 64, 0:512] = key_r
        kvr_ref[m * 64 : (m + 1) * 64, 512:1024] = val_r
        rb = rb_ref[m]
        nums = []
        dens = []
        for p in range(PAIRS):
            lanes = slice(p * WIDE, (p + 1) * WIDE)
            scores = mm_nt(far_q[:, lanes], stacked(key_r[:, lanes], masks))
            wr = jnp.exp2(scores * SCALE2 + rb).astype(BF)
            wr_ref[m * 32 : (m + 1) * 32, lanes] = wr
            both = mm(wr, jnp.concatenate([stacked(val_r[:, lanes], masks), ones], axis=1))
            nums.append(both[:, :WIDE])
            dens.append(both[:, WIDE:])
        far_num[...] = jnp.concatenate(nums, axis=1)
        far_den[...] = jnp.concatenate(dens, axis=1)
        for r in range(0, length, STEP):
            own = slice(r, r + STEP)
            part = slice(m * length + r, m * length + r + STEP)
            num = num_ref[own, :] + mm_split(spread[own, :], far_num[...])
            den = den_ref[own, :] + mm_split(spread[own, :], far_den[...])
            inverse_den = 1.0 / den
            centred_o = num * inverse_den
            attended = (centred_o + vbar).astype(BF)
            att_ref[part, :] = attended
            mixed = x_ref[part, :].astype(F32) + mm(attended, w_out[...])
            normal, inverse = normalize(mixed)
            normed = (normal * vec_ref[1:2, :] + vec_ref[3:4, :]).astype(BF)
            norm_ref[part, :] = normed
            top_b = go_ref[part, :]
            result = mixed + vec_ref[4:5, :]
            g_norm = jnp.zeros_like(mixed)
            def products(c):
                lanes = slice(c * CHUNK, (c + 1) * CHUNK)
                return mm(normed, w_in[:, lanes]), mm_nt(top_b, w_back[lanes, :])

            ahead = products(0)
            for c in range(2048 // CHUNK):
                lanes = slice(c * CHUNK, (c + 1) * CHUNK)
                pre, g_hidden = ahead
                if c + 1 < 2048 // CHUNK:
                    ahead = products(c + 1)
                pre = pre + bias_ref[0:1, lanes]
                cdf = 0.5 + 0.5 * lax.erf(pre * math.sqrt(0.5))
                hidden = (pre * cdf).astype(BF)
                hid_ref[part, lanes] = hidden
                slope = cdf + pre * (jnp.exp(-0.5 * pre * pre) * (1.0 / math.sqrt(2.0 * math.pi)))
                g_pre = g_hidden * slope
                total = jnp.broadcast_to(jnp.sum(g_pre, axis=0, keepdims=True), (8, CHUNK))
                sbias_ref[m, :, lanes] = total if r == 0 else sbias_ref[m, :, lanes] + total
                g_pre_b = g_pre.astype(BF)
                gpre_ref[part, lanes] = g_pre_b
                result = result + mm(hidden, w_back[lanes, :])
                g_norm = g_norm + mm_nt(g_pre_b, w_in[:, lanes])
            out_ref[part, :] = result.astype(BF)
            top = top_b.astype(F32)
            scaled = g_norm * vec_ref[1:2, :]
            g_mixed = top + (
                scaled
                - jnp.mean(scaled, axis=-1, keepdims=True)
                - normal * jnp.mean(scaled * normal, axis=-1, keepdims=True)
            ) * inverse
            gmix_ref[part, :] = g_mixed
            total = jnp.concatenate(
                [
                    jnp.sum(g_norm * normal, axis=0, keepdims=True),
                    jnp.sum(g_norm, axis=0, keepdims=True),
                    jnp.sum(top, axis=0, keepdims=True),
                    jnp.zeros((5, 512), F32),
                ],
                axis=0,
            )
            small_ref[m] = total if r == 0 else small_ref[m] + total
            gt = g_mixed.astype(BF)
            gt_ref[part, :] = gt
            ghat = (mm_nt(gt, w_out[...]) * inverse_den).astype(BF)
            ghat_ref[part, :] = ghat
            dots = split_mm(ghat.astype(F32) * centred_o, columns)
            dots_h, dots_l = split(dots)
            ch_ref[part, :] = dots_h
            cl_ref[part, :] = dots_l
        part = slice(m * length, (m + 1) * length)
        g_sum = mm(sums, ghat_ref[part, :]).astype(BF)
        c_sum = mm(sums, ch_ref[part, :]) + mm(sums, cl_ref[part, :])
        c_sum = c_sum + split_mm(g_sum.astype(F32) * vbar, columns)
        c_h, c_l = split(c_sum)
        pay = slice(m * BLOCK, (m + 1) * BLOCK)
        pay_ref[pay, 0:512] = far_q[0:BLOCK, :]
        pay_ref[pay, 512:1024] = g_sum
        pay_ref[pay, 1024:1152] = even_columns(c_h, c_l)


def wide_in_kernel(layout, me_ref, gpre_ref, norm_ref, att_ref, gt_ref, *refs):
    rows = layout["rows"]
    up, out = refs[-2:]
    for c in range(4):
        lanes = slice(c * 512, (c + 1) * 512)
        up[:, lanes] = mm_tn(norm_ref[...], gpre_ref[:, lanes]).astype(BF)
    out[...] = mm_tn(att_ref[...], gt_ref[...]).astype(BF)
    if layout["direct"]:
        for half, ref in enumerate(refs[:2]):
            for i, s in enumerate(layout["order"]):
                at = pl.multiple_of((me_ref[0] ^ (s ^ half)) * rows, rows)
                for c in range(4):
                    ref[i, c * rows : (c + 1) * rows, :] = up[pl.ds(at, rows), c * 512 : (c + 1) * 512]
                ref[i, 4 * rows : 5 * rows, :] = out[pl.ds(at, rows), :]


def wide_back_kernel(layout, me_ref, hid_ref, go_ref, *refs):
    rows = 4 * layout["rows"]
    back = refs[-1]
    for c in range(4):
        lanes = slice(c * 512, (c + 1) * 512)
        back[lanes, :] = mm_tn(hid_ref[:, lanes], go_ref[...]).astype(BF)
    if layout["direct"]:
        for half, ref in enumerate(refs[:2]):
            for i, s in enumerate(layout["order"]):
                at = pl.multiple_of((me_ref[0] ^ (s ^ half)) * rows, rows)
                ref[i] = back[pl.ds(at, rows), :]


def back_kernel(m, qkv_ref, coarse_ref, w_ref, ghat_ref, ch_ref, cl_ref, vbar_ref, wr_ref, kvr_ref, grad_ref,
                vals, gsum, ext_f, ext_c, gcoarse, matrix, minus_ref):
    masks = head_masks()
    length = vals.shape[0]
    base = m * length
    whole = slice(base, base + length)
    vals[...] = (qkv_ref[whole, 1024:1536].astype(F32) - vbar_ref[0:1, :]).astype(BF)
    matrix[...] = sum_rows(length, 0, length)
    for p in range(PAIRS):
        minus_ref[p] = minus_columns(p, 128)
    gsum[...] = mm(matrix[...], ghat_ref[whole, :]).astype(BF)
    c_sum = mm(matrix[...], ch_ref[whole, :]) + mm(matrix[...], cl_ref[whole, :])
    c_h, c_l = split(c_sum)
    ext_c[...] = even_columns(c_h, c_l)
    ext_f[...] = even_columns(ch_ref[whole, :], cl_ref[whole, :])
    zero = jnp.zeros((128, WIDE), BF)
    for t in range(8):
        rows = slice((t % 4) * 128, (t % 4) * 128 + 128)
        far = slice(base + (t % 4) * 128, base + (t % 4) * 128 + 128)
        for p in range(PAIRS):
            lanes = slice(p * WIDE, (p + 1) * WIDE)
            lanes_k = slice(512 + p * WIDE, 512 + (p + 1) * WIDE)
            lanes_v = slice(1024 + p * WIDE, 1024 + (p + 1) * WIDE)
            if t < 4:
                q, k, v = qkv_ref[far, lanes], qkv_ref[far, lanes_k], vals[rows, lanes]
                g, ext = ghat_ref[far, lanes], ext_f[rows, :]
            else:
                q, k, v = coarse_ref[rows, lanes], coarse_ref[rows, lanes_k], coarse_ref[rows, lanes_v]
                g, ext = gsum[rows, lanes], ext_c[rows, :]
            weights = w_ref[t, :, p * 256 : (p + 1) * 256]
            left = jnp.concatenate([g, ext], axis=1)
            right = jnp.concatenate([stacked(v, masks), minus_ref[p]], axis=1)
            gs = (weights.astype(F32) * mm_nt(left, right)).astype(BF)
            g_q = mm(gs, stacked(k, masks)) * SCALE
            g_kv = mm_tn(
                jnp.concatenate([gs, weights], axis=0),
                jnp.concatenate([jnp.concatenate([q, zero], axis=1), jnp.concatenate([zero, g], axis=1)], axis=0),
            )
            g_k = unstacked(g_kv[:, :WIDE], masks) * SCALE
            g_v = unstacked(g_kv[:, WIDE:], masks)
            if t < 4:
                grad_ref[rows, lanes] = g_q
                grad_ref[rows, lanes_k] = g_k
                grad_ref[rows, lanes_v] = g_v
            else:
                gcoarse[rows, lanes] = g_q.astype(BF)
                gcoarse[rows, lanes_k] = g_k.astype(BF)
                gcoarse[rows, lanes_v] = g_v.astype(BF)
    far = slice(480, 512)
    for p in range(PAIRS):
        lanes = slice(p * WIDE, (p + 1) * WIDE)
        left = jnp.concatenate([gsum[far, lanes], ext_c[far, :]], axis=1)
        minus = minus_columns(p, 64)
        part = slice(m * 64, (m + 1) * 64)
        right = jnp.concatenate([stacked(kvr_ref[part, 512 + p * WIDE : 512 + (p + 1) * WIDE], masks), minus], axis=1)
        gs = (wr_ref[m * 32 : (m + 1) * 32, lanes].astype(F32) * mm_nt(left, right)).astype(BF)
        gcoarse[far, lanes] = (mm(gs, stacked(kvr_ref[part, lanes], masks)) * SCALE).astype(BF)
    matrix[...] = share_columns(length, 0, length)
    grad_ref[...] += mm(matrix[...], gcoarse[...])


def last_kernel(layout, ints_ref, x_ref, gmix_ref, norm_ref, w_ref, vec_ref, rb_ref, small_ref, sbias_ref, *refs):
    local, refs = (refs[0:3], refs[3:6]), refs[6:]
    count = len(layout["slots"])
    pieces = refs[:count]
    if layout["direct"]:
        ingrad_ref, keep_ref, sent_ref, slots_v, buf, gqkv, wgrad = refs[count:]
    else:
        ingrad_ref, wgrad, tail_ref, buf, gqkv = refs[count:]
    me = ints_ref[0]
    rows = layout["rows"]
    devices = layout["devices"]
    masks = head_masks()
    if layout["direct"]:
        fill_slots(pieces, layout["slots"], slots_v)
    buf[...] = jnp.zeros_like(buf)
    length = x_ref.shape[0] // 2
    lane = lax.broadcasted_iota(jnp.int32, (1, 128), 1)
    select, select_sum = sibling_rows(True), sibling_rows(False)
    spread = share_columns(length, length - 32, 32)
    columns, twins = head_columns(), twin_columns()
    for m in range(2):
        grad_ref, coarse_ref, vbar_ref = local[m]
        vbar = vbar_ref[0:1, :]
        take_siblings(layout, ints_ref, m, slots_v if layout["direct"] else pieces[0], buf)
        q_r = mm(select, buf[:, 0:512]).astype(BF)
        g_r = mm(select_sum, buf[:, 512:1024]).astype(BF)
        c_r = mm_split(select_sum, mm(buf[:, 1024:1152], twins))
        c_r = c_r - split_mm(g_r.astype(F32) * vbar, columns)
        c_h, c_l = split(c_r)
        ext = even_columns(c_h, c_l).astype(F32)
        rb = rb_ref[m]
        g_keys = []
        g_vals = []
        for p in range(PAIRS):
            lanes = slice(p * WIDE, (p + 1) * WIDE)
            k = coarse_ref[length - 32 : length, 512 + p * WIDE : 512 + (p + 1) * WIDE]
            v = coarse_ref[length - 32 : length, 1024 + p * WIDE : 1024 + (p + 1) * WIDE]
            qq = stacked(q_r[:, lanes], masks)
            gg = stacked(g_r[:, lanes], masks)
            weights = jnp.exp2(mm_nt(k, qq) * SCALE2 + rb)
            ones_a = ((lane // 2) == 4 * p).astype(F32)
            ones_b = ((lane // 2) == 4 * p + 1).astype(F32)
            ext_p = jnp.concatenate([ext * ones_a, ext * ones_b], axis=0).astype(BF)
            left = jnp.concatenate([v, jnp.full((32, 128), -1.0, BF)], axis=1)
            gs = (weights * mm_nt(left, jnp.concatenate([gg, ext_p], axis=1))).astype(BF)
            g_keys.append(mm(gs, qq) * SCALE)
            g_vals.append(mm(weights.astype(BF), gg))
        extra = mm_split(spread, jnp.concatenate(g_keys + g_vals, axis=1))
        part = slice(m * length, (m + 1) * length)
        gqkv[part, 0:512] = grad_ref[:, 0:512].astype(BF)
        gqkv[part, 512:1536] = (grad_ref[:, 512:1536] + extra).astype(BF)
    g_norm = mm_nt(gqkv[...], w_ref[...])
    normal, inverse = normalize(x_ref[...].astype(F32))
    scaled = g_norm * vec_ref[0:1, :]
    ingrad_ref[...] = gmix_ref[...] + (
        scaled
        - jnp.mean(scaled, axis=-1, keepdims=True)
        - normal * jnp.mean(scaled * normal, axis=-1, keepdims=True)
    ) * inverse
    for part in range(3):
        lanes = slice(part * 512, (part + 1) * 512)
        wgrad[:, lanes] = mm_tn(norm_ref[...], gqkv[:, lanes]).astype(BF)
    vectors = [
        jnp.sum(g_norm * normal, axis=0, keepdims=True),
        small_ref[0, 0:1, :] + small_ref[1, 0:1, :],
        jnp.sum(g_norm, axis=0, keepdims=True),
        small_ref[0, 1:2, :] + small_ref[1, 1:2, :],
        small_ref[0, 2:3, :] + small_ref[1, 2:3, :],
    ]
    bias = sbias_ref[0, 0:1, :] + sbias_ref[1, 0:1, :]
    halves = ((0, 0), (1, 1)) if layout["direct"] else ((None, None),)
    for half, _ in halves:
        order = list(layout["order"]) if half is not None else list(range(devices))
        owner = slot_numbers(order, (len(order), 1), 0)
        if half is not None:
            owner = (owner ^ half) ^ me
        tail = gather_small(vectors, bias, owner, devices)
        if half is None:
            tail_ref[...] = tail
            continue
        ref = (keep_ref, sent_ref)[half]
        for i, s in enumerate(order):
            at = pl.multiple_of((me ^ (s ^ half)) * rows, rows)
            for part in range(3):
                ref[i, part * rows : (part + 1) * rows, :] = wgrad[pl.ds(at, rows), part * 512 : (part + 1) * 512]
            ref[i, 3 * rows : 3 * rows + 8, 0:256] = jnp.broadcast_to(tail[i : i + 1, :], (8, 256)).astype(BF)
            ref[i, 3 * rows : 3 * rows + 8, 256:512] = jnp.zeros((8, 256), BF)


def gather_small(vectors, bias, owner, devices):
    w = 512 // devices
    wide = 2048 // devices
    count = owner.shape[0]
    col = lax.broadcasted_iota(jnp.int32, (count, 512), 1)
    mine = (col // w == owner).astype(F32)
    col_t = lax.broadcasted_iota(jnp.int32, (512, 128), 0)
    lane_t = lax.broadcasted_iota(jnp.int32, (512, 128), 1)
    total = jnp.zeros((count, 128), F32)
    for p, row in enumerate(vectors):
        place = ((lane_t // w == p) & (lane_t % w == col_t % w)).astype(F32).astype(BF)
        total = total + split_mm(row * mine, place)
    col_w = lax.broadcasted_iota(jnp.int32, (count, 2048), 1)
    mine_w = (col_w // wide == owner).astype(F32)
    col_tw = lax.broadcasted_iota(jnp.int32, (2048, 128), 0)
    lane_tw = lax.broadcasted_iota(jnp.int32, (2048, 128), 1)
    place_w = (lane_tw == col_tw % wide).astype(F32).astype(BF)
    return jnp.concatenate([total, split_mm(bias * mine_w, place_w)], axis=1)


def total_of(refs, rows):
    total = refs[0][0, rows, :].astype(F32)
    for r in refs[1:]:
        total = total + r[0, rows, :].astype(F32)
    return total


def finish_wide_kernel(rows, *refs):
    ins, (back_ref, in_ref, out_ref) = refs[:-3], refs[-3:]
    for c in range(4):
        in_ref[:, c * 512 : (c + 1) * 512] = total_of(ins, slice(c * rows, (c + 1) * rows))
    out_ref[...] = total_of(ins, slice(4 * rows, 5 * rows))
    back_ref[...] = total_of(ins, slice(5 * rows, 9 * rows))


def finish_qkv_kernel(rows, *refs):
    ins, (q_ref, k_ref, v_ref, gain_ref, shift_ref, bi_ref, bo_ref) = refs[:-7], refs[-7:]
    for part, ref in enumerate((q_ref, k_ref, v_ref)):
        ref[...] = total_of(ins, slice(part * rows, (part + 1) * rows))
    tail = total_of(ins, slice(3 * rows, 3 * rows + 8))[0:1]
    for r in range(2):
        gain_ref[r : r + 1, :] = tail[:, r * rows : (r + 1) * rows]
        shift_ref[r : r + 1, :] = tail[:, (2 + r) * rows : (3 + r) * rows]
    bo_ref[...] = tail[:, 4 * rows : 5 * rows]
    bi_ref[...] = tail[:, 128 : 128 + bi_ref.shape[1]]


def remote_plan(lengths, group_order, position, devices, length):
    count = lengths.shape[1]
    lower = np.tril(np.ones((count, count), np.int32))
    seq_ends = jnp.sum(lengths[:, None, :] * lower[None], axis=2)
    device_ids = np.arange(devices, dtype=np.int32)
    group_id = jnp.sum(jnp.where(device_ids == position, group_order, 0), axis=1)[:, None]
    level_s = np.repeat(np.arange(4, dtype=np.int32), [1, 2, 4, 8])
    index_s = np.concatenate([np.arange(1 << level, dtype=np.int32) for level in range(4)])
    siblings = (((group_id >> level_s) ^ 1) << level_s) + index_s
    owner = jnp.sum(jnp.where(group_order[:, None, :] == siblings[:, :, None], device_ids, 0), axis=2)
    level_q = np.full((32,), -1, np.int32)
    start_q = np.zeros((32,), np.int32)
    row = 0
    for level in range(4):
        for i in range(length // (32 << level)):
            level_q[row] = level
            start_q[row] = i * (32 << level)
            row += 1
    level_k = np.tile(np.repeat(np.arange(4, dtype=np.int32), BLOCK), 2)
    start_k = np.tile(np.arange(BLOCK, dtype=np.int32), 8) * (32 << level_k)
    first_k = (((group_id >> level_k) ^ 1) << level_k) * length
    starts = np.concatenate([start_q, np.array([0, length // 2], np.int32)])
    places = jnp.concatenate([first_k + start_k, group_id * length + starts], axis=1)
    seq = jnp.sum((places[:, :, None] >= seq_ends[:, None, :]).astype(jnp.int32), axis=2)
    same = (seq[:, 128:160, None] == seq[:, None, :128]) & (level_q[:, None] == level_k[None, :])
    bias = jnp.where(same, (level_k + 5).astype(np.float32), OFF)
    apart = (seq[:, 160] != seq[:, 161]).astype(jnp.int32)
    ints = jnp.concatenate([jnp.reshape(position, (1,)), (owner ^ position).reshape(-1), apart]).astype(jnp.int32)
    return ints, bias


def exchange_order(stack, position, devices):
    rest = stack.shape[1:]
    for bit in range(devices.bit_length() - 1):
        cut = stack.reshape((devices >> (bit + 1), 2, 1 << bit) + rest)
        stack = jnp.where((position >> bit) & 1 > 0, cut[:, ::-1], cut).reshape((devices,) + rest)
    return stack


def reordered(stack, order):
    return jnp.concatenate([stack[int(i) : int(i) + 1] for i in order], axis=0)


def natural(pieces, position, devices):
    order = [s for _, sl in pieces for s in sl]
    stack = jnp.concatenate([p for p, _ in pieces], axis=0)
    return exchange_order(reordered(stack, np.argsort(np.array(order))), position, devices)


def picked(pieces, ints, micro_n):
    order = [s for _, sl in pieces for s in sl]
    stack = reordered(jnp.concatenate([p for p, _ in pieces], axis=0), np.argsort(np.array(order)))
    blocks = []
    for m in range(micro_n):
        for b in range(SIBS):
            block = lax.dynamic_slice_in_dim(stack, ints[1 + m * SIBS + b], 1, axis=0)
            blocks.append(block[:, m * BLOCK : (m + 1) * BLOCK])
    return jnp.concatenate(blocks, axis=0)


def on_device(
    layer_in,
    out_grad,
    lengths,
    group_order,
    w_query,
    w_key,
    w_value,
    w_out,
    w_in,
    w_back,
    norm_gain,
    norm_shift,
    ffn_bias_in,
    ffn_bias_out,
):
    devices = lax.axis_size("fsdp")
    position = lax.axis_index("fsdp")
    micro_n, length, width = layer_in.shape
    hidden_n = w_in.shape[1]
    tokens = micro_n * length
    rows = w_query.shape[0]
    half = devices // 2
    direct = rows % 16 == 0
    x = layer_in.reshape(tokens, width)
    top = out_grad.reshape(tokens, width)

    small_rows = -(-3 * rows // 8) * 8
    biases = (ffn_bias_in.reshape(1, -1), ffn_bias_out.reshape(1, -1))
    if direct:
        shards = (w_query, w_key, w_value, w_out, w_in, w_back, norm_gain, norm_shift, *biases)
        packed, packed_w = pl.pallas_call(
            lambda *refs: pack_kernel(rows, *refs),
            grid=(1,),
            in_specs=[pl.BlockSpec(a.shape, lambda i: (0, 0)) for a in shards],
            out_specs=[pl.BlockSpec(memory_space=pltpu.VMEM)] * 2,
            out_shape=[shape_of((3 * rows + 8, width), BF), shape_of((9 * rows, width), BF)],
            name="pack",
        )(*shards)
    else:
        tail = jnp.concatenate(
            [
                norm_gain.reshape(-1),
                norm_shift.reshape(-1),
                ffn_bias_out,
                jnp.zeros((128 - 5 * rows,), BF),
                ffn_bias_in,
                jnp.zeros((384 - ffn_bias_in.shape[0],), BF),
            ]
        )
        packed = jnp.concatenate(
            [
                w_query,
                w_key,
                w_value,
                jnp.zeros((small_rows - 3 * rows, width), BF),
                jnp.broadcast_to(tail[None, :], (8, width)),
            ],
            axis=0,
        )
        packed_w = jnp.concatenate(
            [w_back, w_out] + [w_in[:, c * width : (c + 1) * width] for c in range(hidden_n // width)], axis=0
        )
    marks_q, marks_w = [], []
    pieces_q = core_gather(staged_gather(packed, devices, marks=marks_q), devices)
    lengths, group_order = follow((lengths, group_order), marks_q[0])
    pieces_bo, pieces_in = crossed_gather(packed_w, 5 * rows, devices, marks_w, [])
    ints, remote_bias = remote_plan(lengths, group_order, position, devices, length)

    layout = {
        "rows": rows,
        "devices": devices,
        "direct": direct,
        "small": small_rows,
        "slots": [sl for _, sl in pieces_q],
        "first_slot": 1,
        "order": scatter_order(devices),
    }
    flag_at = 1 + micro_n * SIBS
    arrays_q = [p for p, _ in pieces_q]
    if not direct:
        nat = natural(pieces_q, position, devices)
        arrays_q.append(
            jnp.concatenate([nat[:, part * rows : (part + 1) * rows].reshape(width, width) for part in range(3)], axis=1)
        )
    me = jnp.reshape(position, (1,)).astype(jnp.int32)
    qkv, normed, w_qkv, vectors, bias_row, coarse_kv = call(
        lambda *refs: first_kernel(layout, *refs),
        "norm_qkv",
        [
            ((tokens, 3 * width), BF),
            ((tokens, width), BF),
            ((width, 3 * width), BF),
            ((8, width), F32),
            ((8, hidden_n), F32),
            ((micro_n * BLOCK, 2 * width), BF),
        ],
        (ints, x, *arrays_q),
        scalars=1,
        mib=12,
        us=5.0,
    )

    local = [
        call(
            lambda *refs, m=m: local_kernel(m, flag_at, *refs),
            f"local_forward_{m}",
            [
                ((length, width), F32),
                ((length, width), F32),
                ((length, 3 * width), BF),
                ((8, 128, 256 * PAIRS), BF),
                ((8, width), F32),
            ],
            (ints, qkv),
            scalars=1,
            scratch=[
                ((length, width), BF),
                ((length, width), F32),
                ((length, width), F32),
                ((256, WIDE), BF),
                ((length, length), BF),
                ((4, 128, 256), F32),
            ],
            mib=12,
            us=4.0,
            after=marks_w if m == 0 else (),
        )
        for m in range(micro_n)
    ]

    pieces_kv = staged_gather(coarse_kv, devices, [(local[0][4], *marks_w), (local[1][4],)])
    pieces_kv = core_gather(pieces_kv, devices)
    arrays_kv = [p for p, _ in pieces_kv] if direct else [picked(pieces_kv, ints, micro_n)]
    if direct:
        weights_in = [p for p, _ in pieces_bo + pieces_in]
    else:
        nat_bo, nat_in = natural(pieces_bo, position, devices), natural(pieces_in, position, devices)
        weights_in = [
            nat_bo[:, 4 * rows :].reshape(width, width),
            jnp.concatenate([nat_in[:, c * rows : (c + 1) * rows].reshape(width, width) for c in range(4)], axis=1),
            nat_bo[:, : 4 * rows].reshape(hidden_n, width),
        ]
    layout_m = dict(
        layout,
        slots=[sl for _, sl in pieces_kv][: len(arrays_kv)],
        wslots=[sl for _, sl in pieces_bo + pieces_in],
        n_weights=len(weights_in),
    )
    per_local = [a for num, den, coarse, _, vbar in local for a in (num, den, vbar, coarse)]
    (layer_out, hidden, g_pre, normed_two, attended, gt, g_mixed, ghat, dots_h, dots_l, payload, far_kv, far_w,
     small_sums, bias_sums) = call(
        lambda *refs: middle_kernel(layout_m, *refs),
        "middle",
        [
            ((tokens, width), BF),
            ((tokens, hidden_n), BF),
            ((tokens, hidden_n), BF),
            ((tokens, width), BF),
            ((tokens, width), BF),
            ((tokens, width), BF),
            ((tokens, width), F32),
            ((tokens, width), BF),
            ((tokens, 128), BF),
            ((tokens, 128), BF),
            ((micro_n * BLOCK, 2 * width + 128), BF),
            ((micro_n * 64, 2 * width), BF),
            ((micro_n * 32, width), BF),
            ((micro_n, 8, width), F32),
            ((micro_n, 8, hidden_n), F32),
        ],
        (ints, x, top, remote_bias, vectors, bias_row, *per_local, *arrays_kv, *weights_in),
        scalars=1,
        scratch=[((devices, micro_n * BLOCK, 2 * width), BF)] * direct
        + [
            ((256, 2 * width), BF),
            ((width, width), BF),
            ((width, hidden_n), BF),
            ((hidden_n, width), BF),
            ((32, width), F32),
            ((32, width), F32),
        ],
        mib=22,
        us=20.0,
    )

    order = np.array(layout["order"], np.int32)
    stages = bit_groups(devices)[::-1]

    def halves(stack):
        stack = exchange_order(stack, position, devices)
        return reordered(stack, order), reordered(stack, order ^ 1)

    def wide_grads(body, name, ins, plain, count, after):
        blocks = [((half, count, width), BF)] * 2
        return call(
            lambda *refs: body(layout, *refs),
            name,
            blocks if direct else plain,
            ins,
            scalars=1,
            scratch=plain if direct else (),
            mib=10,
            us=3.0,
            after=after,
        )

    begun = first_sends(payload, devices)
    grads_a = wide_grads(
        wide_in_kernel,
        "wide_in",
        (me, g_pre, normed_two, attended, gt),
        [((width, hidden_n), BF), ((width, width), BF)],
        5 * rows,
        (begun[1],),
    )
    grads_b = wide_grads(
        wide_back_kernel, "wide_back", (me, hidden, top), [((hidden_n, width), BF)], 4 * rows, (begun[1],)
    )
    pieces_g = staged_gather(payload, devices, [(grads_a[0], grads_b[0])], begun=begun)
    if direct:
        keeps, sents = (grads_a[0], grads_b[0]), (grads_a[1], grads_b[1])
    else:
        g_in, g_out = grads_a
        stack = [g_in[:, c * width : (c + 1) * width].reshape(devices, rows, width) for c in range(4)]
        stack = jnp.concatenate(stack + [g_out.reshape(devices, rows, width)], axis=1)
        keeps, sents = zip(halves(stack), halves(grads_b[0].reshape(devices, 4 * rows, width)))
    arrived = [send(a, 1, devices) for a in sents]

    def local_backward(m, after):
        return call(
            lambda *refs: back_kernel(m, *refs),
            f"local_backward_{m}",
            [((length, 3 * width), F32)],
            (qkv, local[m][2], local[m][3], ghat, dots_h, dots_l, local[m][4], far_w, far_kv),
            scratch=[
                ((length, width), BF),
                ((length, width), BF),
                ((length, 128), BF),
                ((length, 128), BF),
                ((length, 3 * width), BF),
                ((length, length), BF),
                ((PAIRS, 256, 128), BF),
            ],
            mib=12,
            us=8.0,
            after=after,
        )[0]

    grads = [local_backward(0, tuple(sents))]
    held_w, received_w = scatter_step(keeps, [arrived], stages[0], devices, "add_wide_0", (grads[0],))
    pieces_g = core_gather(pieces_g, devices, held_w)
    arrivals = [p for p, _ in pieces_g]
    grads.append(local_backward(1, (*held_w, *arrivals)))

    arrays_g = [p for p, _ in pieces_g] if direct else [picked(pieces_g, ints, micro_n)]
    layout_l = dict(layout, slots=[sl for _, sl in pieces_g][: len(arrays_g)])
    per_local = [a for m in range(micro_n) for a in (grads[m], local[m][2], local[m][4])]
    last_in = (ints, x, g_mixed, normed, w_qkv, vectors, remote_bias, small_sums, bias_sums, *per_local, *arrays_g)
    scratch = [((devices, micro_n * BLOCK, 2 * width + 128), BF)] * direct + [
        ((256, 2 * width + 128), BF),
        ((tokens, 3 * width), BF),
    ]
    mib = 19
    if direct:
        in_grad, keep_q, sent_q = call(
            lambda *refs: last_kernel(layout_l, *refs),
            "qkv_grads",
            [((tokens, width), F32)] + [((half, 3 * rows + 8, width), BF)] * 2,
            last_in,
            scalars=1,
            scratch=scratch + [((width, 3 * width), BF)],
            mib=mib,
            us=10.0,
        )
    else:
        in_grad, g_qkv, tails = call(
            lambda *refs: last_kernel(layout_l, *refs),
            "qkv_grads",
            [((tokens, width), F32), ((width, 3 * width), BF), ((devices, 256), F32)],
            last_in,
            scalars=1,
            scratch=scratch,
            mib=mib,
            us=10.0,
        )
        stack = jnp.concatenate(
            [g_qkv[:, c * width : (c + 1) * width].reshape(devices, rows, width) for c in range(3)]
            + [jnp.broadcast_to(jnp.pad(tails, ((0, 0), (0, 256)))[:, None, :], (devices, 8, width)).astype(BF)],
            axis=1,
        )
        keep_q, sent_q = halves(stack)
    for stage, group in enumerate(stages):
        late = [keep_q] if stage == 0 else held_q
        if stage + 1 < len(stages):
            held_w, received_w = scatter_step(held_w, received_w, stages[stage + 1], devices, f"add_wide_{stage + 1}", late)
        if stage == 0:
            held_q, received_q = [keep_q], [[send(follow(sent_q, *held_w), 1, devices)]]
        held_q, received_q = scatter_step(held_q, received_q, group, devices, f"add_qkv_{stage}")
    g_back, g_in, g_out = call(
        lambda *refs: finish_wide_kernel(rows, *refs),
        "finish_wide",
        [((4 * rows, width), F32), ((rows, hidden_n), F32), ((rows, width), F32)],
        (*held_w, *(r for (r,) in received_w)),
        mib=4,
        us=1.0,
    )
    g_query, g_key, g_value, g_gain, g_shift, g_bias_in, g_bias_out = call(
        lambda *refs: finish_qkv_kernel(rows, *refs),
        "finish_qkv",
        [((rows, width), F32)] * 3
        + [((2, rows), F32)] * 2
        + [((1, hidden_n // devices), F32), ((1, rows), F32)],
        (*held_q, *(r for (r,) in received_q)),
        mib=4,
        us=1.0,
    )
    return (
        layer_out.reshape(micro_n, length, width),
        in_grad.reshape(micro_n, length, width),
        g_query,
        g_key,
        g_value,
        g_out,
        g_in,
        g_back,
        g_gain,
        g_shift,
        g_bias_in.reshape(-1),
        g_bias_out.reshape(-1),
    )


def solution(mesh):
    placed = (
        P(None, "fsdp", None),
        P(None, "fsdp", None),
        P(),
        P(),
        P("fsdp", None),
        P("fsdp", None),
        P("fsdp", None),
        P("fsdp", None),
        P("fsdp", None),
        P("fsdp", None),
        P(None, "fsdp"),
        P(None, "fsdp"),
        P("fsdp"),
        P("fsdp"),
    )
    return jax.shard_map(
        on_device,
        mesh=mesh,
        in_specs=placed,
        out_specs=(
            P(None, "fsdp", None),
            P(None, "fsdp", None),
            P("fsdp", None),
            P("fsdp", None),
            P("fsdp", None),
            P("fsdp", None),
            P("fsdp", None),
            P("fsdp", None),
            P(None, "fsdp"),
            P(None, "fsdp"),
            P("fsdp"),
            P("fsdp"),
        ),
        check_vma=False,
    )
```

```python
import math

import jax
import jax.numpy as jnp
import numpy as np
from jax import lax
from jax.experimental import pallas as pl
from jax.experimental.pallas import tpu as pltpu
from jax.sharding import PartitionSpec as P

HEADS = 8
HEAD_DIM = 64
BLOCK = 16
LEVELS = 9
EPSILON = 1e-05
OFF = -1e30
PAIRS = HEADS // 2
WIDE = 2 * HEAD_DIM
SCALE2 = math.log2(math.e) / math.sqrt(HEAD_DIM)
SCALE = 1.0 / math.sqrt(HEAD_DIM)
BF = jnp.bfloat16
F32 = jnp.float32
SIBS = 15
STEP = 512
CHUNK = 1024


def iota(shape, dim):
    return lax.broadcasted_iota(jnp.int32, shape, dim)


def ones_where(condition, value=1.0):
    return jnp.where(condition, value, 0.0).astype(BF)


def coarse_places(index, length):
    shift = jnp.zeros_like(index)
    start = jnp.zeros_like(index)
    row = 0
    for level_id in range(2, LEVELS + 1):
        shift = shift + (index >= row).astype(jnp.int32)
        start = jnp.where(index >= row, row, start)
        row += length >> (level_id - 1)
    return shift, jnp.where(index >= row, length, index - start)


def members(length, first, count, by_rows):
    shape = (count, length) if by_rows else (length, count)
    narrow = (count, 1) if by_rows else (1, count)
    shift, place = coarse_places(iota(narrow, 0 if by_rows else 1) + first, length)
    covers = (iota(shape, 1 if by_rows else 0) >> shift) == place
    return covers, jnp.exp2(-shift.astype(F32))


def mean_rows(length, first, count):
    covers, share = members(length, first, count, True)
    return ones_where(covers, share)


def sum_rows(length, first, count):
    return ones_where(members(length, first, count, True)[0])


def share_columns(length, first, count):
    covers, share = members(length, first, count, False)
    return ones_where(covers, share)


def copy_columns(length, first, count):
    return ones_where(members(length, first, count, False)[0])


def tile_bias(kind, limit=0):
    row = iota((128, 256), 0)
    key = iota((128, 256), 1) & 127
    block_r, block_k = row // BLOCK, key // BLOCK
    sibling = block_r == (block_k ^ 1)
    if kind == 0:
        return jnp.where(block_r // 2 == block_k // 2, 0.0, OFF)
    if kind < 3:
        return jnp.where(sibling, float(kind), OFF)
    last = jnp.where(row < limit, 4.0, OFF)
    return jnp.where(sibling, jnp.where(row < 64, 3.0, last), OFF)


def sibling_rows(mean):
    row = iota((64, 256), 0)
    level, k = row // BLOCK, row % BLOCK
    span = jnp.left_shift(1, level)
    block = span - 1 + (k >> (4 - level))
    inside = k & ((BLOCK >> level) - 1)
    offset = iota((64, 256), 1) - (block * BLOCK + (inside << level))
    chosen = (offset >= 0) & (offset < span)
    return ones_where(chosen, 1.0 / span.astype(F32)) if mean else ones_where(chosen)


def head_columns():
    head = iota((512, 128), 0) // HEAD_DIM
    return ones_where(iota((512, 128), 1) // 2 == 4 * (head // 2) + head % 2)


def minus_columns(pair, keys):
    second = (iota((2 * keys, 128), 0) >= keys).astype(jnp.int32)
    return ones_where(iota((2 * keys, 128), 1) // 2 == 4 * pair + second, -1.0)


def twin_columns():
    return ones_where(iota((128, 128), 0) // 2 == iota((128, 128), 1) // 2)


def mm(a, b):
    return lax.dot_general(a, b, (((1,), (0,)), ((), ())), preferred_element_type=F32)


def mm_nt(a, b):
    return lax.dot_general(a, b, (((1,), (1,)), ((), ())), preferred_element_type=F32)


def mm_tn(a, b):
    return lax.dot_general(a, b, (((0,), (0,)), ((), ())), preferred_element_type=F32)


def split(a):
    high = a.astype(BF)
    return high, (a - high.astype(F32)).astype(BF)


def mm_split(a, b):
    high, low = split(b)
    return mm(a, high) + mm(a, low)


def split_mm(a, b):
    high, low = split(a)
    return mm(high, b) + mm(low, b)


def head_masks():
    lane = lax.broadcasted_iota(jnp.int32, (1, WIDE), 1)
    first = (lane < HEAD_DIM).astype(F32)
    return first, 1.0 - first


def stacked(a, masks):
    return jnp.concatenate([a * masks[0].astype(a.dtype), a * masks[1].astype(a.dtype)], axis=0)


def unstacked(a, masks):
    half = a.shape[0] // 2
    return a[:half] * masks[0] + a[half:] * masks[1]


def head_ones(keys):
    row = lax.broadcasted_iota(jnp.int32, (2 * keys, WIDE), 0)
    lane = lax.broadcasted_iota(jnp.int32, (2 * keys, WIDE), 1)
    return ((row < keys) == (lane < HEAD_DIM)).astype(F32).astype(BF)


def even_columns(high, low):
    col = lax.broadcasted_iota(jnp.int32, high.shape, 1)
    return jnp.where(col % 2 == 0, high.astype(F32), low.astype(F32)).astype(BF)


def normalize(values):
    centre = jnp.mean(values, axis=-1, keepdims=True)
    centred = values - centre
    spread = jnp.mean(centred * centred, axis=-1, keepdims=True)
    inverse = lax.rsqrt(spread + EPSILON)
    return centred * inverse, inverse


def shape_of(shape, dtype):
    return jax.ShapeDtypeStruct(shape, dtype)


def call(body, name, outs, ins, scalars=0, scratch=(), mib=8, us=2.0, after=()):
    vmem = pl.BlockSpec(memory_space=pltpu.VMEM)
    smem = pl.BlockSpec(memory_space=pltpu.SMEM)
    count, late = len(ins), len(after)

    def kernel(*refs):
        body(*refs[:count], *refs[count + late :])

    return pl.pallas_call(
        kernel,
        in_specs=[smem] * scalars + [vmem] * (count - scalars) + [pl.BlockSpec(memory_space=pl.ANY)] * late,
        out_specs=[pl.BlockSpec(memory_space=pltpu.VMEM)] * len(outs),
        out_shape=[shape_of(shape, dtype) for shape, dtype in outs],
        scratch_shapes=[pltpu.VMEM(shape, dtype) for shape, dtype in scratch],
        compiler_params=pltpu.CompilerParams(vmem_limit_bytes=int(mib * 2**20)),
        cost_estimate=pl.CostEstimate(flops=int(us * 1.1e9), transcendentals=0, bytes_accessed=1024),
        name=name,
    )(*ins, *after)


def bit_groups(devices):
    groups = []
    high = devices.bit_length() - 2
    while high >= 1:
        low = max(1, high - 1)
        groups.append(tuple(range(low, high + 1)))
        high = low - 1
    return groups


def offsets_of(group):
    return [sum(1 << b for i, b in enumerate(group) if k >> i & 1) for k in range(1 << len(group))]


def send(value, offset, devices):
    return lax.ppermute(value, "fsdp", [(i, i ^ offset) for i in range(devices)])


def joined(parts):
    return parts[0] if len(parts) == 1 else jnp.concatenate(parts, axis=0)


def follow(values, *earlier):
    return lax.optimization_barrier((values, earlier))[0] if earlier else values


def first_sends(block, devices):
    held = block[None]
    return [held] + [send(held, k, devices) for k in offsets_of(bit_groups(devices)[0])[1:]]


def staged_gather(block, devices, between=(), marks=None, begun=None):
    between = list(between) + [()] * len(bit_groups(devices))
    held = block[None]
    slots = [0]
    groups = bit_groups(devices)
    for group_id, group in enumerate(groups):
        offsets = offsets_of(group)
        parts = begun if begun and group_id == 0 else [held] + [send(held, k, devices) for k in offsets[1:]]
        parts = follow(parts, *between[group_id])
        if group_id < len(groups) - 1:
            held = joined(parts)
            slots = [s ^ k for k in offsets for s in slots]
            if marks is not None:
                marks.append(held)
    return [(p, [s ^ k for s in slots]) for p, k in zip(parts, offsets)]


def core_gather(pieces, devices, after=()):
    held = follow([p for p, _ in pieces], *after)
    return pieces + [(send(p, 1, devices), [s ^ 1 for s in sl]) for p, (_, sl) in zip(held, pieces)]


def crossed_gather(block, cut, devices, marks, earlier):
    groups = bit_groups(devices)
    parts = [block[None]]
    slots = [0]
    for group in groups[:-1]:
        held = joined(parts)
        offsets = offsets_of(group)
        parts = [held] + [send(held, k, devices) for k in offsets[1:]]
        slots = [s ^ k for k in offsets for s in slots]
    parts = follow(parts, *earlier)
    halves = []
    for rows, order in ((slice(0, cut), groups[-1]), (slice(cut, None), groups[-1][::-1])):
        held, own = joined([p[:, rows] for p in parts]), slots
        for bit in order[:-1]:
            held = joined([held, send(held, 1 << bit, devices)])
            own = own + [s ^ (1 << bit) for s in own]
        marks.append(held)
        last = 1 << order[-1]
        halves.append([(held, own), (send(held, last, devices), [s ^ last for s in own])])
    first, second = follow([[p for p, _ in pieces] for pieces in halves], halves[0][1][0], halves[1][1][0])
    return [
        pieces + [(send(p, 1, devices), [s ^ 1 for s in sl]) for p, (_, sl) in zip(held, pieces)]
        for held, pieces in zip((first, second), halves)
    ]


def add_parts(keeps, received, outs_dtype, name, after=()):
    cuts = len(outs_dtype)
    part = keeps[0].shape[0] // cuts
    count = len(keeps)
    sizes = [k.shape[1] for k in keeps]
    ins = [a for arrays in (keeps, *received) for a in arrays]

    def body(*refs):
        outs = refs[len(ins) :]
        for c in range(cuts):
            for i in range(part):
                row = 0
                for j, size in enumerate(sizes):
                    total = refs[j][c * part + i].astype(F32)
                    for r in refs[count + j : len(ins) : count]:
                        total = total + r[c * part + i].astype(F32)
                    outs[c][i, row : row + size] = total.astype(outs[c].dtype)
                    row += size

    shape = (part, sum(sizes)) + keeps[0].shape[2:]
    return call(body, name, [(shape, d) for d in outs_dtype], ins, mib=4, us=1.5, after=after)


def scatter_order(devices):
    order = [0]
    for group in bit_groups(devices)[::-1]:
        order = [s ^ k for s in order for k in offsets_of(group)]
    return order


def scatter_step(held, received, group, devices, name, after=()):
    offsets = offsets_of(group)
    outs = add_parts(held, received, [F32] + [BF] * (len(offsets) - 1), name, after)
    return outs[:1], [[send(o, k, devices)] for o, k in zip(outs[1:], offsets[1:])]


def pack_kernel(rows, wq_ref, wk_ref, wv_ref, wo_ref, wi_ref, wb_ref, gain_ref, shift_ref, bi_ref, bo_ref, first_ref, second_ref):
    for part, ref in enumerate((wq_ref, wk_ref, wv_ref)):
        first_ref[part * rows : (part + 1) * rows, :] = ref[...]
    tail = jnp.zeros((1, 512), F32)
    for ref, at in ((gain_ref, 0), (shift_ref, 2 * rows), (bo_ref, 4 * rows), (bi_ref, 128)):
        for r in range(ref.shape[0]):
            count = ref.shape[1]
            index = lax.broadcasted_iota(jnp.int32, (count, 512), 0)
            lane = lax.broadcasted_iota(jnp.int32, (count, 512), 1)
            place = (lane == index + (at + r * count)).astype(F32).astype(BF)
            tail = tail + mm(ref[r : r + 1, :], place)
    first_ref[3 * rows : 3 * rows + 8, :] = jnp.broadcast_to(tail, (8, 512)).astype(BF)
    second_ref[0 : 4 * rows, :] = wb_ref[...]
    second_ref[4 * rows : 5 * rows, :] = wo_ref[...]
    for c in range(4):
        second_ref[(5 + c) * rows : (6 + c) * rows, :] = wi_ref[:, c * 512 : (c + 1) * 512]


def first_kernel(layout, ints_ref, x_ref, *refs):
    count = len(layout["slots"])
    pieces, refs = refs[:count], refs[count:]
    if not layout["direct"]:
        given, refs = refs[0], refs[1:]
    qkv_ref, w_ref, vec_ref, bias_ref, coarse_ref = refs
    rows, devices = layout["rows"], layout["devices"]
    me = ints_ref[0]
    small = []
    order = []
    if not layout["direct"]:
        w_ref[...] = given[...]
    for ref, slots in zip(pieces, layout["slots"]):
        for i, s in enumerate(slots):
            if layout["direct"]:
                at = pl.multiple_of((me ^ s) * rows, rows)
                for part in range(3):
                    w_ref[pl.ds(at, rows), part * 512 : (part + 1) * 512] = ref[i, part * rows : (part + 1) * rows, :]
            small.append(ref[i, layout["small"] : layout["small"] + 8, :].astype(F32)[:1])
            order.append(s)
    table = jnp.concatenate(small, axis=0)
    vec_ref[...], bias_ref[...] = spread_small(table, order, me, devices)
    for r in range(4):
        part = slice(r * 256, (r + 1) * 256)
        normal, _ = normalize(x_ref[part, :].astype(F32))
        normed = (normal * vec_ref[0:1, :] + vec_ref[2:3, :]).astype(BF)
        qkv = mm(normed, w_ref[...]).astype(BF)
        qkv_ref[part, :] = qkv
        means = jnp.mean(qkv[:, 512:1536].astype(F32).reshape(8, 32, 1024), axis=1)
        coarse_ref[r * 8 : (r + 1) * 8, :] = means.astype(BF)


def slot_numbers(order, shape, dim):
    index = lax.broadcasted_iota(jnp.int32, shape, dim)
    value = jnp.zeros(shape, jnp.int32)
    for bit in range(max(order).bit_length()):
        on = None
        mask = 0
        for k in range((len(order) - 1).bit_length()):
            if order[1 << k] >> bit & 1:
                mask |= 1 << k
        parity = jnp.zeros(shape, jnp.int32)
        for k in range((len(order) - 1).bit_length()):
            if mask >> k & 1:
                parity = parity ^ ((index >> k) & 1)
        value = value | (parity << bit)
    return value


def spread_small(table, order, me, devices):
    w = 512 // devices
    wide = 2048 // devices
    owner = slot_numbers(order, (devices, 512), 0) ^ me
    col = lax.broadcasted_iota(jnp.int32, (devices, 512), 1)
    mine = (col // w == owner).astype(F32)
    lane = lax.broadcasted_iota(jnp.int32, (devices, 128), 1)
    lane_t = lax.broadcasted_iota(jnp.int32, (128, 512), 0)
    col_t = lax.broadcasted_iota(jnp.int32, (128, 512), 1)
    match = (lane_t % w == col_t % w).astype(F32).astype(BF)
    head = table[:, :128]
    rows = []
    for p in range(5):
        own = (head * (lane // w == p).astype(F32)).astype(BF)
        rows.append(jnp.sum(mm(own, match) * mine, axis=0, keepdims=True))
    rows = rows + [jnp.zeros((1, 512), F32)] * 3
    owner_w = slot_numbers(order, (devices, 2048), 0) ^ me
    col_w = lax.broadcasted_iota(jnp.int32, (devices, 2048), 1)
    mine_w = (col_w // wide == owner_w).astype(F32)
    lane_w = lax.broadcasted_iota(jnp.int32, (128, 2048), 0)
    col_tw = lax.broadcasted_iota(jnp.int32, (128, 2048), 1)
    match_w = (lane_w == col_tw % wide).astype(F32).astype(BF)
    bias = jnp.sum(mm(table[:, 128:256].astype(BF), match_w) * mine_w, axis=0, keepdims=True)
    return jnp.concatenate(rows, axis=0), jnp.broadcast_to(bias, (8, 2048))


def local_kernel(
    m, flag_at, ints_ref, qkv_ref, num_ref, den_ref, coarse_ref, w_ref, vbar_ref, vals, num_c, den_c, ones, matrix, biases,
):
    limit = jnp.where(ints_ref[flag_at + m] > 0, 64, 96)
    masks = head_masks()
    ones[...] = head_ones(128)
    length = num_ref.shape[0]
    base = m * length
    whole = slice(base, base + length)
    value = qkv_ref[whole, 1024:1536].astype(F32)
    vbar = jnp.mean(value, axis=0, keepdims=True)
    vbar_ref[...] = jnp.broadcast_to(vbar, (8, 512))
    vals[...] = (value - vbar).astype(BF)
    matrix[...] = mean_rows(length, 0, length)
    for kind in range(4):
        biases[kind] = tile_bias(kind, limit)
    coarse_ref[:, 0:1024] = mm(matrix[...], qkv_ref[whole, 0:1024]).astype(BF)
    coarse_ref[:, 1024:1536] = mm(matrix[...], vals[...]).astype(BF)
    for t in range(8):
        rows = slice((t % 4) * 128, (t % 4) * 128 + 128)
        far = slice(base + (t % 4) * 128, base + (t % 4) * 128 + 128)
        kind = 0 if t < 4 else (1, 1, 2, 3)[t - 4]
        bias = biases[kind]
        for p in range(PAIRS):
            lanes = slice(p * WIDE, (p + 1) * WIDE)
            lanes_k = slice(512 + p * WIDE, 512 + (p + 1) * WIDE)
            if t < 4:
                q, k, v = qkv_ref[far, lanes], qkv_ref[far, lanes_k], vals[rows, lanes]
            else:
                q, k = coarse_ref[rows, lanes], coarse_ref[rows, lanes_k]
                v = coarse_ref[rows, 1024 + p * WIDE : 1024 + (p + 1) * WIDE]
            scores = mm_nt(q, stacked(k, masks))
            weights = jnp.exp2(scores * SCALE2 + bias).astype(BF)
            w_ref[t, :, p * 256 : (p + 1) * 256] = weights
            both = mm(weights, jnp.concatenate([stacked(v, masks), ones[...]], axis=1))
            if t < 4:
                num_ref[rows, lanes] = both[:, :WIDE]
                den_ref[rows, lanes] = both[:, WIDE:]
            else:
                num_c[rows, lanes] = both[:, :WIDE]
                den_c[rows, lanes] = both[:, WIDE:]
    matrix[...] = copy_columns(length, 0, length)
    num_ref[...] += mm_split(matrix[...], num_c[...])
    den_ref[...] += mm_split(matrix[...], den_c[...])


def fill_slots(pieces, slots, target):
    for ref, sl in zip(pieces, slots):
        for i, s in enumerate(sl):
            target[s] = ref[i]


def output_kernel(layout, ints_ref, hid_ref, att_ref, x_ref, vec_ref, *refs):
    weights, (out_ref, mark_ref, w_out, w_back) = refs[:-4], refs[-4:]
    mark_ref[...] = jnp.zeros_like(mark_ref)
    rows = layout["rows"]
    if layout["direct"]:
        for ref, sl in zip(weights, layout["wslots"]):
            for i, s in enumerate(sl):
                d = ints_ref[0] ^ s
                w_back[pl.ds(pl.multiple_of(d * 4 * rows, 4 * rows), 4 * rows), :] = ref[i, 0 : 4 * rows, :]
                w_out[pl.ds(pl.multiple_of(d * rows, rows), rows), :] = ref[i, 4 * rows : 5 * rows, :]
    else:
        w_out[...] = weights[0][...]
        w_back[...] = weights[1][...]
    for r in range(0, hid_ref.shape[0], STEP):
        part = slice(r, r + STEP)
        mixed = x_ref[part, :].astype(F32) + mm(att_ref[part, :], w_out[...])
        out_ref[part, :] = (mixed + mm(hid_ref[part, :], w_back[...]) + vec_ref[4:5, :]).astype(BF)


def take_siblings(layout, ints_ref, m, source, buf):
    for b in range(SIBS):
        if layout["direct"]:
            slot = ints_ref[layout["first_slot"] + m * SIBS + b]
            block = source[slot, m * BLOCK : (m + 1) * BLOCK, :]
        else:
            block = source[m * SIBS + b]
        buf[b * BLOCK : (b + 1) * BLOCK, :] = block


def middle_kernel(layout, ints_ref, x_ref, go_ref, rb_ref, vec_ref, bias_ref, *refs):
    local, refs = (refs[0:4], refs[4:8]), refs[8:]
    count = len(layout["slots"])
    kv_pieces, weights = refs[:count], refs[count : count + layout["n_weights"]]
    (hid_ref, gpre_ref, norm_ref, att_ref, gt_ref, gmix_ref, ghat_ref, ch_ref, cl_ref, pay_ref,
     kvr_ref, wr_ref, small_ref, sbias_ref) = refs[count + layout["n_weights"] : count + layout["n_weights"] + 14]
    scratch = refs[count + layout["n_weights"] + 14 :]
    kvs, (buf, w_out, w_in, w_back, far_num, far_den) = scratch[0], scratch[-6:]
    me = ints_ref[0]
    rows = layout["rows"]
    length = local[0][0].shape[0]
    buf[...] = jnp.zeros_like(buf)
    if layout["direct"]:
        fill_slots(kv_pieces, layout["slots"], kvs)
        for ref, sl in zip(weights, layout["wslots"]):
            for i, s in enumerate(sl):
                d = me ^ s
                at = pl.multiple_of(d * rows, rows)
                if ref.shape[1] == 5 * rows:
                    w_back[pl.ds(pl.multiple_of(d * 4 * rows, 4 * rows), 4 * rows), :] = ref[i, 0 : 4 * rows, :]
                    w_out[pl.ds(at, rows), :] = ref[i, 4 * rows : 5 * rows, :]
                else:
                    for c in range(4):
                        w_in[pl.ds(at, rows), c * 512 : (c + 1) * 512] = ref[i, c * rows : (c + 1) * rows, :]
    else:
        w_out[...] = weights[0][...]
        w_in[...] = weights[1][...]
        w_back[...] = weights[2][...]

    masks = head_masks()
    ones = head_ones(64)
    select = sibling_rows(True)
    spread = copy_columns(length, length - 32, 32)
    sums = sum_rows(length, length - 32, BLOCK)
    columns = head_columns()
    for m in range(2):
        num_ref, den_ref, vbar_ref, coarse_ref = local[m]
        vbar = vbar_ref[0:1, :]
        far_q = coarse_ref[length - 32 : length, 0:512]
        take_siblings(layout, ints_ref, m, kvs if layout["direct"] else kv_pieces[0], buf)
        remote = mm(select, buf[...])
        key_r = remote[:, 0:512].astype(BF)
        val_r = (remote[:, 512:1024].astype(BF).astype(F32) - vbar).astype(BF)
        kvr_ref[m * 64 : (m + 1) * 64, 0:512] = key_r
        kvr_ref[m * 64 : (m + 1) * 64, 512:1024] = val_r
        rb = rb_ref[m]
        nums = []
        dens = []
        for p in range(PAIRS):
            lanes = slice(p * WIDE, (p + 1) * WIDE)
            scores = mm_nt(far_q[:, lanes], stacked(key_r[:, lanes], masks))
            wr = jnp.exp2(scores * SCALE2 + rb).astype(BF)
            wr_ref[m * 32 : (m + 1) * 32, lanes] = wr
            both = mm(wr, jnp.concatenate([stacked(val_r[:, lanes], masks), ones], axis=1))
            nums.append(both[:, :WIDE])
            dens.append(both[:, WIDE:])
        far_num[...] = jnp.concatenate(nums, axis=1)
        far_den[...] = jnp.concatenate(dens, axis=1)
        for r in range(0, length, STEP):
            own = slice(r, r + STEP)
            part = slice(m * length + r, m * length + r + STEP)
            num = num_ref[own, :] + mm_split(spread[own, :], far_num[...])
            den = den_ref[own, :] + mm_split(spread[own, :], far_den[...])
            inverse_den = 1.0 / den
            centred_o = num * inverse_den
            attended = (centred_o + vbar).astype(BF)
            att_ref[part, :] = attended
            mixed = x_ref[part, :].astype(F32) + mm(attended, w_out[...])
            normal, inverse = normalize(mixed)
            normed = (normal * vec_ref[1:2, :] + vec_ref[3:4, :]).astype(BF)
            norm_ref[part, :] = normed
            top_b = go_ref[part, :]
            g_norm = jnp.zeros_like(mixed)
            def products(c):
                lanes = slice(c * CHUNK, (c + 1) * CHUNK)
                return mm(normed, w_in[:, lanes]), mm_nt(top_b, w_back[lanes, :])

            ahead = products(0)
            for c in range(2048 // CHUNK):
                lanes = slice(c * CHUNK, (c + 1) * CHUNK)
                pre, g_hidden = ahead
                if c + 1 < 2048 // CHUNK:
                    ahead = products(c + 1)
                pre = pre + bias_ref[0:1, lanes]
                cdf = 0.5 + 0.5 * lax.erf(pre * math.sqrt(0.5))
                hidden = (pre * cdf).astype(BF)
                hid_ref[part, lanes] = hidden
                slope = cdf + pre * (jnp.exp(-0.5 * pre * pre) * (1.0 / math.sqrt(2.0 * math.pi)))
                g_pre = g_hidden * slope
                total = jnp.broadcast_to(jnp.sum(g_pre, axis=0, keepdims=True), (8, CHUNK))
                sbias_ref[m, :, lanes] = total if r == 0 else sbias_ref[m, :, lanes] + total
                g_pre_b = g_pre.astype(BF)
                gpre_ref[part, lanes] = g_pre_b
                g_norm = g_norm + mm_nt(g_pre_b, w_in[:, lanes])
            top = top_b.astype(F32)
            scaled = g_norm * vec_ref[1:2, :]
            g_mixed = top + (
                scaled
                - jnp.mean(scaled, axis=-1, keepdims=True)
                - normal * jnp.mean(scaled * normal, axis=-1, keepdims=True)
            ) * inverse
            gmix_ref[part, :] = g_mixed
            total = jnp.concatenate(
                [
                    jnp.sum(g_norm * normal, axis=0, keepdims=True),
                    jnp.sum(g_norm, axis=0, keepdims=True),
                    jnp.sum(top, axis=0, keepdims=True),
                    jnp.zeros((5, 512), F32),
                ],
                axis=0,
            )
            small_ref[m] = total if r == 0 else small_ref[m] + total
            gt = g_mixed.astype(BF)
            gt_ref[part, :] = gt
            ghat = (mm_nt(gt, w_out[...]) * inverse_den).astype(BF)
            ghat_ref[part, :] = ghat
            dots = split_mm(ghat.astype(F32) * centred_o, columns)
            dots_h, dots_l = split(dots)
            ch_ref[part, :] = dots_h
            cl_ref[part, :] = dots_l
        part = slice(m * length, (m + 1) * length)
        g_sum = mm(sums, ghat_ref[part, :]).astype(BF)
        c_sum = mm(sums, ch_ref[part, :]) + mm(sums, cl_ref[part, :])
        c_sum = c_sum + split_mm(g_sum.astype(F32) * vbar, columns)
        c_h, c_l = split(c_sum)
        pay = slice(m * BLOCK, (m + 1) * BLOCK)
        pay_ref[pay, 0:512] = far_q[0:BLOCK, :]
        pay_ref[pay, 512:1024] = g_sum
        pay_ref[pay, 1024:1152] = even_columns(c_h, c_l)


def wide_in_kernel(layout, me_ref, gpre_ref, norm_ref, att_ref, gt_ref, *refs):
    rows = layout["rows"]
    up, out = refs[-2:]
    for c in range(4):
        lanes = slice(c * 512, (c + 1) * 512)
        up[:, lanes] = mm_tn(norm_ref[...], gpre_ref[:, lanes]).astype(BF)
    out[...] = mm_tn(att_ref[...], gt_ref[...]).astype(BF)
    if layout["direct"]:
        for half, ref in enumerate(refs[:2]):
            for i, s in enumerate(layout["order"]):
                at = pl.multiple_of((me_ref[0] ^ (s ^ half)) * rows, rows)
                for c in range(4):
                    ref[i, c * rows : (c + 1) * rows, :] = up[pl.ds(at, rows), c * 512 : (c + 1) * 512]
                ref[i, 4 * rows : 5 * rows, :] = out[pl.ds(at, rows), :]


def wide_back_kernel(layout, me_ref, hid_ref, go_ref, *refs):
    rows = 4 * layout["rows"]
    back = refs[-1]
    for c in range(4):
        lanes = slice(c * 512, (c + 1) * 512)
        back[lanes, :] = mm_tn(hid_ref[:, lanes], go_ref[...]).astype(BF)
    if layout["direct"]:
        for half, ref in enumerate(refs[:2]):
            for i, s in enumerate(layout["order"]):
                at = pl.multiple_of((me_ref[0] ^ (s ^ half)) * rows, rows)
                ref[i] = back[pl.ds(at, rows), :]


def back_kernel(m, qkv_ref, coarse_ref, w_ref, ghat_ref, ch_ref, cl_ref, vbar_ref, wr_ref, kvr_ref, grad_ref,
                vals, gsum, ext_f, ext_c, gcoarse, matrix, minus_ref):
    masks = head_masks()
    length = vals.shape[0]
    base = m * length
    whole = slice(base, base + length)
    vals[...] = (qkv_ref[whole, 1024:1536].astype(F32) - vbar_ref[0:1, :]).astype(BF)
    matrix[...] = sum_rows(length, 0, length)
    for p in range(PAIRS):
        minus_ref[p] = minus_columns(p, 128)
    gsum[...] = mm(matrix[...], ghat_ref[whole, :]).astype(BF)
    c_sum = mm(matrix[...], ch_ref[whole, :]) + mm(matrix[...], cl_ref[whole, :])
    c_h, c_l = split(c_sum)
    ext_c[...] = even_columns(c_h, c_l)
    ext_f[...] = even_columns(ch_ref[whole, :], cl_ref[whole, :])
    zero = jnp.zeros((128, WIDE), BF)
    for t in range(8):
        rows = slice((t % 4) * 128, (t % 4) * 128 + 128)
        far = slice(base + (t % 4) * 128, base + (t % 4) * 128 + 128)
        for p in range(PAIRS):
            lanes = slice(p * WIDE, (p + 1) * WIDE)
            lanes_k = slice(512 + p * WIDE, 512 + (p + 1) * WIDE)
            lanes_v = slice(1024 + p * WIDE, 1024 + (p + 1) * WIDE)
            if t < 4:
                q, k, v = qkv_ref[far, lanes], qkv_ref[far, lanes_k], vals[rows, lanes]
                g, ext = ghat_ref[far, lanes], ext_f[rows, :]
            else:
                q, k, v = coarse_ref[rows, lanes], coarse_ref[rows, lanes_k], coarse_ref[rows, lanes_v]
                g, ext = gsum[rows, lanes], ext_c[rows, :]
            weights = w_ref[t, :, p * 256 : (p + 1) * 256]
            left = jnp.concatenate([g, ext], axis=1)
            right = jnp.concatenate([stacked(v, masks), minus_ref[p]], axis=1)
            gs = (weights.astype(F32) * mm_nt(left, right)).astype(BF)
            g_q = mm(gs, stacked(k, masks)) * SCALE
            g_kv = mm_tn(
                jnp.concatenate([gs, weights], axis=0),
                jnp.concatenate([jnp.concatenate([q, zero], axis=1), jnp.concatenate([zero, g], axis=1)], axis=0),
            )
            g_k = unstacked(g_kv[:, :WIDE], masks) * SCALE
            g_v = unstacked(g_kv[:, WIDE:], masks)
            if t < 4:
                grad_ref[rows, lanes] = g_q
                grad_ref[rows, lanes_k] = g_k
                grad_ref[rows, lanes_v] = g_v
            else:
                gcoarse[rows, lanes] = g_q.astype(BF)
                gcoarse[rows, lanes_k] = g_k.astype(BF)
                gcoarse[rows, lanes_v] = g_v.astype(BF)
    far = slice(480, 512)
    for p in range(PAIRS):
        lanes = slice(p * WIDE, (p + 1) * WIDE)
        left = jnp.concatenate([gsum[far, lanes], ext_c[far, :]], axis=1)
        minus = minus_columns(p, 64)
        part = slice(m * 64, (m + 1) * 64)
        right = jnp.concatenate([stacked(kvr_ref[part, 512 + p * WIDE : 512 + (p + 1) * WIDE], masks), minus], axis=1)
        gs = (wr_ref[m * 32 : (m + 1) * 32, lanes].astype(F32) * mm_nt(left, right)).astype(BF)
        gcoarse[far, lanes] = (mm(gs, stacked(kvr_ref[part, lanes], masks)) * SCALE).astype(BF)
    matrix[...] = share_columns(length, 0, length)
    grad_ref[...] += mm(matrix[...], gcoarse[...])


def last_kernel(layout, ints_ref, x_ref, gmix_ref, w_ref, vec_ref, rb_ref, small_ref, sbias_ref, *refs):
    local, refs = (refs[0:3], refs[3:6]), refs[6:]
    count = len(layout["slots"])
    pieces = refs[:count]
    if layout["direct"]:
        ingrad_ref, *blocks, slots_v, buf, gqkv, wgrad = refs[count:]
    else:
        ingrad_ref, wgrad, tail_ref, buf, gqkv = refs[count:]
    me = ints_ref[0]
    rows = layout["rows"]
    devices = layout["devices"]
    masks = head_masks()
    if layout["direct"]:
        fill_slots(pieces, layout["slots"], slots_v)
    buf[...] = jnp.zeros_like(buf)
    length = x_ref.shape[0] // 2
    lane = lax.broadcasted_iota(jnp.int32, (1, 128), 1)
    select, select_sum = sibling_rows(True), sibling_rows(False)
    spread = share_columns(length, length - 32, 32)
    columns, twins = head_columns(), twin_columns()
    for m in range(2):
        grad_ref, coarse_ref, vbar_ref = local[m]
        vbar = vbar_ref[0:1, :]
        take_siblings(layout, ints_ref, m, slots_v if layout["direct"] else pieces[0], buf)
        q_r = mm(select, buf[:, 0:512]).astype(BF)
        g_r = mm(select_sum, buf[:, 512:1024]).astype(BF)
        c_r = mm_split(select_sum, mm(buf[:, 1024:1152], twins))
        c_r = c_r - split_mm(g_r.astype(F32) * vbar, columns)
        c_h, c_l = split(c_r)
        ext = even_columns(c_h, c_l).astype(F32)
        rb = rb_ref[m]
        g_keys = []
        g_vals = []
        for p in range(PAIRS):
            lanes = slice(p * WIDE, (p + 1) * WIDE)
            k = coarse_ref[length - 32 : length, 512 + p * WIDE : 512 + (p + 1) * WIDE]
            v = coarse_ref[length - 32 : length, 1024 + p * WIDE : 1024 + (p + 1) * WIDE]
            qq = stacked(q_r[:, lanes], masks)
            gg = stacked(g_r[:, lanes], masks)
            weights = jnp.exp2(mm_nt(k, qq) * SCALE2 + rb)
            ones_a = ((lane // 2) == 4 * p).astype(F32)
            ones_b = ((lane // 2) == 4 * p + 1).astype(F32)
            ext_p = jnp.concatenate([ext * ones_a, ext * ones_b], axis=0).astype(BF)
            left = jnp.concatenate([v, jnp.full((32, 128), -1.0, BF)], axis=1)
            gs = (weights * mm_nt(left, jnp.concatenate([gg, ext_p], axis=1))).astype(BF)
            g_keys.append(mm(gs, qq) * SCALE)
            g_vals.append(mm(weights.astype(BF), gg))
        extra = mm_split(spread, jnp.concatenate(g_keys + g_vals, axis=1))
        part = slice(m * length, (m + 1) * length)
        gqkv[part, 0:512] = grad_ref[:, 0:512].astype(BF)
        gqkv[part, 512:1536] = (grad_ref[:, 512:1536] + extra).astype(BF)
    g_norm = mm_nt(gqkv[...], w_ref[...])
    normal, inverse = normalize(x_ref[...].astype(F32))
    normed = (normal * vec_ref[0:1, :] + vec_ref[2:3, :]).astype(BF)
    scaled = g_norm * vec_ref[0:1, :]
    ingrad_ref[...] = gmix_ref[...] + (
        scaled
        - jnp.mean(scaled, axis=-1, keepdims=True)
        - normal * jnp.mean(scaled * normal, axis=-1, keepdims=True)
    ) * inverse
    for part in range(3):
        lanes = slice(part * 512, (part + 1) * 512)
        wgrad[:, lanes] = mm_tn(normed, gqkv[:, lanes]).astype(BF)
    vectors = [
        jnp.sum(g_norm * normal, axis=0, keepdims=True),
        small_ref[0, 0:1, :] + small_ref[1, 0:1, :],
        jnp.sum(g_norm, axis=0, keepdims=True),
        small_ref[0, 1:2, :] + small_ref[1, 1:2, :],
        small_ref[0, 2:3, :] + small_ref[1, 2:3, :],
    ]
    bias = sbias_ref[0, 0:1, :] + sbias_ref[1, 0:1, :]
    halves = ((0, 0), (1, 1)) if layout["direct"] else ((None, None),)
    for half, _ in halves:
        order = list(layout["order"]) if half is not None else list(range(devices))
        owner = slot_numbers(order, (len(order), 1), 0)
        if half is not None:
            owner = (owner ^ half) ^ me
        tail = gather_small(vectors, bias, owner, devices)
        if half is None:
            tail_ref[...] = tail
            continue
        first, second = blocks[2 * half : 2 * half + 2]
        for i, s in enumerate(order):
            at = pl.multiple_of((me ^ (s ^ half)) * rows, rows)
            for part in range(2):
                first[i, part * rows : (part + 1) * rows, :] = wgrad[pl.ds(at, rows), part * 512 : (part + 1) * 512]
            second[i, 0:rows, :] = wgrad[pl.ds(at, rows), 1024:1536]
            second[i, rows : rows + 8, 0:256] = jnp.broadcast_to(tail[i : i + 1, :], (8, 256)).astype(BF)
            second[i, rows : rows + 8, 256:512] = jnp.zeros((8, 256), BF)


def gather_small(vectors, bias, owner, devices):
    w = 512 // devices
    wide = 2048 // devices
    count = owner.shape[0]
    col = lax.broadcasted_iota(jnp.int32, (count, 512), 1)
    mine = (col // w == owner).astype(F32)
    col_t = lax.broadcasted_iota(jnp.int32, (512, 128), 0)
    lane_t = lax.broadcasted_iota(jnp.int32, (512, 128), 1)
    total = jnp.zeros((count, 128), F32)
    for p, row in enumerate(vectors):
        place = ((lane_t // w == p) & (lane_t % w == col_t % w)).astype(F32).astype(BF)
        total = total + split_mm(row * mine, place)
    col_w = lax.broadcasted_iota(jnp.int32, (count, 2048), 1)
    mine_w = (col_w // wide == owner).astype(F32)
    col_tw = lax.broadcasted_iota(jnp.int32, (2048, 128), 0)
    lane_tw = lax.broadcasted_iota(jnp.int32, (2048, 128), 1)
    place_w = (lane_tw == col_tw % wide).astype(F32).astype(BF)
    return jnp.concatenate([total, split_mm(bias * mine_w, place_w)], axis=1)


def total_of(refs, rows):
    total = refs[0][0, rows, :].astype(F32)
    for r in refs[1:]:
        total = total + r[0, rows, :].astype(F32)
    return total


def finish_wide_kernel(rows, *refs):
    ins, (back_ref, in_ref, out_ref) = refs[:-3], refs[-3:]
    for c in range(4):
        in_ref[:, c * 512 : (c + 1) * 512] = total_of(ins, slice(c * rows, (c + 1) * rows))
    out_ref[...] = total_of(ins, slice(4 * rows, 5 * rows))
    back_ref[...] = total_of(ins, slice(5 * rows, 9 * rows))


def finish_qkv_kernel(rows, *refs):
    ins, (q_ref, k_ref, v_ref, gain_ref, shift_ref, bi_ref, bo_ref) = refs[:-7], refs[-7:]
    for part, ref in enumerate((q_ref, k_ref, v_ref)):
        ref[...] = total_of(ins, slice(part * rows, (part + 1) * rows))
    tail = total_of(ins, slice(3 * rows, 3 * rows + 8))[0:1]
    for r in range(2):
        gain_ref[r : r + 1, :] = tail[:, r * rows : (r + 1) * rows]
        shift_ref[r : r + 1, :] = tail[:, (2 + r) * rows : (3 + r) * rows]
    bo_ref[...] = tail[:, 4 * rows : 5 * rows]
    bi_ref[...] = tail[:, 128 : 128 + bi_ref.shape[1]]


def remote_plan(lengths, group_order, position, devices, length):
    count = lengths.shape[1]
    lower = np.tril(np.ones((count, count), np.int32))
    seq_ends = jnp.sum(lengths[:, None, :] * lower[None], axis=2)
    device_ids = np.arange(devices, dtype=np.int32)
    group_id = jnp.sum(jnp.where(device_ids == position, group_order, 0), axis=1)[:, None]
    level_s = np.repeat(np.arange(4, dtype=np.int32), [1, 2, 4, 8])
    index_s = np.concatenate([np.arange(1 << level, dtype=np.int32) for level in range(4)])
    siblings = (((group_id >> level_s) ^ 1) << level_s) + index_s
    owner = jnp.sum(jnp.where(group_order[:, None, :] == siblings[:, :, None], device_ids, 0), axis=2)
    level_q = np.full((32,), -1, np.int32)
    start_q = np.zeros((32,), np.int32)
    row = 0
    for level in range(4):
        for i in range(length // (32 << level)):
            level_q[row] = level
            start_q[row] = i * (32 << level)
            row += 1
    level_k = np.tile(np.repeat(np.arange(4, dtype=np.int32), BLOCK), 2)
    start_k = np.tile(np.arange(BLOCK, dtype=np.int32), 8) * (32 << level_k)
    first_k = (((group_id >> level_k) ^ 1) << level_k) * length
    starts = np.concatenate([start_q, np.array([0, length // 2], np.int32)])
    places = jnp.concatenate([first_k + start_k, group_id * length + starts], axis=1)
    seq = jnp.sum((places[:, :, None] >= seq_ends[:, None, :]).astype(jnp.int32), axis=2)
    same = (seq[:, 128:160, None] == seq[:, None, :128]) & (level_q[:, None] == level_k[None, :])
    bias = jnp.where(same, (level_k + 5).astype(np.float32), OFF)
    apart = (seq[:, 160] != seq[:, 161]).astype(jnp.int32)
    ints = jnp.concatenate([jnp.reshape(position, (1,)), (owner ^ position).reshape(-1), apart]).astype(jnp.int32)
    return ints, bias


def exchange_order(stack, position, devices):
    rest = stack.shape[1:]
    for bit in range(devices.bit_length() - 1):
        cut = stack.reshape((devices >> (bit + 1), 2, 1 << bit) + rest)
        stack = jnp.where((position >> bit) & 1 > 0, cut[:, ::-1], cut).reshape((devices,) + rest)
    return stack


def reordered(stack, order):
    return jnp.concatenate([stack[int(i) : int(i) + 1] for i in order], axis=0)


def natural(pieces, position, devices):
    order = [s for _, sl in pieces for s in sl]
    stack = jnp.concatenate([p for p, _ in pieces], axis=0)
    return exchange_order(reordered(stack, np.argsort(np.array(order))), position, devices)


def picked(pieces, ints, micro_n):
    order = [s for _, sl in pieces for s in sl]
    stack = reordered(jnp.concatenate([p for p, _ in pieces], axis=0), np.argsort(np.array(order)))
    blocks = []
    for m in range(micro_n):
        for b in range(SIBS):
            block = lax.dynamic_slice_in_dim(stack, ints[1 + m * SIBS + b], 1, axis=0)
            blocks.append(block[:, m * BLOCK : (m + 1) * BLOCK])
    return jnp.concatenate(blocks, axis=0)


def on_device(
    layer_in,
    out_grad,
    lengths,
    group_order,
    w_query,
    w_key,
    w_value,
    w_out,
    w_in,
    w_back,
    norm_gain,
    norm_shift,
    ffn_bias_in,
    ffn_bias_out,
):
    devices = lax.axis_size("fsdp")
    position = lax.axis_index("fsdp")
    micro_n, length, width = layer_in.shape
    hidden_n = w_in.shape[1]
    tokens = micro_n * length
    rows = w_query.shape[0]
    half = devices // 2
    direct = rows % 16 == 0
    x = layer_in.reshape(tokens, width)
    top = out_grad.reshape(tokens, width)

    small_rows = -(-3 * rows // 8) * 8
    biases = (ffn_bias_in.reshape(1, -1), ffn_bias_out.reshape(1, -1))
    if direct:
        shards = (w_query, w_key, w_value, w_out, w_in, w_back, norm_gain, norm_shift, *biases)
        packed, packed_w = pl.pallas_call(
            lambda *refs: pack_kernel(rows, *refs),
            grid=(1,),
            in_specs=[pl.BlockSpec(a.shape, lambda i: (0, 0)) for a in shards],
            out_specs=[pl.BlockSpec(memory_space=pltpu.VMEM)] * 2,
            out_shape=[shape_of((3 * rows + 8, width), BF), shape_of((9 * rows, width), BF)],
            name="pack",
        )(*shards)
    else:
        tail = jnp.concatenate(
            [
                norm_gain.reshape(-1),
                norm_shift.reshape(-1),
                ffn_bias_out,
                jnp.zeros((128 - 5 * rows,), BF),
                ffn_bias_in,
                jnp.zeros((384 - ffn_bias_in.shape[0],), BF),
            ]
        )
        packed = jnp.concatenate(
            [
                w_query,
                w_key,
                w_value,
                jnp.zeros((small_rows - 3 * rows, width), BF),
                jnp.broadcast_to(tail[None, :], (8, width)),
            ],
            axis=0,
        )
        packed_w = jnp.concatenate(
            [w_back, w_out] + [w_in[:, c * width : (c + 1) * width] for c in range(hidden_n // width)], axis=0
        )
    marks_q, marks_w = [], []
    pieces_q = core_gather(staged_gather(packed, devices, marks=marks_q), devices)
    lengths, group_order = follow((lengths, group_order), marks_q[0])
    pieces_bo, pieces_in = crossed_gather(packed_w, 5 * rows, devices, marks_w, [])
    ints, remote_bias = remote_plan(lengths, group_order, position, devices, length)

    layout = {
        "rows": rows,
        "devices": devices,
        "direct": direct,
        "small": small_rows,
        "slots": [sl for _, sl in pieces_q],
        "first_slot": 1,
        "order": scatter_order(devices),
    }
    flag_at = 1 + micro_n * SIBS
    arrays_q = [p for p, _ in pieces_q]
    if not direct:
        nat = natural(pieces_q, position, devices)
        arrays_q.append(
            jnp.concatenate([nat[:, part * rows : (part + 1) * rows].reshape(width, width) for part in range(3)], axis=1)
        )
    me = jnp.reshape(position, (1,)).astype(jnp.int32)
    qkv, w_qkv, vectors, bias_row, coarse_kv = call(
        lambda *refs: first_kernel(layout, *refs),
        "norm_qkv",
        [
            ((tokens, 3 * width), BF),
            ((width, 3 * width), BF),
            ((8, width), F32),
            ((8, hidden_n), F32),
            ((micro_n * BLOCK, 2 * width), BF),
        ],
        (ints, x, *arrays_q),
        scalars=1,
        mib=8,
        us=5.0,
    )

    local = [
        call(
            lambda *refs, m=m: local_kernel(m, flag_at, *refs),
            f"local_forward_{m}",
            [
                ((length, width), F32),
                ((length, width), F32),
                ((length, 3 * width), BF),
                ((8, 128, 256 * PAIRS), BF),
                ((8, width), F32),
            ],
            (ints, qkv),
            scalars=1,
            scratch=[
                ((length, width), BF),
                ((length, width), F32),
                ((length, width), F32),
                ((256, WIDE), BF),
                ((length, length), BF),
                ((4, 128, 256), F32),
            ],
            mib=8,
            us=4.0,
            after=marks_w if m == 0 else (),
        )
        for m in range(micro_n)
    ]

    pieces_kv = staged_gather(coarse_kv, devices, [(local[0][4], *marks_w), (local[1][4],)])
    pieces_kv = core_gather(pieces_kv, devices)
    arrays_kv = [p for p, _ in pieces_kv] if direct else [picked(pieces_kv, ints, micro_n)]
    if direct:
        weights_in = [p for p, _ in pieces_bo + pieces_in]
    else:
        nat_bo, nat_in = natural(pieces_bo, position, devices), natural(pieces_in, position, devices)
        weights_in = [
            nat_bo[:, 4 * rows :].reshape(width, width),
            jnp.concatenate([nat_in[:, c * rows : (c + 1) * rows].reshape(width, width) for c in range(4)], axis=1),
            nat_bo[:, : 4 * rows].reshape(hidden_n, width),
        ]
    layout_m = dict(
        layout,
        slots=[sl for _, sl in pieces_kv][: len(arrays_kv)],
        wslots=[sl for _, sl in pieces_bo + pieces_in],
        n_weights=len(weights_in),
    )
    per_local = [a for num, den, coarse, _, vbar in local for a in (num, den, vbar, coarse)]
    (hidden, g_pre, normed_two, attended, gt, g_mixed, ghat, dots_h, dots_l, payload, far_kv, far_w,
     small_sums, bias_sums) = call(
        lambda *refs: middle_kernel(layout_m, *refs),
        "middle",
        [
            ((tokens, hidden_n), BF),
            ((tokens, hidden_n), BF),
            ((tokens, width), BF),
            ((tokens, width), BF),
            ((tokens, width), BF),
            ((tokens, width), F32),
            ((tokens, width), BF),
            ((tokens, 128), BF),
            ((tokens, 128), BF),
            ((micro_n * BLOCK, 2 * width + 128), BF),
            ((micro_n * 64, 2 * width), BF),
            ((micro_n * 32, width), BF),
            ((micro_n, 8, width), F32),
            ((micro_n, 8, hidden_n), F32),
        ],
        (ints, x, top, remote_bias, vectors, bias_row, *per_local, *arrays_kv, *weights_in),
        scalars=1,
        scratch=[((devices, micro_n * BLOCK, 2 * width), BF)] * direct
        + [
            ((256, 2 * width), BF),
            ((width, width), BF),
            ((width, hidden_n), BF),
            ((hidden_n, width), BF),
            ((32, width), F32),
            ((32, width), F32),
        ],
        mib=20,
        us=20.0,
    )

    order = np.array(layout["order"], np.int32)
    stages = bit_groups(devices)[::-1]

    def halves(stack):
        stack = exchange_order(stack, position, devices)
        return reordered(stack, order), reordered(stack, order ^ 1)

    def wide_grads(body, name, ins, plain, count, after):
        blocks = [((half, count, width), BF)] * 2
        return call(
            lambda *refs: body(layout, *refs),
            name,
            blocks if direct else plain,
            ins,
            scalars=1,
            scratch=plain if direct else (),
            mib=8,
            us=3.0,
            after=after,
        )

    begun = first_sends(payload, devices)
    grads_a = wide_grads(
        wide_in_kernel,
        "wide_in",
        (me, g_pre, normed_two, attended, gt),
        [((width, hidden_n), BF), ((width, width), BF)],
        5 * rows,
        (begun[1],),
    )
    grads_b = wide_grads(
        wide_back_kernel, "wide_back", (me, hidden, top), [((hidden_n, width), BF)], 4 * rows, (begun[1],)
    )
    pieces_g = staged_gather(payload, devices, [(grads_a[0], grads_b[0])], begun=begun)
    if direct:
        keeps, sents = (grads_a[0], grads_b[0]), (grads_a[1], grads_b[1])
    else:
        g_in, g_out = grads_a
        stack = [g_in[:, c * width : (c + 1) * width].reshape(devices, rows, width) for c in range(4)]
        stack = jnp.concatenate(stack + [g_out.reshape(devices, rows, width)], axis=1)
        keeps, sents = zip(halves(stack), halves(grads_b[0].reshape(devices, 4 * rows, width)))
    arrived = [send(a, 1, devices) for a in sents]

    def local_backward(m, after):
        return call(
            lambda *refs: back_kernel(m, *refs),
            f"local_backward_{m}",
            [((length, 3 * width), F32)],
            (qkv, local[m][2], local[m][3], ghat, dots_h, dots_l, local[m][4], far_w, far_kv),
            scratch=[
                ((length, width), BF),
                ((length, width), BF),
                ((length, 128), BF),
                ((length, 128), BF),
                ((length, 3 * width), BF),
                ((length, length), BF),
                ((PAIRS, 256, 128), BF),
            ],
            mib=8,
            us=8.0,
            after=after,
        )[0]

    grads = [local_backward(0, tuple(sents))]
    held_w, received_w = scatter_step(keeps, [arrived], stages[0], devices, "add_wide_0", (grads[0],))
    pieces_g = core_gather(pieces_g, devices, held_w)
    arrivals = [p for p, _ in pieces_g]
    grads.append(local_backward(1, (*held_w, *arrivals)))

    arrays_g = [p for p, _ in pieces_g] if direct else [picked(pieces_g, ints, micro_n)]
    layout_l = dict(layout, slots=[sl for _, sl in pieces_g][: len(arrays_g)])
    per_local = [a for m in range(micro_n) for a in (grads[m], local[m][2], local[m][4])]
    last_in = (ints, x, g_mixed, w_qkv, vectors, remote_bias, small_sums, bias_sums, *per_local, *arrays_g)
    scratch = [((devices, micro_n * BLOCK, 2 * width + 128), BF)] * direct + [
        ((256, 2 * width + 128), BF),
        ((tokens, 3 * width), BF),
    ]
    mib = 17
    if direct:
        in_grad, *blocks = call(
            lambda *refs: last_kernel(layout_l, *refs),
            "qkv_grads",
            [((tokens, width), F32)] + [((half, 2 * rows, width), BF), ((half, rows + 8, width), BF)] * 2,
            last_in,
            scalars=1,
            scratch=scratch + [((width, 3 * width), BF)],
            mib=mib,
            us=10.0,
        )
    else:
        in_grad, g_qkv, tails = call(
            lambda *refs: last_kernel(layout_l, *refs),
            "qkv_grads",
            [((tokens, width), F32), ((width, 3 * width), BF), ((devices, 256), F32)],
            last_in,
            scalars=1,
            scratch=scratch,
            mib=mib,
            us=10.0,
        )
        stack = jnp.concatenate(
            [g_qkv[:, c * width : (c + 1) * width].reshape(devices, rows, width) for c in range(3)]
            + [jnp.broadcast_to(jnp.pad(tails, ((0, 0), (0, 256)))[:, None, :], (devices, 8, width)).astype(BF)],
            axis=1,
        )
        blocks = [a[:, cut] for a in halves(stack) for cut in (slice(0, 2 * rows), slice(2 * rows, None))]
    keep_q, sent_q = blocks[:2], blocks[2:]
    given = [p for p, _ in pieces_bo] if direct else [weights_in[0], weights_in[2]]
    layer_out, mark = call(
        lambda *refs: output_kernel(layout_m, *refs),
        "layer_out",
        [((tokens, width), BF), ((8, 128), F32)],
        (me, hidden, attended, x, vectors, *given),
        scalars=1,
        scratch=[((width, width), BF), ((hidden_n, width), BF)],
        mib=8,
        us=3.0,
        after=(keep_q[0],),
    )
    received_q = [[send(a, 1, devices) for a in sent_q]]
    held_q = keep_q
    for stage, group in enumerate(stages):
        if stage + 1 < len(stages):
            late = (mark,) if stage == 0 else held_q
            held_w, received_w = scatter_step(held_w, received_w, stages[stage + 1], devices, f"add_wide_{stage + 1}", late)
        held_q, received_q = scatter_step(held_q, received_q, group, devices, f"add_qkv_{stage}", held_w if stage == 0 else ())
    g_back, g_in, g_out = call(
        lambda *refs: finish_wide_kernel(rows, *refs),
        "finish_wide",
        [((4 * rows, width), F32), ((rows, hidden_n), F32), ((rows, width), F32)],
        (*held_w, *(r for (r,) in received_w)),
        mib=4,
        us=1.0,
    )
    g_query, g_key, g_value, g_gain, g_shift, g_bias_in, g_bias_out = call(
        lambda *refs: finish_qkv_kernel(rows, *refs),
        "finish_qkv",
        [((rows, width), F32)] * 3
        + [((2, rows), F32)] * 2
        + [((1, hidden_n // devices), F32), ((1, rows), F32)],
        (*held_q, *(r for (r,) in received_q)),
        mib=4,
        us=1.0,
    )
    return (
        layer_out.reshape(micro_n, length, width),
        in_grad.reshape(micro_n, length, width),
        g_query,
        g_key,
        g_value,
        g_out,
        g_in,
        g_back,
        g_gain,
        g_shift,
        g_bias_in.reshape(-1),
        g_bias_out.reshape(-1),
    )


def solution(mesh):
    placed = (
        P(None, "fsdp", None),
        P(None, "fsdp", None),
        P(),
        P(),
        P("fsdp", None),
        P("fsdp", None),
        P("fsdp", None),
        P("fsdp", None),
        P("fsdp", None),
        P("fsdp", None),
        P(None, "fsdp"),
        P(None, "fsdp"),
        P("fsdp"),
        P("fsdp"),
    )
    return jax.shard_map(
        on_device,
        mesh=mesh,
        in_specs=placed,
        out_specs=(
            P(None, "fsdp", None),
            P(None, "fsdp", None),
            P("fsdp", None),
            P("fsdp", None),
            P("fsdp", None),
            P("fsdp", None),
            P("fsdp", None),
            P("fsdp", None),
            P(None, "fsdp"),
            P(None, "fsdp"),
            P("fsdp"),
            P("fsdp"),
        ),
        check_vma=False,
    )
```

```python
import math

import jax
import jax.numpy as jnp
import numpy as np
from jax import lax
from jax.experimental import pallas as pl
from jax.experimental.pallas import tpu as pltpu
from jax.sharding import PartitionSpec as P

HEADS = 8
HEAD_DIM = 64
BLOCK = 16
LEVELS = 9
EPSILON = 1e-05
OFF = -1e30
PAIRS = HEADS // 2
WIDE = 2 * HEAD_DIM
SCALE2 = math.log2(math.e) / math.sqrt(HEAD_DIM)
SCALE = 1.0 / math.sqrt(HEAD_DIM)
BF = jnp.bfloat16
F32 = jnp.float32
SIBS = 15
STEP = 512
CHUNK = 1024


def iota(shape, dim):
    return lax.broadcasted_iota(jnp.int32, shape, dim)


def ones_where(condition, value=1.0):
    return jnp.where(condition, value, 0.0).astype(BF)


def coarse_places(index, length):
    shift = jnp.zeros_like(index)
    start = jnp.zeros_like(index)
    row = 0
    for level_id in range(2, LEVELS + 1):
        shift = shift + (index >= row).astype(jnp.int32)
        start = jnp.where(index >= row, row, start)
        row += length >> (level_id - 1)
    return shift, jnp.where(index >= row, length, index - start)


def members(length, first, count, by_rows):
    shape = (count, length) if by_rows else (length, count)
    narrow = (count, 1) if by_rows else (1, count)
    shift, place = coarse_places(iota(narrow, 0 if by_rows else 1) + first, length)
    covers = (iota(shape, 1 if by_rows else 0) >> shift) == place
    return covers, jnp.exp2(-shift.astype(F32))


def mean_rows(length, first, count):
    covers, share = members(length, first, count, True)
    return ones_where(covers, share)


def sum_rows(length, first, count):
    return ones_where(members(length, first, count, True)[0])


def share_columns(length, first, count):
    covers, share = members(length, first, count, False)
    return ones_where(covers, share)


def copy_columns(length, first, count):
    return ones_where(members(length, first, count, False)[0])


def tile_bias(kind, limit=0):
    row = iota((128, 256), 0)
    key = iota((128, 256), 1) & 127
    block_r, block_k = row // BLOCK, key // BLOCK
    sibling = block_r == (block_k ^ 1)
    if kind == 0:
        return jnp.where(block_r // 2 == block_k // 2, 0.0, OFF)
    if kind < 3:
        return jnp.where(sibling, float(kind), OFF)
    last = jnp.where(row < limit, 4.0, OFF)
    return jnp.where(sibling, jnp.where(row < 64, 3.0, last), OFF)


def sibling_rows(mean):
    row = iota((64, 256), 0)
    level, k = row // BLOCK, row % BLOCK
    span = jnp.left_shift(1, level)
    block = span - 1 + (k >> (4 - level))
    inside = k & ((BLOCK >> level) - 1)
    offset = iota((64, 256), 1) - (block * BLOCK + (inside << level))
    chosen = (offset >= 0) & (offset < span)
    return ones_where(chosen, 1.0 / span.astype(F32)) if mean else ones_where(chosen)


def head_columns():
    head = iota((512, 128), 0) // HEAD_DIM
    return ones_where(iota((512, 128), 1) // 2 == 4 * (head // 2) + head % 2)


def minus_columns(pair, keys):
    second = (iota((2 * keys, 128), 0) >= keys).astype(jnp.int32)
    return ones_where(iota((2 * keys, 128), 1) // 2 == 4 * pair + second, -1.0)


def twin_columns():
    return ones_where(iota((128, 128), 0) // 2 == iota((128, 128), 1) // 2)


def mm(a, b):
    return lax.dot_general(a, b, (((1,), (0,)), ((), ())), preferred_element_type=F32)


def mm_nt(a, b):
    return lax.dot_general(a, b, (((1,), (1,)), ((), ())), preferred_element_type=F32)


def mm_tn(a, b):
    return lax.dot_general(a, b, (((0,), (0,)), ((), ())), preferred_element_type=F32)


def split(a):
    high = a.astype(BF)
    return high, (a - high.astype(F32)).astype(BF)


def mm_split(a, b):
    high, low = split(b)
    return mm(a, high) + mm(a, low)


def split_mm(a, b):
    high, low = split(a)
    return mm(high, b) + mm(low, b)


def head_masks():
    lane = lax.broadcasted_iota(jnp.int32, (1, WIDE), 1)
    first = (lane < HEAD_DIM).astype(F32)
    return first, 1.0 - first


def stacked(a, masks):
    return jnp.concatenate([a * masks[0].astype(a.dtype), a * masks[1].astype(a.dtype)], axis=0)


def unstacked(a, masks):
    half = a.shape[0] // 2
    return a[:half] * masks[0] + a[half:] * masks[1]


def head_ones(keys):
    row = lax.broadcasted_iota(jnp.int32, (2 * keys, WIDE), 0)
    lane = lax.broadcasted_iota(jnp.int32, (2 * keys, WIDE), 1)
    return ((row < keys) == (lane < HEAD_DIM)).astype(F32).astype(BF)


def even_columns(high, low):
    col = lax.broadcasted_iota(jnp.int32, high.shape, 1)
    return jnp.where(col % 2 == 0, high.astype(F32), low.astype(F32)).astype(BF)


def normalize(values):
    centre = jnp.mean(values, axis=-1, keepdims=True)
    centred = values - centre
    spread = jnp.mean(centred * centred, axis=-1, keepdims=True)
    inverse = lax.rsqrt(spread + EPSILON)
    return centred * inverse, inverse


def shape_of(shape, dtype):
    return jax.ShapeDtypeStruct(shape, dtype)


def call(body, name, outs, ins, scalars=0, scratch=(), mib=8, us=2.0, after=()):
    vmem = pl.BlockSpec(memory_space=pltpu.VMEM)
    smem = pl.BlockSpec(memory_space=pltpu.SMEM)
    count, late = len(ins), len(after)

    def kernel(*refs):
        body(*refs[:count], *refs[count + late :])

    return pl.pallas_call(
        kernel,
        in_specs=[smem] * scalars + [vmem] * (count - scalars) + [pl.BlockSpec(memory_space=pl.ANY)] * late,
        out_specs=[pl.BlockSpec(memory_space=pltpu.VMEM)] * len(outs),
        out_shape=[shape_of(shape, dtype) for shape, dtype in outs],
        scratch_shapes=[pltpu.VMEM(shape, dtype) for shape, dtype in scratch],
        compiler_params=pltpu.CompilerParams(vmem_limit_bytes=int(mib * 2**20)),
        cost_estimate=pl.CostEstimate(flops=int(us * 1.8e9), transcendentals=0, bytes_accessed=1024),
        name=name,
    )(*ins, *after)


def bit_groups(devices):
    groups = []
    high = devices.bit_length() - 2
    while high >= 1:
        low = max(1, high - 1)
        groups.append(tuple(range(low, high + 1)))
        high = low - 1
    return groups


def offsets_of(group):
    return [sum(1 << b for i, b in enumerate(group) if k >> i & 1) for k in range(1 << len(group))]


def send(value, offset, devices):
    return lax.ppermute(value, "fsdp", [(i, i ^ offset) for i in range(devices)])


def joined(parts):
    return parts[0] if len(parts) == 1 else jnp.concatenate(parts, axis=0)


def follow(values, *earlier):
    return lax.optimization_barrier((values, earlier))[0] if earlier else values


def first_sends(block, devices):
    held = block[None]
    return [held] + [send(held, k, devices) for k in offsets_of(bit_groups(devices)[0])[1:]]


def staged_gather(block, devices, between=(), marks=None, begun=None):
    between = list(between) + [()] * len(bit_groups(devices))
    held = block[None]
    slots = [0]
    groups = bit_groups(devices)
    for group_id, group in enumerate(groups):
        offsets = offsets_of(group)
        parts = begun if begun and group_id == 0 else [held] + [send(held, k, devices) for k in offsets[1:]]
        parts = follow(parts, *between[group_id])
        if group_id < len(groups) - 1:
            held = joined(parts)
            slots = [s ^ k for k in offsets for s in slots]
            if marks is not None:
                marks.append(held)
    return [(p, [s ^ k for s in slots]) for p, k in zip(parts, offsets)]


def core_gather(pieces, devices, after=()):
    held = follow([p for p, _ in pieces], *after)
    return pieces + [(send(p, 1, devices), [s ^ 1 for s in sl]) for p, (_, sl) in zip(held, pieces)]


def crossed_gather(block, cut, devices, marks, earlier):
    groups = bit_groups(devices)
    parts = [block[None]]
    slots = [0]
    for group in groups[:-1]:
        held = joined(parts)
        offsets = offsets_of(group)
        parts = [held] + [send(held, k, devices) for k in offsets[1:]]
        slots = [s ^ k for k in offsets for s in slots]
    parts = follow(parts, *earlier)
    halves = []
    for rows, order in ((slice(0, cut), groups[-1]), (slice(cut, None), groups[-1][::-1])):
        held, own = joined([p[:, rows] for p in parts]), slots
        for bit in order[:-1]:
            held = joined([held, send(held, 1 << bit, devices)])
            own = own + [s ^ (1 << bit) for s in own]
        marks.append(held)
        last = 1 << order[-1]
        halves.append([(held, own), (send(held, last, devices), [s ^ last for s in own])])
    first, second = follow([[p for p, _ in pieces] for pieces in halves], halves[0][1][0], halves[1][1][0])
    return [
        pieces + [(send(p, 1, devices), [s ^ 1 for s in sl]) for p, (_, sl) in zip(held, pieces)]
        for held, pieces in zip((first, second), halves)
    ]


def add_parts(keeps, received, outs_dtype, name, after=()):
    cuts = len(outs_dtype)
    part = keeps[0].shape[0] // cuts
    count = len(keeps)
    sizes = [k.shape[1] for k in keeps]
    ins = [a for arrays in (keeps, *received) for a in arrays]

    def body(*refs):
        outs = refs[len(ins) :]
        for c in range(cuts):
            for i in range(part):
                row = 0
                for j, size in enumerate(sizes):
                    total = refs[j][c * part + i].astype(F32)
                    for r in refs[count + j : len(ins) : count]:
                        total = total + r[c * part + i].astype(F32)
                    outs[c][i, row : row + size] = total.astype(outs[c].dtype)
                    row += size

    shape = (part, sum(sizes)) + keeps[0].shape[2:]
    return call(body, name, [(shape, d) for d in outs_dtype], ins, mib=4, us=1.5, after=after)


def scatter_order(devices):
    order = [0]
    for group in bit_groups(devices)[::-1]:
        order = [s ^ k for s in order for k in offsets_of(group)]
    return order


def scatter_step(held, received, group, devices, name, after=()):
    offsets = offsets_of(group)
    outs = add_parts(held, received, [F32] + [BF] * (len(offsets) - 1), name, after)
    return outs[:1], [[send(o, k, devices)] for o, k in zip(outs[1:], offsets[1:])]


def pack_kernel(rows, wq_ref, wk_ref, wv_ref, wo_ref, wi_ref, wb_ref, gain_ref, shift_ref, bi_ref, bo_ref, first_ref, second_ref):
    for part, ref in enumerate((wq_ref, wk_ref, wv_ref)):
        first_ref[part * rows : (part + 1) * rows, :] = ref[...]
    tail = jnp.zeros((1, 512), F32)
    for ref, at in ((gain_ref, 0), (shift_ref, 2 * rows), (bo_ref, 4 * rows), (bi_ref, 128)):
        for r in range(ref.shape[0]):
            count = ref.shape[1]
            index = lax.broadcasted_iota(jnp.int32, (count, 512), 0)
            lane = lax.broadcasted_iota(jnp.int32, (count, 512), 1)
            place = (lane == index + (at + r * count)).astype(F32).astype(BF)
            tail = tail + mm(ref[r : r + 1, :], place)
    first_ref[3 * rows : 3 * rows + 8, :] = jnp.broadcast_to(tail, (8, 512)).astype(BF)
    second_ref[0 : 4 * rows, :] = wb_ref[...]
    second_ref[4 * rows : 5 * rows, :] = wo_ref[...]
    for c in range(4):
        second_ref[(5 + c) * rows : (6 + c) * rows, :] = wi_ref[:, c * 512 : (c + 1) * 512]


def first_kernel(layout, ints_ref, x_ref, *refs):
    count = len(layout["slots"])
    pieces, refs = refs[:count], refs[count:]
    if not layout["direct"]:
        given, refs = refs[0], refs[1:]
    qkv_ref, w_ref, vec_ref, bias_ref, coarse_ref = refs
    rows, devices = layout["rows"], layout["devices"]
    me = ints_ref[0]
    small = []
    order = []
    if not layout["direct"]:
        w_ref[...] = given[...]
    for ref, slots in zip(pieces, layout["slots"]):
        for i, s in enumerate(slots):
            if layout["direct"]:
                at = pl.multiple_of((me ^ s) * rows, rows)
                for part in range(3):
                    w_ref[pl.ds(at, rows), part * 512 : (part + 1) * 512] = ref[i, part * rows : (part + 1) * rows, :]
            small.append(ref[i, layout["small"] : layout["small"] + 8, :].astype(F32)[:1])
            order.append(s)
    table = jnp.concatenate(small, axis=0)
    vec_ref[...], bias_ref[...] = spread_small(table, order, me, devices)
    for r in range(4):
        part = slice(r * 256, (r + 1) * 256)
        normal, _ = normalize(x_ref[part, :].astype(F32))
        normed = (normal * vec_ref[0:1, :] + vec_ref[2:3, :]).astype(BF)
        qkv = mm(normed, w_ref[...]).astype(BF)
        qkv_ref[part, :] = qkv
        means = jnp.mean(qkv[:, 512:1536].astype(F32).reshape(8, 32, 1024), axis=1)
        coarse_ref[r * 8 : (r + 1) * 8, :] = means.astype(BF)


def slot_numbers(order, shape, dim):
    index = lax.broadcasted_iota(jnp.int32, shape, dim)
    value = jnp.zeros(shape, jnp.int32)
    for bit in range(max(order).bit_length()):
        on = None
        mask = 0
        for k in range((len(order) - 1).bit_length()):
            if order[1 << k] >> bit & 1:
                mask |= 1 << k
        parity = jnp.zeros(shape, jnp.int32)
        for k in range((len(order) - 1).bit_length()):
            if mask >> k & 1:
                parity = parity ^ ((index >> k) & 1)
        value = value | (parity << bit)
    return value


def spread_small(table, order, me, devices):
    w = 512 // devices
    wide = 2048 // devices
    owner = slot_numbers(order, (devices, 512), 0) ^ me
    col = lax.broadcasted_iota(jnp.int32, (devices, 512), 1)
    mine = (col // w == owner).astype(F32)
    lane = lax.broadcasted_iota(jnp.int32, (devices, 128), 1)
    lane_t = lax.broadcasted_iota(jnp.int32, (128, 512), 0)
    col_t = lax.broadcasted_iota(jnp.int32, (128, 512), 1)
    match = (lane_t % w == col_t % w).astype(F32).astype(BF)
    head = table[:, :128]
    rows = []
    for p in range(5):
        own = (head * (lane // w == p).astype(F32)).astype(BF)
        rows.append(jnp.sum(mm(own, match) * mine, axis=0, keepdims=True))
    rows = rows + [jnp.zeros((1, 512), F32)] * 3
    owner_w = slot_numbers(order, (devices, 2048), 0) ^ me
    col_w = lax.broadcasted_iota(jnp.int32, (devices, 2048), 1)
    mine_w = (col_w // wide == owner_w).astype(F32)
    lane_w = lax.broadcasted_iota(jnp.int32, (128, 2048), 0)
    col_tw = lax.broadcasted_iota(jnp.int32, (128, 2048), 1)
    match_w = (lane_w == col_tw % wide).astype(F32).astype(BF)
    bias = jnp.sum(mm(table[:, 128:256].astype(BF), match_w) * mine_w, axis=0, keepdims=True)
    return jnp.concatenate(rows, axis=0), jnp.broadcast_to(bias, (8, 2048))


def local_kernel(
    m, flag_at, ints_ref, qkv_ref, num_ref, den_ref, coarse_ref, w_ref, vbar_ref, vals, num_c, den_c, ones, matrix, biases,
):
    limit = jnp.where(ints_ref[flag_at + m] > 0, 64, 96)
    masks = head_masks()
    ones[...] = head_ones(128)
    length = num_ref.shape[0]
    base = m * length
    whole = slice(base, base + length)
    value = qkv_ref[whole, 1024:1536].astype(F32)
    vbar = jnp.mean(value, axis=0, keepdims=True)
    vbar_ref[...] = jnp.broadcast_to(vbar, (8, 512))
    vals[...] = (value - vbar).astype(BF)
    matrix[...] = mean_rows(length, 0, length)
    for kind in range(4):
        biases[kind] = tile_bias(kind, limit)
    coarse_ref[:, 0:1024] = mm(matrix[...], qkv_ref[whole, 0:1024]).astype(BF)
    coarse_ref[:, 1024:1536] = mm(matrix[...], vals[...]).astype(BF)
    for t in range(8):
        rows = slice((t % 4) * 128, (t % 4) * 128 + 128)
        far = slice(base + (t % 4) * 128, base + (t % 4) * 128 + 128)
        kind = 0 if t < 4 else (1, 1, 2, 3)[t - 4]
        bias = biases[kind]
        for p in range(PAIRS):
            lanes = slice(p * WIDE, (p + 1) * WIDE)
            lanes_k = slice(512 + p * WIDE, 512 + (p + 1) * WIDE)
            if t < 4:
                q, k, v = qkv_ref[far, lanes], qkv_ref[far, lanes_k], vals[rows, lanes]
            else:
                q, k = coarse_ref[rows, lanes], coarse_ref[rows, lanes_k]
                v = coarse_ref[rows, 1024 + p * WIDE : 1024 + (p + 1) * WIDE]
            scores = mm_nt(q, stacked(k, masks))
            weights = jnp.exp2(scores * SCALE2 + bias).astype(BF)
            w_ref[t, :, p * 256 : (p + 1) * 256] = weights
            both = mm(weights, jnp.concatenate([stacked(v, masks), ones[...]], axis=1))
            if t < 4:
                num_ref[rows, lanes] = both[:, :WIDE]
                den_ref[rows, lanes] = both[:, WIDE:]
            else:
                num_c[rows, lanes] = both[:, :WIDE]
                den_c[rows, lanes] = both[:, WIDE:]
    matrix[...] = copy_columns(length, 0, length)
    num_ref[...] += mm_split(matrix[...], num_c[...])
    den_ref[...] += mm_split(matrix[...], den_c[...])


def fill_slots(pieces, slots, target):
    for ref, sl in zip(pieces, slots):
        for i, s in enumerate(sl):
            target[s] = ref[i]


def output_kernel(layout, ints_ref, hid_ref, att_ref, x_ref, vec_ref, *refs):
    weights, (out_ref, mark_ref, w_out, w_back) = refs[:-4], refs[-4:]
    mark_ref[...] = jnp.zeros_like(mark_ref)
    rows = layout["rows"]
    if layout["direct"]:
        for ref, sl in zip(weights, layout["wslots"]):
            for i, s in enumerate(sl):
                d = ints_ref[0] ^ s
                w_back[pl.ds(pl.multiple_of(d * 4 * rows, 4 * rows), 4 * rows), :] = ref[i, 0 : 4 * rows, :]
                w_out[pl.ds(pl.multiple_of(d * rows, rows), rows), :] = ref[i, 4 * rows : 5 * rows, :]
    else:
        w_out[...] = weights[0][...]
        w_back[...] = weights[1][...]
    for r in range(0, hid_ref.shape[0], STEP):
        part = slice(r, r + STEP)
        mixed = x_ref[part, :].astype(F32) + mm(att_ref[part, :], w_out[...])
        out_ref[part, :] = (mixed + mm(hid_ref[part, :], w_back[...]) + vec_ref[4:5, :]).astype(BF)


def take_siblings(layout, ints_ref, m, source, buf):
    for b in range(SIBS):
        if layout["direct"]:
            slot = ints_ref[layout["first_slot"] + m * SIBS + b]
            block = source[slot, m * BLOCK : (m + 1) * BLOCK, :]
        else:
            block = source[m * SIBS + b]
        buf[b * BLOCK : (b + 1) * BLOCK, :] = block


def middle_kernel(layout, ints_ref, x_ref, go_ref, rb_ref, vec_ref, bias_ref, *refs):
    local, refs = (refs[0:4], refs[4:8]), refs[8:]
    count = len(layout["slots"])
    kv_pieces, weights = refs[:count], refs[count : count + layout["n_weights"]]
    (hid_ref, gpre_ref, norm_ref, att_ref, gt_ref, gmix_ref, ghat_ref, ch_ref, cl_ref, pay_ref,
     kvr_ref, wr_ref, small_ref, sbias_ref) = refs[count + layout["n_weights"] : count + layout["n_weights"] + 14]
    scratch = refs[count + layout["n_weights"] + 14 :]
    kvs, (buf, w_out, w_in, w_back, far_num, far_den) = scratch[0], scratch[-6:]
    me = ints_ref[0]
    rows = layout["rows"]
    length = local[0][0].shape[0]
    buf[...] = jnp.zeros_like(buf)
    if layout["direct"]:
        fill_slots(kv_pieces, layout["slots"], kvs)
        for ref, sl in zip(weights, layout["wslots"]):
            for i, s in enumerate(sl):
                d = me ^ s
                at = pl.multiple_of(d * rows, rows)
                if ref.shape[1] == 5 * rows:
                    w_back[pl.ds(pl.multiple_of(d * 4 * rows, 4 * rows), 4 * rows), :] = ref[i, 0 : 4 * rows, :]
                    w_out[pl.ds(at, rows), :] = ref[i, 4 * rows : 5 * rows, :]
                else:
                    for c in range(4):
                        w_in[pl.ds(at, rows), c * 512 : (c + 1) * 512] = ref[i, c * rows : (c + 1) * rows, :]
    else:
        w_out[...] = weights[0][...]
        w_in[...] = weights[1][...]
        w_back[...] = weights[2][...]

    masks = head_masks()
    ones = head_ones(64)
    select = sibling_rows(True)
    spread = copy_columns(length, length - 32, 32)
    sums = sum_rows(length, length - 32, BLOCK)
    columns = head_columns()
    for m in range(2):
        num_ref, den_ref, vbar_ref, coarse_ref = local[m]
        vbar = vbar_ref[0:1, :]
        far_q = coarse_ref[length - 32 : length, 0:512]
        take_siblings(layout, ints_ref, m, kvs if layout["direct"] else kv_pieces[0], buf)
        remote = mm(select, buf[...])
        key_r = remote[:, 0:512].astype(BF)
        val_r = (remote[:, 512:1024].astype(BF).astype(F32) - vbar).astype(BF)
        kvr_ref[m * 64 : (m + 1) * 64, 0:512] = key_r
        kvr_ref[m * 64 : (m + 1) * 64, 512:1024] = val_r
        rb = rb_ref[m]
        nums = []
        dens = []
        for p in range(PAIRS):
            lanes = slice(p * WIDE, (p + 1) * WIDE)
            scores = mm_nt(far_q[:, lanes], stacked(key_r[:, lanes], masks))
            wr = jnp.exp2(scores * SCALE2 + rb).astype(BF)
            wr_ref[m * 32 : (m + 1) * 32, lanes] = wr
            both = mm(wr, jnp.concatenate([stacked(val_r[:, lanes], masks), ones], axis=1))
            nums.append(both[:, :WIDE])
            dens.append(both[:, WIDE:])
        far_num[...] = jnp.concatenate(nums, axis=1)
        far_den[...] = jnp.concatenate(dens, axis=1)
        for r in range(0, length, STEP):
            own = slice(r, r + STEP)
            part = slice(m * length + r, m * length + r + STEP)
            num = num_ref[own, :] + mm_split(spread[own, :], far_num[...])
            den = den_ref[own, :] + mm_split(spread[own, :], far_den[...])
            inverse_den = 1.0 / den
            centred_o = num * inverse_den
            attended = (centred_o + vbar).astype(BF)
            att_ref[part, :] = attended
            mixed = x_ref[part, :].astype(F32) + mm(attended, w_out[...])
            normal, inverse = normalize(mixed)
            normed = (normal * vec_ref[1:2, :] + vec_ref[3:4, :]).astype(BF)
            norm_ref[part, :] = normed
            top_b = go_ref[part, :]
            g_norm = jnp.zeros_like(mixed)
            def products(c):
                lanes = slice(c * CHUNK, (c + 1) * CHUNK)
                return mm(normed, w_in[:, lanes]), mm_nt(top_b, w_back[lanes, :])

            ahead = products(0)
            for c in range(2048 // CHUNK):
                lanes = slice(c * CHUNK, (c + 1) * CHUNK)
                pre, g_hidden = ahead
                if c + 1 < 2048 // CHUNK:
                    ahead = products(c + 1)
                pre = pre + bias_ref[0:1, lanes]
                cdf = 0.5 + 0.5 * lax.erf(pre * math.sqrt(0.5))
                hidden = (pre * cdf).astype(BF)
                hid_ref[part, lanes] = hidden
                slope = cdf + pre * (jnp.exp(-0.5 * pre * pre) * (1.0 / math.sqrt(2.0 * math.pi)))
                g_pre = g_hidden * slope
                total = jnp.broadcast_to(jnp.sum(g_pre, axis=0, keepdims=True), (8, CHUNK))
                sbias_ref[m, :, lanes] = total if r == 0 else sbias_ref[m, :, lanes] + total
                g_pre_b = g_pre.astype(BF)
                gpre_ref[part, lanes] = g_pre_b
                g_norm = g_norm + mm_nt(g_pre_b, w_in[:, lanes])
            top = top_b.astype(F32)
            scaled = g_norm * vec_ref[1:2, :]
            g_mixed = top + (
                scaled
                - jnp.mean(scaled, axis=-1, keepdims=True)
                - normal * jnp.mean(scaled * normal, axis=-1, keepdims=True)
            ) * inverse
            gmix_ref[part, :] = g_mixed
            total = jnp.concatenate(
                [
                    jnp.sum(g_norm * normal, axis=0, keepdims=True),
                    jnp.sum(g_norm, axis=0, keepdims=True),
                    jnp.sum(top, axis=0, keepdims=True),
                    jnp.zeros((5, 512), F32),
                ],
                axis=0,
            )
            small_ref[m] = total if r == 0 else small_ref[m] + total
            gt = g_mixed.astype(BF)
            gt_ref[part, :] = gt
            ghat = (mm_nt(gt, w_out[...]) * inverse_den).astype(BF)
            ghat_ref[part, :] = ghat
            dots = split_mm(ghat.astype(F32) * centred_o, columns)
            dots_h, dots_l = split(dots)
            ch_ref[part, :] = dots_h
            cl_ref[part, :] = dots_l
        part = slice(m * length, (m + 1) * length)
        g_sum = mm(sums, ghat_ref[part, :]).astype(BF)
        c_sum = mm(sums, ch_ref[part, :]) + mm(sums, cl_ref[part, :])
        c_sum = c_sum + split_mm(g_sum.astype(F32) * vbar, columns)
        c_h, c_l = split(c_sum)
        pay = slice(m * BLOCK, (m + 1) * BLOCK)
        pay_ref[pay, 0:512] = far_q[0:BLOCK, :]
        pay_ref[pay, 512:1024] = g_sum
        pay_ref[pay, 1024:1152] = even_columns(c_h, c_l)


def wide_in_kernel(layout, me_ref, gpre_ref, norm_ref, att_ref, gt_ref, *refs):
    rows = layout["rows"]
    up, out = refs[-2:]
    for c in range(4):
        lanes = slice(c * 512, (c + 1) * 512)
        up[:, lanes] = mm_tn(norm_ref[...], gpre_ref[:, lanes]).astype(BF)
    out[...] = mm_tn(att_ref[...], gt_ref[...]).astype(BF)
    if layout["direct"]:
        for half, ref in enumerate(refs[:2]):
            for i, s in enumerate(layout["order"]):
                at = pl.multiple_of((me_ref[0] ^ (s ^ half)) * rows, rows)
                for c in range(4):
                    ref[i, c * rows : (c + 1) * rows, :] = up[pl.ds(at, rows), c * 512 : (c + 1) * 512]
                ref[i, 4 * rows : 5 * rows, :] = out[pl.ds(at, rows), :]


def wide_back_kernel(layout, me_ref, hid_ref, go_ref, *refs):
    rows = 4 * layout["rows"]
    back = refs[-1]
    for c in range(4):
        lanes = slice(c * 512, (c + 1) * 512)
        back[lanes, :] = mm_tn(hid_ref[:, lanes], go_ref[...]).astype(BF)
    if layout["direct"]:
        for half, ref in enumerate(refs[:2]):
            for i, s in enumerate(layout["order"]):
                at = pl.multiple_of((me_ref[0] ^ (s ^ half)) * rows, rows)
                ref[i] = back[pl.ds(at, rows), :]


def back_kernel(m, qkv_ref, coarse_ref, w_ref, ghat_ref, ch_ref, cl_ref, vbar_ref, wr_ref, kvr_ref, grad_ref,
                vals, gsum, ext_f, ext_c, gcoarse, matrix, minus_ref):
    masks = head_masks()
    length = vals.shape[0]
    base = m * length
    whole = slice(base, base + length)
    vals[...] = (qkv_ref[whole, 1024:1536].astype(F32) - vbar_ref[0:1, :]).astype(BF)
    matrix[...] = sum_rows(length, 0, length)
    for p in range(PAIRS):
        minus_ref[p] = minus_columns(p, 128)
    gsum[...] = mm(matrix[...], ghat_ref[whole, :]).astype(BF)
    c_sum = mm(matrix[...], ch_ref[whole, :]) + mm(matrix[...], cl_ref[whole, :])
    c_h, c_l = split(c_sum)
    ext_c[...] = even_columns(c_h, c_l)
    ext_f[...] = even_columns(ch_ref[whole, :], cl_ref[whole, :])
    zero = jnp.zeros((128, WIDE), BF)
    for t in range(8):
        rows = slice((t % 4) * 128, (t % 4) * 128 + 128)
        far = slice(base + (t % 4) * 128, base + (t % 4) * 128 + 128)
        for p in range(PAIRS):
            lanes = slice(p * WIDE, (p + 1) * WIDE)
            lanes_k = slice(512 + p * WIDE, 512 + (p + 1) * WIDE)
            lanes_v = slice(1024 + p * WIDE, 1024 + (p + 1) * WIDE)
            if t < 4:
                q, k, v = qkv_ref[far, lanes], qkv_ref[far, lanes_k], vals[rows, lanes]
                g, ext = ghat_ref[far, lanes], ext_f[rows, :]
            else:
                q, k, v = coarse_ref[rows, lanes], coarse_ref[rows, lanes_k], coarse_ref[rows, lanes_v]
                g, ext = gsum[rows, lanes], ext_c[rows, :]
            weights = w_ref[t, :, p * 256 : (p + 1) * 256]
            left = jnp.concatenate([g, ext], axis=1)
            right = jnp.concatenate([stacked(v, masks), minus_ref[p]], axis=1)
            gs = (weights.astype(F32) * mm_nt(left, right)).astype(BF)
            g_q = mm(gs, stacked(k, masks)) * SCALE
            g_kv = mm_tn(
                jnp.concatenate([gs, weights], axis=0),
                jnp.concatenate([jnp.concatenate([q, zero], axis=1), jnp.concatenate([zero, g], axis=1)], axis=0),
            )
            g_k = unstacked(g_kv[:, :WIDE], masks) * SCALE
            g_v = unstacked(g_kv[:, WIDE:], masks)
            if t < 4:
                grad_ref[rows, lanes] = g_q
                grad_ref[rows, lanes_k] = g_k
                grad_ref[rows, lanes_v] = g_v
            else:
                gcoarse[rows, lanes] = g_q.astype(BF)
                gcoarse[rows, lanes_k] = g_k.astype(BF)
                gcoarse[rows, lanes_v] = g_v.astype(BF)
    far = slice(480, 512)
    for p in range(PAIRS):
        lanes = slice(p * WIDE, (p + 1) * WIDE)
        left = jnp.concatenate([gsum[far, lanes], ext_c[far, :]], axis=1)
        minus = minus_columns(p, 64)
        part = slice(m * 64, (m + 1) * 64)
        right = jnp.concatenate([stacked(kvr_ref[part, 512 + p * WIDE : 512 + (p + 1) * WIDE], masks), minus], axis=1)
        gs = (wr_ref[m * 32 : (m + 1) * 32, lanes].astype(F32) * mm_nt(left, right)).astype(BF)
        gcoarse[far, lanes] = (mm(gs, stacked(kvr_ref[part, lanes], masks)) * SCALE).astype(BF)
    matrix[...] = share_columns(length, 0, length)
    grad_ref[...] += mm(matrix[...], gcoarse[...])


def last_kernel(layout, ints_ref, x_ref, gmix_ref, w_ref, vec_ref, rb_ref, small_ref, sbias_ref, *refs):
    local, refs = (refs[0:3], refs[3:6]), refs[6:]
    count = len(layout["slots"])
    pieces = refs[:count]
    if layout["direct"]:
        ingrad_ref, *blocks, slots_v, buf, gqkv, wgrad = refs[count:]
    else:
        ingrad_ref, wgrad, tail_ref, buf, gqkv = refs[count:]
    me = ints_ref[0]
    rows = layout["rows"]
    devices = layout["devices"]
    masks = head_masks()
    if layout["direct"]:
        fill_slots(pieces, layout["slots"], slots_v)
    buf[...] = jnp.zeros_like(buf)
    length = x_ref.shape[0] // 2
    lane = lax.broadcasted_iota(jnp.int32, (1, 128), 1)
    select, select_sum = sibling_rows(True), sibling_rows(False)
    spread = share_columns(length, length - 32, 32)
    columns, twins = head_columns(), twin_columns()
    for m in range(2):
        grad_ref, coarse_ref, vbar_ref = local[m]
        vbar = vbar_ref[0:1, :]
        take_siblings(layout, ints_ref, m, slots_v if layout["direct"] else pieces[0], buf)
        q_r = mm(select, buf[:, 0:512]).astype(BF)
        g_r = mm(select_sum, buf[:, 512:1024]).astype(BF)
        c_r = mm_split(select_sum, mm(buf[:, 1024:1152], twins))
        c_r = c_r - split_mm(g_r.astype(F32) * vbar, columns)
        c_h, c_l = split(c_r)
        ext = even_columns(c_h, c_l).astype(F32)
        rb = rb_ref[m]
        g_keys = []
        g_vals = []
        for p in range(PAIRS):
            lanes = slice(p * WIDE, (p + 1) * WIDE)
            k = coarse_ref[length - 32 : length, 512 + p * WIDE : 512 + (p + 1) * WIDE]
            v = coarse_ref[length - 32 : length, 1024 + p * WIDE : 1024 + (p + 1) * WIDE]
            qq = stacked(q_r[:, lanes], masks)
            gg = stacked(g_r[:, lanes], masks)
            weights = jnp.exp2(mm_nt(k, qq) * SCALE2 + rb)
            ones_a = ((lane // 2) == 4 * p).astype(F32)
            ones_b = ((lane // 2) == 4 * p + 1).astype(F32)
            ext_p = jnp.concatenate([ext * ones_a, ext * ones_b], axis=0).astype(BF)
            left = jnp.concatenate([v, jnp.full((32, 128), -1.0, BF)], axis=1)
            gs = (weights * mm_nt(left, jnp.concatenate([gg, ext_p], axis=1))).astype(BF)
            g_keys.append(mm(gs, qq) * SCALE)
            g_vals.append(mm(weights.astype(BF), gg))
        extra = mm_split(spread, jnp.concatenate(g_keys + g_vals, axis=1))
        part = slice(m * length, (m + 1) * length)
        gqkv[part, 0:512] = grad_ref[:, 0:512].astype(BF)
        gqkv[part, 512:1536] = (grad_ref[:, 512:1536] + extra).astype(BF)
    g_norm = mm_nt(gqkv[...], w_ref[...])
    normal, inverse = normalize(x_ref[...].astype(F32))
    normed = (normal * vec_ref[0:1, :] + vec_ref[2:3, :]).astype(BF)
    scaled = g_norm * vec_ref[0:1, :]
    ingrad_ref[...] = gmix_ref[...] + (
        scaled
        - jnp.mean(scaled, axis=-1, keepdims=True)
        - normal * jnp.mean(scaled * normal, axis=-1, keepdims=True)
    ) * inverse
    for part in range(3):
        lanes = slice(part * 512, (part + 1) * 512)
        wgrad[:, lanes] = mm_tn(normed, gqkv[:, lanes]).astype(BF)
    vectors = [
        jnp.sum(g_norm * normal, axis=0, keepdims=True),
        small_ref[0, 0:1, :] + small_ref[1, 0:1, :],
        jnp.sum(g_norm, axis=0, keepdims=True),
        small_ref[0, 1:2, :] + small_ref[1, 1:2, :],
        small_ref[0, 2:3, :] + small_ref[1, 2:3, :],
    ]
    bias = sbias_ref[0, 0:1, :] + sbias_ref[1, 0:1, :]
    halves = ((0, 0), (1, 1)) if layout["direct"] else ((None, None),)
    for half, _ in halves:
        order = list(layout["order"]) if half is not None else list(range(devices))
        owner = slot_numbers(order, (len(order), 1), 0)
        if half is not None:
            owner = (owner ^ half) ^ me
        tail = gather_small(vectors, bias, owner, devices)
        if half is None:
            tail_ref[...] = tail
            continue
        first, second = blocks[2 * half : 2 * half + 2]
        for i, s in enumerate(order):
            at = pl.multiple_of((me ^ (s ^ half)) * rows, rows)
            for part in range(2):
                first[i, part * rows : (part + 1) * rows, :] = wgrad[pl.ds(at, rows), part * 512 : (part + 1) * 512]
            second[i, 0:rows, :] = wgrad[pl.ds(at, rows), 1024:1536]
            second[i, rows : rows + 8, 0:256] = jnp.broadcast_to(tail[i : i + 1, :], (8, 256)).astype(BF)
            second[i, rows : rows + 8, 256:512] = jnp.zeros((8, 256), BF)


def gather_small(vectors, bias, owner, devices):
    w = 512 // devices
    wide = 2048 // devices
    count = owner.shape[0]
    col = lax.broadcasted_iota(jnp.int32, (count, 512), 1)
    mine = (col // w == owner).astype(F32)
    col_t = lax.broadcasted_iota(jnp.int32, (512, 128), 0)
    lane_t = lax.broadcasted_iota(jnp.int32, (512, 128), 1)
    total = jnp.zeros((count, 128), F32)
    for p, row in enumerate(vectors):
        place = ((lane_t // w == p) & (lane_t % w == col_t % w)).astype(F32).astype(BF)
        total = total + split_mm(row * mine, place)
    col_w = lax.broadcasted_iota(jnp.int32, (count, 2048), 1)
    mine_w = (col_w // wide == owner).astype(F32)
    col_tw = lax.broadcasted_iota(jnp.int32, (2048, 128), 0)
    lane_tw = lax.broadcasted_iota(jnp.int32, (2048, 128), 1)
    place_w = (lane_tw == col_tw % wide).astype(F32).astype(BF)
    return jnp.concatenate([total, split_mm(bias * mine_w, place_w)], axis=1)


def total_of(refs, rows):
    total = refs[0][0, rows, :].astype(F32)
    for r in refs[1:]:
        total = total + r[0, rows, :].astype(F32)
    return total


def finish_wide_kernel(rows, *refs):
    ins, (back_ref, in_ref, out_ref) = refs[:-3], refs[-3:]
    for c in range(4):
        in_ref[:, c * 512 : (c + 1) * 512] = total_of(ins, slice(c * rows, (c + 1) * rows))
    out_ref[...] = total_of(ins, slice(4 * rows, 5 * rows))
    back_ref[...] = total_of(ins, slice(5 * rows, 9 * rows))


def finish_qkv_kernel(rows, *refs):
    ins, (q_ref, k_ref, v_ref, gain_ref, shift_ref, bi_ref, bo_ref) = refs[:-7], refs[-7:]
    for part, ref in enumerate((q_ref, k_ref, v_ref)):
        ref[...] = total_of(ins, slice(part * rows, (part + 1) * rows))
    tail = total_of(ins, slice(3 * rows, 3 * rows + 8))[0:1]
    for r in range(2):
        gain_ref[r : r + 1, :] = tail[:, r * rows : (r + 1) * rows]
        shift_ref[r : r + 1, :] = tail[:, (2 + r) * rows : (3 + r) * rows]
    bo_ref[...] = tail[:, 4 * rows : 5 * rows]
    bi_ref[...] = tail[:, 128 : 128 + bi_ref.shape[1]]


def remote_plan(lengths, group_order, position, devices, length):
    count = lengths.shape[1]
    lower = np.tril(np.ones((count, count), np.int32))
    seq_ends = jnp.sum(lengths[:, None, :] * lower[None], axis=2)
    device_ids = np.arange(devices, dtype=np.int32)
    group_id = jnp.sum(jnp.where(device_ids == position, group_order, 0), axis=1)[:, None]
    level_s = np.repeat(np.arange(4, dtype=np.int32), [1, 2, 4, 8])
    index_s = np.concatenate([np.arange(1 << level, dtype=np.int32) for level in range(4)])
    siblings = (((group_id >> level_s) ^ 1) << level_s) + index_s
    owner = jnp.sum(jnp.where(group_order[:, None, :] == siblings[:, :, None], device_ids, 0), axis=2)
    level_q = np.full((32,), -1, np.int32)
    start_q = np.zeros((32,), np.int32)
    row = 0
    for level in range(4):
        for i in range(length // (32 << level)):
            level_q[row] = level
            start_q[row] = i * (32 << level)
            row += 1
    level_k = np.tile(np.repeat(np.arange(4, dtype=np.int32), BLOCK), 2)
    start_k = np.tile(np.arange(BLOCK, dtype=np.int32), 8) * (32 << level_k)
    first_k = (((group_id >> level_k) ^ 1) << level_k) * length
    starts = np.concatenate([start_q, np.array([0, length // 2], np.int32)])
    places = jnp.concatenate([first_k + start_k, group_id * length + starts], axis=1)
    seq = jnp.sum((places[:, :, None] >= seq_ends[:, None, :]).astype(jnp.int32), axis=2)
    same = (seq[:, 128:160, None] == seq[:, None, :128]) & (level_q[:, None] == level_k[None, :])
    bias = jnp.where(same, (level_k + 5).astype(np.float32), OFF)
    apart = (seq[:, 160] != seq[:, 161]).astype(jnp.int32)
    ints = jnp.concatenate([jnp.reshape(position, (1,)), (owner ^ position).reshape(-1), apart]).astype(jnp.int32)
    return ints, bias


def exchange_order(stack, position, devices):
    rest = stack.shape[1:]
    for bit in range(devices.bit_length() - 1):
        cut = stack.reshape((devices >> (bit + 1), 2, 1 << bit) + rest)
        stack = jnp.where((position >> bit) & 1 > 0, cut[:, ::-1], cut).reshape((devices,) + rest)
    return stack


def reordered(stack, order):
    return jnp.concatenate([stack[int(i) : int(i) + 1] for i in order], axis=0)


def natural(pieces, position, devices):
    order = [s for _, sl in pieces for s in sl]
    stack = jnp.concatenate([p for p, _ in pieces], axis=0)
    return exchange_order(reordered(stack, np.argsort(np.array(order))), position, devices)


def picked(pieces, ints, micro_n):
    order = [s for _, sl in pieces for s in sl]
    stack = reordered(jnp.concatenate([p for p, _ in pieces], axis=0), np.argsort(np.array(order)))
    blocks = []
    for m in range(micro_n):
        for b in range(SIBS):
            block = lax.dynamic_slice_in_dim(stack, ints[1 + m * SIBS + b], 1, axis=0)
            blocks.append(block[:, m * BLOCK : (m + 1) * BLOCK])
    return jnp.concatenate(blocks, axis=0)


def on_device(
    layer_in,
    out_grad,
    lengths,
    group_order,
    w_query,
    w_key,
    w_value,
    w_out,
    w_in,
    w_back,
    norm_gain,
    norm_shift,
    ffn_bias_in,
    ffn_bias_out,
):
    devices = lax.axis_size("fsdp")
    position = lax.axis_index("fsdp")
    micro_n, length, width = layer_in.shape
    hidden_n = w_in.shape[1]
    tokens = micro_n * length
    rows = w_query.shape[0]
    half = devices // 2
    direct = rows % 16 == 0
    x = layer_in.reshape(tokens, width)
    top = out_grad.reshape(tokens, width)

    small_rows = -(-3 * rows // 8) * 8
    biases = (ffn_bias_in.reshape(1, -1), ffn_bias_out.reshape(1, -1))
    if direct:
        shards = (w_query, w_key, w_value, w_out, w_in, w_back, norm_gain, norm_shift, *biases)
        packed, packed_w = pl.pallas_call(
            lambda *refs: pack_kernel(rows, *refs),
            grid=(1,),
            in_specs=[pl.BlockSpec(a.shape, lambda i: (0, 0)) for a in shards],
            out_specs=[pl.BlockSpec(memory_space=pltpu.VMEM)] * 2,
            out_shape=[shape_of((3 * rows + 8, width), BF), shape_of((9 * rows, width), BF)],
            name="pack",
        )(*shards)
    else:
        tail = jnp.concatenate(
            [
                norm_gain.reshape(-1),
                norm_shift.reshape(-1),
                ffn_bias_out,
                jnp.zeros((128 - 5 * rows,), BF),
                ffn_bias_in,
                jnp.zeros((384 - ffn_bias_in.shape[0],), BF),
            ]
        )
        packed = jnp.concatenate(
            [
                w_query,
                w_key,
                w_value,
                jnp.zeros((small_rows - 3 * rows, width), BF),
                jnp.broadcast_to(tail[None, :], (8, width)),
            ],
            axis=0,
        )
        packed_w = jnp.concatenate(
            [w_back, w_out] + [w_in[:, c * width : (c + 1) * width] for c in range(hidden_n // width)], axis=0
        )
    marks_q, marks_w = [], []
    pieces_q = core_gather(staged_gather(packed, devices, marks=marks_q), devices)
    lengths, group_order = follow((lengths, group_order), marks_q[0])
    pieces_bo, pieces_in = crossed_gather(packed_w, 5 * rows, devices, marks_w, [])
    ints, remote_bias = remote_plan(lengths, group_order, position, devices, length)

    layout = {
        "rows": rows,
        "devices": devices,
        "direct": direct,
        "small": small_rows,
        "slots": [sl for _, sl in pieces_q],
        "first_slot": 1,
        "order": scatter_order(devices),
    }
    flag_at = 1 + micro_n * SIBS
    arrays_q = [p for p, _ in pieces_q]
    if not direct:
        nat = natural(pieces_q, position, devices)
        arrays_q.append(
            jnp.concatenate([nat[:, part * rows : (part + 1) * rows].reshape(width, width) for part in range(3)], axis=1)
        )
    me = jnp.reshape(position, (1,)).astype(jnp.int32)
    qkv, w_qkv, vectors, bias_row, coarse_kv = call(
        lambda *refs: first_kernel(layout, *refs),
        "norm_qkv",
        [
            ((tokens, 3 * width), BF),
            ((width, 3 * width), BF),
            ((8, width), F32),
            ((8, hidden_n), F32),
            ((micro_n * BLOCK, 2 * width), BF),
        ],
        (ints, x, *arrays_q),
        scalars=1,
        mib=8,
        us=5.0,
    )

    local = [
        call(
            lambda *refs, m=m: local_kernel(m, flag_at, *refs),
            f"local_forward_{m}",
            [
                ((length, width), F32),
                ((length, width), F32),
                ((length, 3 * width), BF),
                ((8, 128, 256 * PAIRS), BF),
                ((8, width), F32),
            ],
            (ints, qkv),
            scalars=1,
            scratch=[
                ((length, width), BF),
                ((length, width), F32),
                ((length, width), F32),
                ((256, WIDE), BF),
                ((length, length), BF),
                ((4, 128, 256), F32),
            ],
            mib=8,
            us=4.0,
            after=marks_w if m == 0 else (),
        )
        for m in range(micro_n)
    ]

    pieces_kv = staged_gather(coarse_kv, devices, [(local[0][4], *marks_w), (local[1][4],)])
    pieces_kv = core_gather(pieces_kv, devices)
    arrays_kv = [p for p, _ in pieces_kv] if direct else [picked(pieces_kv, ints, micro_n)]
    if direct:
        weights_in = [p for p, _ in pieces_bo + pieces_in]
    else:
        nat_bo, nat_in = natural(pieces_bo, position, devices), natural(pieces_in, position, devices)
        weights_in = [
            nat_bo[:, 4 * rows :].reshape(width, width),
            jnp.concatenate([nat_in[:, c * rows : (c + 1) * rows].reshape(width, width) for c in range(4)], axis=1),
            nat_bo[:, : 4 * rows].reshape(hidden_n, width),
        ]
    layout_m = dict(
        layout,
        slots=[sl for _, sl in pieces_kv][: len(arrays_kv)],
        wslots=[sl for _, sl in pieces_bo + pieces_in],
        n_weights=len(weights_in),
    )
    per_local = [a for num, den, coarse, _, vbar in local for a in (num, den, vbar, coarse)]
    (hidden, g_pre, normed_two, attended, gt, g_mixed, ghat, dots_h, dots_l, payload, far_kv, far_w,
     small_sums, bias_sums) = call(
        lambda *refs: middle_kernel(layout_m, *refs),
        "middle",
        [
            ((tokens, hidden_n), BF),
            ((tokens, hidden_n), BF),
            ((tokens, width), BF),
            ((tokens, width), BF),
            ((tokens, width), BF),
            ((tokens, width), F32),
            ((tokens, width), BF),
            ((tokens, 128), BF),
            ((tokens, 128), BF),
            ((micro_n * BLOCK, 2 * width + 128), BF),
            ((micro_n * 64, 2 * width), BF),
            ((micro_n * 32, width), BF),
            ((micro_n, 8, width), F32),
            ((micro_n, 8, hidden_n), F32),
        ],
        (ints, x, top, remote_bias, vectors, bias_row, *per_local, *arrays_kv, *weights_in),
        scalars=1,
        scratch=[((devices, micro_n * BLOCK, 2 * width), BF)] * direct
        + [
            ((256, 2 * width), BF),
            ((width, width), BF),
            ((width, hidden_n), BF),
            ((hidden_n, width), BF),
            ((32, width), F32),
            ((32, width), F32),
        ],
        mib=20,
        us=20.0,
    )

    order = np.array(layout["order"], np.int32)
    stages = bit_groups(devices)[::-1]

    def halves(stack):
        stack = exchange_order(stack, position, devices)
        return reordered(stack, order), reordered(stack, order ^ 1)

    def wide_grads(body, name, ins, plain, count, after):
        blocks = [((half, count, width), BF)] * 2
        return call(
            lambda *refs: body(layout, *refs),
            name,
            blocks if direct else plain,
            ins,
            scalars=1,
            scratch=plain if direct else (),
            mib=8,
            us=3.0,
            after=after,
        )

    begun = first_sends(payload, devices)
    grads_a = wide_grads(
        wide_in_kernel,
        "wide_in",
        (me, g_pre, normed_two, attended, gt),
        [((width, hidden_n), BF), ((width, width), BF)],
        5 * rows,
        (begun[1],),
    )
    grads_b = wide_grads(
        wide_back_kernel, "wide_back", (me, hidden, top), [((hidden_n, width), BF)], 4 * rows, (begun[1],)
    )
    pieces_g = staged_gather(payload, devices, [(grads_a[0], grads_b[0])], begun=begun)
    if direct:
        keeps, sents = (grads_a[0], grads_b[0]), (grads_a[1], grads_b[1])
    else:
        g_in, g_out = grads_a
        stack = [g_in[:, c * width : (c + 1) * width].reshape(devices, rows, width) for c in range(4)]
        stack = jnp.concatenate(stack + [g_out.reshape(devices, rows, width)], axis=1)
        keeps, sents = zip(halves(stack), halves(grads_b[0].reshape(devices, 4 * rows, width)))
    arrived = [send(a, 1, devices) for a in sents]

    def local_backward(m, after):
        return call(
            lambda *refs: back_kernel(m, *refs),
            f"local_backward_{m}",
            [((length, 3 * width), F32)],
            (qkv, local[m][2], local[m][3], ghat, dots_h, dots_l, local[m][4], far_w, far_kv),
            scratch=[
                ((length, width), BF),
                ((length, width), BF),
                ((length, 128), BF),
                ((length, 128), BF),
                ((length, 3 * width), BF),
                ((length, length), BF),
                ((PAIRS, 256, 128), BF),
            ],
            mib=8,
            us=8.0,
            after=after,
        )[0]

    grads = [local_backward(0, tuple(sents))]
    held_w, received_w = scatter_step(keeps, [arrived], stages[0], devices, "add_wide_0", (grads[0],))
    pieces_g = core_gather(pieces_g, devices, held_w)
    arrivals = [p for p, _ in pieces_g]
    grads.append(local_backward(1, (*held_w, *arrivals)))

    arrays_g = [p for p, _ in pieces_g] if direct else [picked(pieces_g, ints, micro_n)]
    layout_l = dict(layout, slots=[sl for _, sl in pieces_g][: len(arrays_g)])
    per_local = [a for m in range(micro_n) for a in (grads[m], local[m][2], local[m][4])]
    last_in = (ints, x, g_mixed, w_qkv, vectors, remote_bias, small_sums, bias_sums, *per_local, *arrays_g)
    scratch = [((devices, micro_n * BLOCK, 2 * width + 128), BF)] * direct + [
        ((256, 2 * width + 128), BF),
        ((tokens, 3 * width), BF),
    ]
    mib = 17
    if direct:
        in_grad, *blocks = call(
            lambda *refs: last_kernel(layout_l, *refs),
            "qkv_grads",
            [((tokens, width), F32)] + [((half, 2 * rows, width), BF), ((half, rows + 8, width), BF)] * 2,
            last_in,
            scalars=1,
            scratch=scratch + [((width, 3 * width), BF)],
            mib=mib,
            us=10.0,
        )
    else:
        in_grad, g_qkv, tails = call(
            lambda *refs: last_kernel(layout_l, *refs),
            "qkv_grads",
            [((tokens, width), F32), ((width, 3 * width), BF), ((devices, 256), F32)],
            last_in,
            scalars=1,
            scratch=scratch,
            mib=mib,
            us=10.0,
        )
        stack = jnp.concatenate(
            [g_qkv[:, c * width : (c + 1) * width].reshape(devices, rows, width) for c in range(3)]
            + [jnp.broadcast_to(jnp.pad(tails, ((0, 0), (0, 256)))[:, None, :], (devices, 8, width)).astype(BF)],
            axis=1,
        )
        blocks = [a[:, cut] for a in halves(stack) for cut in (slice(0, 2 * rows), slice(2 * rows, None))]
    keep_q, sent_q = blocks[:2], blocks[2:]
    given = [p for p, _ in pieces_bo] if direct else [weights_in[0], weights_in[2]]
    layer_out, mark = call(
        lambda *refs: output_kernel(layout_m, *refs),
        "layer_out",
        [((tokens, width), BF), ((8, 128), F32)],
        (me, hidden, attended, x, vectors, *given),
        scalars=1,
        scratch=[((width, width), BF), ((hidden_n, width), BF)],
        mib=8,
        us=3.0,
        after=(keep_q[0],),
    )
    received_q = [[send(a, 1, devices) for a in sent_q]]
    held_q = keep_q
    for stage, group in enumerate(stages):
        if stage + 1 < len(stages):
            late = (mark,) if stage == 0 else held_q
            held_w, received_w = scatter_step(held_w, received_w, stages[stage + 1], devices, f"add_wide_{stage + 1}", late)
        held_q, received_q = scatter_step(held_q, received_q, group, devices, f"add_qkv_{stage}", held_w if stage == 0 else ())
    g_back, g_in, g_out = call(
        lambda *refs: finish_wide_kernel(rows, *refs),
        "finish_wide",
        [((4 * rows, width), F32), ((rows, hidden_n), F32), ((rows, width), F32)],
        (*held_w, *(r for (r,) in received_w)),
        mib=4,
        us=1.0,
    )
    g_query, g_key, g_value, g_gain, g_shift, g_bias_in, g_bias_out = call(
        lambda *refs: finish_qkv_kernel(rows, *refs),
        "finish_qkv",
        [((rows, width), F32)] * 3
        + [((2, rows), F32)] * 2
        + [((1, hidden_n // devices), F32), ((1, rows), F32)],
        (*held_q, *(r for (r,) in received_q)),
        mib=4,
        us=1.0,
    )
    return (
        layer_out.reshape(micro_n, length, width),
        in_grad.reshape(micro_n, length, width),
        g_query,
        g_key,
        g_value,
        g_out,
        g_in,
        g_back,
        g_gain,
        g_shift,
        g_bias_in.reshape(-1),
        g_bias_out.reshape(-1),
    )


def solution(mesh):
    placed = (
        P(None, "fsdp", None),
        P(None, "fsdp", None),
        P(),
        P(),
        P("fsdp", None),
        P("fsdp", None),
        P("fsdp", None),
        P("fsdp", None),
        P("fsdp", None),
        P("fsdp", None),
        P(None, "fsdp"),
        P(None, "fsdp"),
        P("fsdp"),
        P("fsdp"),
    )
    return jax.shard_map(
        on_device,
        mesh=mesh,
        in_specs=placed,
        out_specs=(
            P(None, "fsdp", None),
            P(None, "fsdp", None),
            P("fsdp", None),
            P("fsdp", None),
            P("fsdp", None),
            P("fsdp", None),
            P("fsdp", None),
            P("fsdp", None),
            P(None, "fsdp"),
            P(None, "fsdp"),
            P("fsdp"),
            P("fsdp"),
        ),
        check_vma=False,
    )
```

```python
import math

import jax
import jax.numpy as jnp
import numpy as np
from jax import lax
from jax.experimental import pallas as pl
from jax.experimental.pallas import tpu as pltpu
from jax.sharding import PartitionSpec as P

HEADS = 8
HEAD_DIM = 64
BLOCK = 16
LEVELS = 9
EPSILON = 1e-05
OFF = -1e30
PAIRS = HEADS // 2
WIDE = 2 * HEAD_DIM
SCALE2 = math.log2(math.e) / math.sqrt(HEAD_DIM)
SCALE = 1.0 / math.sqrt(HEAD_DIM)
BF = jnp.bfloat16
F32 = jnp.float32
SIBS = 15
STEP = 512
CHUNK = 1024


def iota(shape, dim):
    return lax.broadcasted_iota(jnp.int32, shape, dim)


def ones_where(condition, value=1.0):
    return jnp.where(condition, value, 0.0).astype(BF)


def coarse_places(index, length):
    shift = jnp.zeros_like(index)
    start = jnp.zeros_like(index)
    row = 0
    for level_id in range(2, LEVELS + 1):
        shift = shift + (index >= row).astype(jnp.int32)
        start = jnp.where(index >= row, row, start)
        row += length >> (level_id - 1)
    return shift, jnp.where(index >= row, length, index - start)


def members(length, first, count, by_rows):
    shape = (count, length) if by_rows else (length, count)
    narrow = (count, 1) if by_rows else (1, count)
    shift, place = coarse_places(iota(narrow, 0 if by_rows else 1) + first, length)
    covers = (iota(shape, 1 if by_rows else 0) >> shift) == place
    return covers, jnp.exp2(-shift.astype(F32))


def mean_rows(length, first, count):
    covers, share = members(length, first, count, True)
    return ones_where(covers, share)


def sum_rows(length, first, count):
    return ones_where(members(length, first, count, True)[0])


def share_columns(length, first, count):
    covers, share = members(length, first, count, False)
    return ones_where(covers, share)


def copy_columns(length, first, count):
    return ones_where(members(length, first, count, False)[0])


def tile_bias(kind, limit=0):
    row = iota((128, 256), 0)
    key = iota((128, 256), 1) & 127
    block_r, block_k = row // BLOCK, key // BLOCK
    sibling = block_r == (block_k ^ 1)
    if kind == 0:
        return jnp.where(block_r // 2 == block_k // 2, 0.0, OFF)
    if kind < 3:
        return jnp.where(sibling, float(kind), OFF)
    last = jnp.where(row < limit, 4.0, OFF)
    return jnp.where(sibling, jnp.where(row < 64, 3.0, last), OFF)


def sibling_rows(mean):
    row = iota((64, 256), 0)
    level, k = row // BLOCK, row % BLOCK
    span = jnp.left_shift(1, level)
    block = span - 1 + (k >> (4 - level))
    inside = k & ((BLOCK >> level) - 1)
    offset = iota((64, 256), 1) - (block * BLOCK + (inside << level))
    chosen = (offset >= 0) & (offset < span)
    return ones_where(chosen, 1.0 / span.astype(F32)) if mean else ones_where(chosen)


def head_columns():
    head = iota((512, 128), 0) // HEAD_DIM
    return ones_where(iota((512, 128), 1) // 2 == 4 * (head // 2) + head % 2)


def minus_columns(pair, keys):
    second = (iota((2 * keys, 128), 0) >= keys).astype(jnp.int32)
    return ones_where(iota((2 * keys, 128), 1) // 2 == 4 * pair + second, -1.0)


def twin_columns():
    return ones_where(iota((128, 128), 0) // 2 == iota((128, 128), 1) // 2)


def mm(a, b):
    return lax.dot_general(a, b, (((1,), (0,)), ((), ())), preferred_element_type=F32)


def mm_nt(a, b):
    return lax.dot_general(a, b, (((1,), (1,)), ((), ())), preferred_element_type=F32)


def mm_tn(a, b):
    return lax.dot_general(a, b, (((0,), (0,)), ((), ())), preferred_element_type=F32)


def split(a):
    high = a.astype(BF)
    return high, (a - high.astype(F32)).astype(BF)


def mm_split(a, b):
    high, low = split(b)
    return mm(a, high) + mm(a, low)


def split_mm(a, b):
    high, low = split(a)
    return mm(high, b) + mm(low, b)


def head_masks():
    lane = lax.broadcasted_iota(jnp.int32, (1, WIDE), 1)
    first = (lane < HEAD_DIM).astype(F32)
    return first, 1.0 - first


def stacked(a, masks):
    return jnp.concatenate([a * masks[0].astype(a.dtype), a * masks[1].astype(a.dtype)], axis=0)


def unstacked(a, masks):
    half = a.shape[0] // 2
    return a[:half] * masks[0] + a[half:] * masks[1]


def head_ones(keys):
    row = lax.broadcasted_iota(jnp.int32, (2 * keys, WIDE), 0)
    lane = lax.broadcasted_iota(jnp.int32, (2 * keys, WIDE), 1)
    return ((row < keys) == (lane < HEAD_DIM)).astype(F32).astype(BF)


def even_columns(high, low):
    col = lax.broadcasted_iota(jnp.int32, high.shape, 1)
    return jnp.where(col % 2 == 0, high.astype(F32), low.astype(F32)).astype(BF)


def normalize(values):
    centre = jnp.mean(values, axis=-1, keepdims=True)
    centred = values - centre
    spread = jnp.mean(centred * centred, axis=-1, keepdims=True)
    inverse = lax.rsqrt(spread + EPSILON)
    return centred * inverse, inverse


def shape_of(shape, dtype):
    return jax.ShapeDtypeStruct(shape, dtype)


def call(body, name, outs, ins, scalars=0, scratch=(), mib=8, us=2.0, after=()):
    vmem = pl.BlockSpec(memory_space=pltpu.VMEM)
    smem = pl.BlockSpec(memory_space=pltpu.SMEM)
    count, late = len(ins), len(after)

    def kernel(*refs):
        body(*refs[:count], *refs[count + late :])

    return pl.pallas_call(
        kernel,
        in_specs=[smem] * scalars + [vmem] * (count - scalars) + [pl.BlockSpec(memory_space=pl.ANY)] * late,
        out_specs=[pl.BlockSpec(memory_space=pltpu.VMEM)] * len(outs),
        out_shape=[shape_of(shape, dtype) for shape, dtype in outs],
        scratch_shapes=[pltpu.VMEM(shape, dtype) for shape, dtype in scratch],
        compiler_params=pltpu.CompilerParams(vmem_limit_bytes=int(mib * 2**20)),
        cost_estimate=pl.CostEstimate(flops=int(us * 1.8e9), transcendentals=0, bytes_accessed=1024),
        name=name,
    )(*ins, *after)


def bit_groups(devices):
    groups = []
    high = devices.bit_length() - 2
    while high >= 1:
        low = max(1, high - 1)
        groups.append(tuple(range(low, high + 1)))
        high = low - 1
    return groups


def offsets_of(group):
    return [sum(1 << b for i, b in enumerate(group) if k >> i & 1) for k in range(1 << len(group))]


def send(value, offset, devices):
    return lax.ppermute(value, "fsdp", [(i, i ^ offset) for i in range(devices)])


def joined(parts):
    return parts[0] if len(parts) == 1 else jnp.concatenate(parts, axis=0)


def follow(values, *earlier):
    return lax.optimization_barrier((values, earlier))[0] if earlier else values


def first_sends(block, devices):
    held = block[None]
    return [held] + [send(held, k, devices) for k in offsets_of(bit_groups(devices)[0])[1:]]


def staged_gather(block, devices, between=(), marks=None, begun=None):
    between = list(between) + [()] * len(bit_groups(devices))
    held = block[None]
    slots = [0]
    groups = bit_groups(devices)
    for group_id, group in enumerate(groups):
        offsets = offsets_of(group)
        parts = begun if begun and group_id == 0 else [held] + [send(held, k, devices) for k in offsets[1:]]
        parts = follow(parts, *between[group_id])
        if group_id < len(groups) - 1:
            held = joined(parts)
            slots = [s ^ k for k in offsets for s in slots]
            if marks is not None:
                marks.append(held)
    return [(p, [s ^ k for s in slots]) for p, k in zip(parts, offsets)]


def core_gather(pieces, devices, after=()):
    held = follow([p for p, _ in pieces], *after)
    return pieces + [(send(p, 1, devices), [s ^ 1 for s in sl]) for p, (_, sl) in zip(held, pieces)]


def crossed_gather(block, cut, devices, marks, earlier):
    groups = bit_groups(devices)
    parts = [block[None]]
    slots = [0]
    for group in groups[:-1]:
        held = joined(parts)
        offsets = offsets_of(group)
        parts = [held] + [send(held, k, devices) for k in offsets[1:]]
        slots = [s ^ k for k in offsets for s in slots]
    parts = follow(parts, *earlier)
    halves = []
    for rows, order in ((slice(0, cut), groups[-1]), (slice(cut, None), groups[-1][::-1])):
        held, own = joined([p[:, rows] for p in parts]), slots
        for bit in order[:-1]:
            held = joined([held, send(held, 1 << bit, devices)])
            own = own + [s ^ (1 << bit) for s in own]
        marks.append(held)
        last = 1 << order[-1]
        halves.append([(held, own), (send(held, last, devices), [s ^ last for s in own])])
    first, second = follow([[p for p, _ in pieces] for pieces in halves], halves[0][1][0], halves[1][1][0])
    return [
        pieces + [(send(p, 1, devices), [s ^ 1 for s in sl]) for p, (_, sl) in zip(held, pieces)]
        for held, pieces in zip((first, second), halves)
    ]


def add_parts(keeps, received, outs_dtype, name, after=()):
    cuts = len(outs_dtype)
    part = keeps[0].shape[0] // cuts
    count = len(keeps)
    sizes = [k.shape[1] for k in keeps]
    ins = [a for arrays in (keeps, *received) for a in arrays]

    def body(*refs):
        outs = refs[len(ins) :]
        for c in range(cuts):
            for i in range(part):
                row = 0
                for j, size in enumerate(sizes):
                    total = refs[j][c * part + i].astype(F32)
                    for r in refs[count + j : len(ins) : count]:
                        total = total + r[c * part + i].astype(F32)
                    outs[c][i, row : row + size] = total.astype(outs[c].dtype)
                    row += size

    shape = (part, sum(sizes)) + keeps[0].shape[2:]
    return call(body, name, [(shape, d) for d in outs_dtype], ins, mib=4, us=1.5, after=after)


def scatter_order(devices):
    order = [0]
    for group in bit_groups(devices)[::-1]:
        order = [s ^ k for s in order for k in offsets_of(group)]
    return order


def scatter_step(held, received, group, devices, name, after=()):
    offsets = offsets_of(group)
    outs = add_parts(held, received, [F32] + [BF] * (len(offsets) - 1), name, after)
    return outs[:1], [[send(o, k, devices)] for o, k in zip(outs[1:], offsets[1:])]


def pack_kernel(rows, wq_ref, wk_ref, wv_ref, wo_ref, wi_ref, wb_ref, gain_ref, shift_ref, bi_ref, bo_ref, first_ref, second_ref):
    for part, ref in enumerate((wq_ref, wk_ref, wv_ref)):
        first_ref[part * rows : (part + 1) * rows, :] = ref[...]
    tail = jnp.zeros((1, 512), F32)
    for ref, at in ((gain_ref, 0), (shift_ref, 2 * rows), (bo_ref, 4 * rows), (bi_ref, 128)):
        for r in range(ref.shape[0]):
            count = ref.shape[1]
            index = lax.broadcasted_iota(jnp.int32, (count, 512), 0)
            lane = lax.broadcasted_iota(jnp.int32, (count, 512), 1)
            place = (lane == index + (at + r * count)).astype(F32).astype(BF)
            tail = tail + mm(ref[r : r + 1, :], place)
    first_ref[3 * rows : 3 * rows + 8, :] = jnp.broadcast_to(tail, (8, 512)).astype(BF)
    second_ref[0 : 4 * rows, :] = wb_ref[...]
    second_ref[4 * rows : 5 * rows, :] = wo_ref[...]
    for c in range(4):
        second_ref[(5 + c) * rows : (6 + c) * rows, :] = wi_ref[:, c * 512 : (c + 1) * 512]


def first_kernel(layout, ints_ref, x_ref, *refs):
    count = len(layout["slots"])
    pieces, refs = refs[:count], refs[count:]
    if not layout["direct"]:
        given, refs = refs[0], refs[1:]
    qkv_ref, w_ref, vec_ref, bias_ref, coarse_ref = refs
    rows, devices = layout["rows"], layout["devices"]
    me = ints_ref[0]
    small = []
    order = []
    if not layout["direct"]:
        w_ref[...] = given[...]
    for ref, slots in zip(pieces, layout["slots"]):
        for i, s in enumerate(slots):
            if layout["direct"]:
                at = pl.multiple_of((me ^ s) * rows, rows)
                for part in range(3):
                    w_ref[pl.ds(at, rows), part * 512 : (part + 1) * 512] = ref[i, part * rows : (part + 1) * rows, :]
            small.append(ref[i, layout["small"] : layout["small"] + 8, :].astype(F32)[:1])
            order.append(s)
    table = jnp.concatenate(small, axis=0)
    vec_ref[...], bias_ref[...] = spread_small(table, order, me, devices)
    for r in range(4):
        part = slice(r * 256, (r + 1) * 256)
        normal, _ = normalize(x_ref[part, :].astype(F32))
        normed = (normal * vec_ref[0:1, :] + vec_ref[2:3, :]).astype(BF)
        qkv = mm(normed, w_ref[...]).astype(BF)
        qkv_ref[part, :] = qkv
        means = jnp.mean(qkv[:, 512:1536].astype(F32).reshape(8, 32, 1024), axis=1)
        coarse_ref[r * 8 : (r + 1) * 8, :] = means.astype(BF)


def slot_numbers(order, shape, dim):
    index = lax.broadcasted_iota(jnp.int32, shape, dim)
    value = jnp.zeros(shape, jnp.int32)
    for bit in range(max(order).bit_length()):
        on = None
        mask = 0
        for k in range((len(order) - 1).bit_length()):
            if order[1 << k] >> bit & 1:
                mask |= 1 << k
        parity = jnp.zeros(shape, jnp.int32)
        for k in range((len(order) - 1).bit_length()):
            if mask >> k & 1:
                parity = parity ^ ((index >> k) & 1)
        value = value | (parity << bit)
    return value


def spread_small(table, order, me, devices):
    w = 512 // devices
    wide = 2048 // devices
    owner = slot_numbers(order, (devices, 512), 0) ^ me
    col = lax.broadcasted_iota(jnp.int32, (devices, 512), 1)
    mine = (col // w == owner).astype(F32)
    lane = lax.broadcasted_iota(jnp.int32, (devices, 128), 1)
    lane_t = lax.broadcasted_iota(jnp.int32, (128, 512), 0)
    col_t = lax.broadcasted_iota(jnp.int32, (128, 512), 1)
    match = (lane_t % w == col_t % w).astype(F32).astype(BF)
    head = table[:, :128]
    rows = []
    for p in range(5):
        own = (head * (lane // w == p).astype(F32)).astype(BF)
        rows.append(jnp.sum(mm(own, match) * mine, axis=0, keepdims=True))
    rows = rows + [jnp.zeros((1, 512), F32)] * 3
    owner_w = slot_numbers(order, (devices, 2048), 0) ^ me
    col_w = lax.broadcasted_iota(jnp.int32, (devices, 2048), 1)
    mine_w = (col_w // wide == owner_w).astype(F32)
    lane_w = lax.broadcasted_iota(jnp.int32, (128, 2048), 0)
    col_tw = lax.broadcasted_iota(jnp.int32, (128, 2048), 1)
    match_w = (lane_w == col_tw % wide).astype(F32).astype(BF)
    bias = jnp.sum(mm(table[:, 128:256].astype(BF), match_w) * mine_w, axis=0, keepdims=True)
    return jnp.concatenate(rows, axis=0), jnp.broadcast_to(bias, (8, 2048))


def local_kernel(
    m, flag_at, ints_ref, qkv_ref, num_ref, den_ref, coarse_ref, w_ref, vbar_ref, vals, num_c, den_c, ones, matrix, biases,
):
    limit = jnp.where(ints_ref[flag_at + m] > 0, 64, 96)
    masks = head_masks()
    ones[...] = head_ones(128)
    length = num_ref.shape[0]
    base = m * length
    whole = slice(base, base + length)
    value = qkv_ref[whole, 1024:1536].astype(F32)
    vbar = jnp.mean(value, axis=0, keepdims=True)
    vbar_ref[...] = jnp.broadcast_to(vbar, (8, 512))
    vals[...] = (value - vbar).astype(BF)
    matrix[...] = mean_rows(length, 0, length)
    for kind in range(4):
        biases[kind] = tile_bias(kind, limit)
    coarse_ref[:, 0:1024] = mm(matrix[...], qkv_ref[whole, 0:1024]).astype(BF)
    coarse_ref[:, 1024:1536] = mm(matrix[...], vals[...]).astype(BF)
    for t in range(8):
        rows = slice((t % 4) * 128, (t % 4) * 128 + 128)
        far = slice(base + (t % 4) * 128, base + (t % 4) * 128 + 128)
        kind = 0 if t < 4 else (1, 1, 2, 3)[t - 4]
        bias = biases[kind]
        for p in range(PAIRS):
            lanes = slice(p * WIDE, (p + 1) * WIDE)
            lanes_k = slice(512 + p * WIDE, 512 + (p + 1) * WIDE)
            if t < 4:
                q, k, v = qkv_ref[far, lanes], qkv_ref[far, lanes_k], vals[rows, lanes]
            else:
                q, k = coarse_ref[rows, lanes], coarse_ref[rows, lanes_k]
                v = coarse_ref[rows, 1024 + p * WIDE : 1024 + (p + 1) * WIDE]
            scores = mm_nt(q, stacked(k, masks))
            weights = jnp.exp2(scores * SCALE2 + bias).astype(BF)
            w_ref[t, :, p * 256 : (p + 1) * 256] = weights
            both = mm(weights, jnp.concatenate([stacked(v, masks), ones[...]], axis=1))
            if t < 4:
                num_ref[rows, lanes] = both[:, :WIDE]
                den_ref[rows, lanes] = both[:, WIDE:]
            else:
                num_c[rows, lanes] = both[:, :WIDE]
                den_c[rows, lanes] = both[:, WIDE:]
    matrix[...] = copy_columns(length, 0, length)
    num_ref[...] += mm_split(matrix[...], num_c[...])
    den_ref[...] += mm_split(matrix[...], den_c[...])


def fill_slots(pieces, slots, target):
    for ref, sl in zip(pieces, slots):
        for i, s in enumerate(sl):
            target[s] = ref[i]


def output_kernel(layout, ints_ref, hid_ref, att_ref, x_ref, vec_ref, *refs):
    weights, (out_ref, mark_ref, w_out, w_back) = refs[:-4], refs[-4:]
    mark_ref[...] = jnp.zeros_like(mark_ref)
    rows = layout["rows"]
    if layout["direct"]:
        for ref, sl in zip(weights, layout["wslots"]):
            for i, s in enumerate(sl):
                d = ints_ref[0] ^ s
                w_back[pl.ds(pl.multiple_of(d * 4 * rows, 4 * rows), 4 * rows), :] = ref[i, 0 : 4 * rows, :]
                w_out[pl.ds(pl.multiple_of(d * rows, rows), rows), :] = ref[i, 4 * rows : 5 * rows, :]
    else:
        w_out[...] = weights[0][...]
        w_back[...] = weights[1][...]
    for r in range(0, hid_ref.shape[0], STEP):
        part = slice(r, r + STEP)
        mixed = x_ref[part, :].astype(F32) + mm(att_ref[part, :], w_out[...])
        out_ref[part, :] = (mixed + mm(hid_ref[part, :], w_back[...]) + vec_ref[4:5, :]).astype(BF)


def take_siblings(layout, ints_ref, m, source, buf):
    for b in range(SIBS):
        if layout["direct"]:
            slot = ints_ref[layout["first_slot"] + m * SIBS + b]
            block = source[slot, m * BLOCK : (m + 1) * BLOCK, :]
        else:
            block = source[m * SIBS + b]
        buf[b * BLOCK : (b + 1) * BLOCK, :] = block


def middle_kernel(layout, ints_ref, x_ref, go_ref, rb_ref, vec_ref, bias_ref, *refs):
    local, refs = (refs[0:4], refs[4:8]), refs[8:]
    count = len(layout["slots"])
    kv_pieces, weights = refs[:count], refs[count : count + layout["n_weights"]]
    (hid_ref, gpre_ref, norm_ref, att_ref, gt_ref, gmix_ref, ghat_ref, ch_ref, cl_ref, pay_ref,
     kvr_ref, wr_ref, small_ref, sbias_ref) = refs[count + layout["n_weights"] : count + layout["n_weights"] + 14]
    scratch = refs[count + layout["n_weights"] + 14 :]
    kvs, (buf, w_out, w_in, w_back, far_num, far_den) = scratch[0], scratch[-6:]
    me = ints_ref[0]
    rows = layout["rows"]
    length = local[0][0].shape[0]
    buf[...] = jnp.zeros_like(buf)
    if layout["direct"]:
        fill_slots(kv_pieces, layout["slots"], kvs)
        for ref, sl in zip(weights, layout["wslots"]):
            for i, s in enumerate(sl):
                d = me ^ s
                at = pl.multiple_of(d * rows, rows)
                if ref.shape[1] == 5 * rows:
                    w_back[pl.ds(pl.multiple_of(d * 4 * rows, 4 * rows), 4 * rows), :] = ref[i, 0 : 4 * rows, :]
                    w_out[pl.ds(at, rows), :] = ref[i, 4 * rows : 5 * rows, :]
                else:
                    for c in range(4):
                        w_in[pl.ds(at, rows), c * 512 : (c + 1) * 512] = ref[i, c * rows : (c + 1) * rows, :]
    else:
        w_out[...] = weights[0][...]
        w_in[...] = weights[1][...]
        w_back[...] = weights[2][...]

    masks = head_masks()
    ones = head_ones(64)
    select = sibling_rows(True)
    spread = copy_columns(length, length - 32, 32)
    sums = sum_rows(length, length - 32, BLOCK)
    columns = head_columns()
    for m in range(2):
        num_ref, den_ref, vbar_ref, coarse_ref = local[m]
        vbar = vbar_ref[0:1, :]
        far_q = coarse_ref[length - 32 : length, 0:512]
        take_siblings(layout, ints_ref, m, kvs if layout["direct"] else kv_pieces[0], buf)
        remote = mm(select, buf[...])
        key_r = remote[:, 0:512].astype(BF)
        val_r = (remote[:, 512:1024].astype(BF).astype(F32) - vbar).astype(BF)
        kvr_ref[m * 64 : (m + 1) * 64, 0:512] = key_r
        kvr_ref[m * 64 : (m + 1) * 64, 512:1024] = val_r
        rb = rb_ref[m]
        nums = []
        dens = []
        for p in range(PAIRS):
            lanes = slice(p * WIDE, (p + 1) * WIDE)
            scores = mm_nt(far_q[:, lanes], stacked(key_r[:, lanes], masks))
            wr = jnp.exp2(scores * SCALE2 + rb).astype(BF)
            wr_ref[m * 32 : (m + 1) * 32, lanes] = wr
            both = mm(wr, jnp.concatenate([stacked(val_r[:, lanes], masks), ones], axis=1))
            nums.append(both[:, :WIDE])
            dens.append(both[:, WIDE:])
        far_num[...] = jnp.concatenate(nums, axis=1)
        far_den[...] = jnp.concatenate(dens, axis=1)
        for r in range(0, length, STEP):
            own = slice(r, r + STEP)
            part = slice(m * length + r, m * length + r + STEP)
            num = num_ref[own, :] + mm_split(spread[own, :], far_num[...])
            den = den_ref[own, :] + mm_split(spread[own, :], far_den[...])
            inverse_den = 1.0 / den
            centred_o = num * inverse_den
            attended = (centred_o + vbar).astype(BF)
            att_ref[part, :] = attended
            mixed = x_ref[part, :].astype(F32) + mm(attended, w_out[...])
            normal, inverse = normalize(mixed)
            normed = (normal * vec_ref[1:2, :] + vec_ref[3:4, :]).astype(BF)
            norm_ref[part, :] = normed
            top_b = go_ref[part, :]
            g_norm = jnp.zeros_like(mixed)
            def products(c):
                lanes = slice(c * CHUNK, (c + 1) * CHUNK)
                return mm(normed, w_in[:, lanes]), mm_nt(top_b, w_back[lanes, :])

            ahead = products(0)
            for c in range(2048 // CHUNK):
                lanes = slice(c * CHUNK, (c + 1) * CHUNK)
                pre, g_hidden = ahead
                if c + 1 < 2048 // CHUNK:
                    ahead = products(c + 1)
                pre = pre + bias_ref[0:1, lanes]
                cdf = 0.5 + 0.5 * lax.erf(pre * math.sqrt(0.5))
                hidden = (pre * cdf).astype(BF)
                hid_ref[part, lanes] = hidden
                slope = cdf + pre * (jnp.exp(-0.5 * pre * pre) * (1.0 / math.sqrt(2.0 * math.pi)))
                g_pre = g_hidden * slope
                total = jnp.broadcast_to(jnp.sum(g_pre, axis=0, keepdims=True), (8, CHUNK))
                sbias_ref[m, :, lanes] = total if r == 0 else sbias_ref[m, :, lanes] + total
                g_pre_b = g_pre.astype(BF)
                gpre_ref[part, lanes] = g_pre_b
                g_norm = g_norm + mm_nt(g_pre_b, w_in[:, lanes])
            top = top_b.astype(F32)
            scaled = g_norm * vec_ref[1:2, :]
            g_mixed = top + (
                scaled
                - jnp.mean(scaled, axis=-1, keepdims=True)
                - normal * jnp.mean(scaled * normal, axis=-1, keepdims=True)
            ) * inverse
            gmix_ref[part, :] = g_mixed
            total = jnp.concatenate(
                [
                    jnp.sum(g_norm * normal, axis=0, keepdims=True),
                    jnp.sum(g_norm, axis=0, keepdims=True),
                    jnp.sum(top, axis=0, keepdims=True),
                    jnp.zeros((5, 512), F32),
                ],
                axis=0,
            )
            small_ref[m] = total if r == 0 else small_ref[m] + total
            gt = g_mixed.astype(BF)
            gt_ref[part, :] = gt
            ghat = (mm_nt(gt, w_out[...]) * inverse_den).astype(BF)
            ghat_ref[part, :] = ghat
            dots = split_mm(ghat.astype(F32) * centred_o, columns)
            dots_h, dots_l = split(dots)
            ch_ref[part, :] = dots_h
            cl_ref[part, :] = dots_l
        part = slice(m * length, (m + 1) * length)
        g_sum = mm(sums, ghat_ref[part, :]).astype(BF)
        c_sum = mm(sums, ch_ref[part, :]) + mm(sums, cl_ref[part, :])
        c_sum = c_sum + split_mm(g_sum.astype(F32) * vbar, columns)
        c_h, c_l = split(c_sum)
        pay = slice(m * BLOCK, (m + 1) * BLOCK)
        pay_ref[pay, 0:512] = far_q[0:BLOCK, :]
        pay_ref[pay, 512:1024] = g_sum
        pay_ref[pay, 1024:1152] = even_columns(c_h, c_l)


def wide_in_kernel(layout, me_ref, gpre_ref, norm_ref, att_ref, gt_ref, *refs):
    rows = layout["rows"]
    up, out = refs[-2:]
    for c in range(4):
        lanes = slice(c * 512, (c + 1) * 512)
        up[:, lanes] = mm_tn(norm_ref[...], gpre_ref[:, lanes]).astype(BF)
    out[...] = mm_tn(att_ref[...], gt_ref[...]).astype(BF)
    if layout["direct"]:
        for half, ref in enumerate(refs[:2]):
            for i, s in enumerate(layout["order"]):
                at = pl.multiple_of((me_ref[0] ^ (s ^ half)) * rows, rows)
                for c in range(4):
                    ref[i, c * rows : (c + 1) * rows, :] = up[pl.ds(at, rows), c * 512 : (c + 1) * 512]
                ref[i, 4 * rows : 5 * rows, :] = out[pl.ds(at, rows), :]


def wide_back_kernel(layout, me_ref, hid_ref, go_ref, *refs):
    rows = 4 * layout["rows"]
    back = refs[-1]
    for c in range(4):
        lanes = slice(c * 512, (c + 1) * 512)
        back[lanes, :] = mm_tn(hid_ref[:, lanes], go_ref[...]).astype(BF)
    if layout["direct"]:
        for half, ref in enumerate(refs[:2]):
            for i, s in enumerate(layout["order"]):
                at = pl.multiple_of((me_ref[0] ^ (s ^ half)) * rows, rows)
                ref[i] = back[pl.ds(at, rows), :]


def back_kernel(m, qkv_ref, coarse_ref, w_ref, ghat_ref, ch_ref, cl_ref, vbar_ref, wr_ref, kvr_ref, grad_ref,
                vals, gsum, ext_f, ext_c, gcoarse, matrix, minus_ref):
    masks = head_masks()
    length = vals.shape[0]
    base = m * length
    whole = slice(base, base + length)
    vals[...] = (qkv_ref[whole, 1024:1536].astype(F32) - vbar_ref[0:1, :]).astype(BF)
    matrix[...] = sum_rows(length, 0, length)
    for p in range(PAIRS):
        minus_ref[p] = minus_columns(p, 128)
    gsum[...] = mm(matrix[...], ghat_ref[whole, :]).astype(BF)
    c_sum = mm(matrix[...], ch_ref[whole, :]) + mm(matrix[...], cl_ref[whole, :])
    c_h, c_l = split(c_sum)
    ext_c[...] = even_columns(c_h, c_l)
    ext_f[...] = even_columns(ch_ref[whole, :], cl_ref[whole, :])
    zero = jnp.zeros((128, WIDE), BF)
    for t in range(8):
        rows = slice((t % 4) * 128, (t % 4) * 128 + 128)
        far = slice(base + (t % 4) * 128, base + (t % 4) * 128 + 128)
        for p in range(PAIRS):
            lanes = slice(p * WIDE, (p + 1) * WIDE)
            lanes_k = slice(512 + p * WIDE, 512 + (p + 1) * WIDE)
            lanes_v = slice(1024 + p * WIDE, 1024 + (p + 1) * WIDE)
            if t < 4:
                q, k, v = qkv_ref[far, lanes], qkv_ref[far, lanes_k], vals[rows, lanes]
                g, ext = ghat_ref[far, lanes], ext_f[rows, :]
            else:
                q, k, v = coarse_ref[rows, lanes], coarse_ref[rows, lanes_k], coarse_ref[rows, lanes_v]
                g, ext = gsum[rows, lanes], ext_c[rows, :]
            weights = w_ref[t, :, p * 256 : (p + 1) * 256]
            left = jnp.concatenate([g, ext], axis=1)
            right = jnp.concatenate([stacked(v, masks), minus_ref[p]], axis=1)
            gs = (weights.astype(F32) * mm_nt(left, right)).astype(BF)
            g_q = mm(gs, stacked(k, masks)) * SCALE
            g_kv = mm_tn(
                jnp.concatenate([gs, weights], axis=0),
                jnp.concatenate([jnp.concatenate([q, zero], axis=1), jnp.concatenate([zero, g], axis=1)], axis=0),
            )
            g_k = unstacked(g_kv[:, :WIDE], masks) * SCALE
            g_v = unstacked(g_kv[:, WIDE:], masks)
            if t < 4:
                grad_ref[rows, lanes] = g_q
                grad_ref[rows, lanes_k] = g_k
                grad_ref[rows, lanes_v] = g_v
            else:
                gcoarse[rows, lanes] = g_q.astype(BF)
                gcoarse[rows, lanes_k] = g_k.astype(BF)
                gcoarse[rows, lanes_v] = g_v.astype(BF)
    far = slice(480, 512)
    for p in range(PAIRS):
        lanes = slice(p * WIDE, (p + 1) * WIDE)
        left = jnp.concatenate([gsum[far, lanes], ext_c[far, :]], axis=1)
        minus = minus_columns(p, 64)
        part = slice(m * 64, (m + 1) * 64)
        right = jnp.concatenate([stacked(kvr_ref[part, 512 + p * WIDE : 512 + (p + 1) * WIDE], masks), minus], axis=1)
        gs = (wr_ref[m * 32 : (m + 1) * 32, lanes].astype(F32) * mm_nt(left, right)).astype(BF)
        gcoarse[far, lanes] = (mm(gs, stacked(kvr_ref[part, lanes], masks)) * SCALE).astype(BF)
    matrix[...] = share_columns(length, 0, length)
    grad_ref[...] += mm(matrix[...], gcoarse[...])


def last_kernel(layout, ints_ref, x_ref, gmix_ref, w_ref, vec_ref, rb_ref, small_ref, sbias_ref, *refs):
    local, refs = (refs[0:3], refs[3:6]), refs[6:]
    count = len(layout["slots"])
    pieces = refs[:count]
    if layout["direct"]:
        ingrad_ref, *blocks, slots_v, buf, gqkv, wgrad = refs[count:]
    else:
        ingrad_ref, wgrad, tail_ref, buf, gqkv = refs[count:]
    me = ints_ref[0]
    rows = layout["rows"]
    devices = layout["devices"]
    masks = head_masks()
    if layout["direct"]:
        fill_slots(pieces, layout["slots"], slots_v)
    buf[...] = jnp.zeros_like(buf)
    length = x_ref.shape[0] // 2
    lane = lax.broadcasted_iota(jnp.int32, (1, 128), 1)
    select, select_sum = sibling_rows(True), sibling_rows(False)
    spread = share_columns(length, length - 32, 32)
    columns, twins = head_columns(), twin_columns()
    for m in range(2):
        grad_ref, coarse_ref, vbar_ref = local[m]
        vbar = vbar_ref[0:1, :]
        take_siblings(layout, ints_ref, m, slots_v if layout["direct"] else pieces[0], buf)
        q_r = mm(select, buf[:, 0:512]).astype(BF)
        g_r = mm(select_sum, buf[:, 512:1024]).astype(BF)
        c_r = mm_split(select_sum, mm(buf[:, 1024:1152], twins))
        c_r = c_r - split_mm(g_r.astype(F32) * vbar, columns)
        c_h, c_l = split(c_r)
        ext = even_columns(c_h, c_l).astype(F32)
        rb = rb_ref[m]
        g_keys = []
        g_vals = []
        for p in range(PAIRS):
            lanes = slice(p * WIDE, (p + 1) * WIDE)
            k = coarse_ref[length - 32 : length, 512 + p * WIDE : 512 + (p + 1) * WIDE]
            v = coarse_ref[length - 32 : length, 1024 + p * WIDE : 1024 + (p + 1) * WIDE]
            qq = stacked(q_r[:, lanes], masks)
            gg = stacked(g_r[:, lanes], masks)
            weights = jnp.exp2(mm_nt(k, qq) * SCALE2 + rb)
            ones_a = ((lane // 2) == 4 * p).astype(F32)
            ones_b = ((lane // 2) == 4 * p + 1).astype(F32)
            ext_p = jnp.concatenate([ext * ones_a, ext * ones_b], axis=0).astype(BF)
            left = jnp.concatenate([v, jnp.full((32, 128), -1.0, BF)], axis=1)
            gs = (weights * mm_nt(left, jnp.concatenate([gg, ext_p], axis=1))).astype(BF)
            g_keys.append(mm(gs, qq) * SCALE)
            g_vals.append(mm(weights.astype(BF), gg))
        extra = mm_split(spread, jnp.concatenate(g_keys + g_vals, axis=1))
        part = slice(m * length, (m + 1) * length)
        gqkv[part, 0:512] = grad_ref[:, 0:512].astype(BF)
        gqkv[part, 512:1536] = (grad_ref[:, 512:1536] + extra).astype(BF)
    g_norm = mm_nt(gqkv[...], w_ref[...])
    normal, inverse = normalize(x_ref[...].astype(F32))
    normed = (normal * vec_ref[0:1, :] + vec_ref[2:3, :]).astype(BF)
    scaled = g_norm * vec_ref[0:1, :]
    ingrad_ref[...] = gmix_ref[...] + (
        scaled
        - jnp.mean(scaled, axis=-1, keepdims=True)
        - normal * jnp.mean(scaled * normal, axis=-1, keepdims=True)
    ) * inverse
    for part in range(3):
        lanes = slice(part * 512, (part + 1) * 512)
        wgrad[:, lanes] = mm_tn(normed, gqkv[:, lanes]).astype(BF)
    vectors = [
        jnp.sum(g_norm * normal, axis=0, keepdims=True),
        small_ref[0, 0:1, :] + small_ref[1, 0:1, :],
        jnp.sum(g_norm, axis=0, keepdims=True),
        small_ref[0, 1:2, :] + small_ref[1, 1:2, :],
        small_ref[0, 2:3, :] + small_ref[1, 2:3, :],
    ]
    bias = sbias_ref[0, 0:1, :] + sbias_ref[1, 0:1, :]
    halves = ((0, 0), (1, 1)) if layout["direct"] else ((None, None),)
    for half, _ in halves:
        order = list(layout["order"]) if half is not None else list(range(devices))
        owner = slot_numbers(order, (len(order), 1), 0)
        if half is not None:
            owner = (owner ^ half) ^ me
        tail = gather_small(vectors, bias, owner, devices)
        if half is None:
            tail_ref[...] = tail
            continue
        first, second = blocks[2 * half : 2 * half + 2]
        for i, s in enumerate(order):
            at = pl.multiple_of((me ^ (s ^ half)) * rows, rows)
            for part in range(2):
                first[i, part * rows : (part + 1) * rows, :] = wgrad[pl.ds(at, rows), part * 512 : (part + 1) * 512]
            second[i, 0:rows, :] = wgrad[pl.ds(at, rows), 1024:1536]
            second[i, rows : rows + 8, 0:256] = jnp.broadcast_to(tail[i : i + 1, :], (8, 256)).astype(BF)
            second[i, rows : rows + 8, 256:512] = jnp.zeros((8, 256), BF)


def gather_small(vectors, bias, owner, devices):
    w = 512 // devices
    wide = 2048 // devices
    count = owner.shape[0]
    col = lax.broadcasted_iota(jnp.int32, (count, 512), 1)
    mine = (col // w == owner).astype(F32)
    col_t = lax.broadcasted_iota(jnp.int32, (512, 128), 0)
    lane_t = lax.broadcasted_iota(jnp.int32, (512, 128), 1)
    total = jnp.zeros((count, 128), F32)
    for p, row in enumerate(vectors):
        place = ((lane_t // w == p) & (lane_t % w == col_t % w)).astype(F32).astype(BF)
        total = total + split_mm(row * mine, place)
    col_w = lax.broadcasted_iota(jnp.int32, (count, 2048), 1)
    mine_w = (col_w // wide == owner).astype(F32)
    col_tw = lax.broadcasted_iota(jnp.int32, (2048, 128), 0)
    lane_tw = lax.broadcasted_iota(jnp.int32, (2048, 128), 1)
    place_w = (lane_tw == col_tw % wide).astype(F32).astype(BF)
    return jnp.concatenate([total, split_mm(bias * mine_w, place_w)], axis=1)


def total_of(refs, rows):
    total = refs[0][0, rows, :].astype(F32)
    for r in refs[1:]:
        total = total + r[0, rows, :].astype(F32)
    return total


def finish_wide_kernel(rows, *refs):
    ins, (back_ref, in_ref, out_ref) = refs[:-3], refs[-3:]
    for c in range(4):
        in_ref[:, c * 512 : (c + 1) * 512] = total_of(ins, slice(c * rows, (c + 1) * rows))
    out_ref[...] = total_of(ins, slice(4 * rows, 5 * rows))
    back_ref[...] = total_of(ins, slice(5 * rows, 9 * rows))


def finish_qkv_kernel(rows, *refs):
    ins, (q_ref, k_ref, v_ref, gain_ref, shift_ref, bi_ref, bo_ref) = refs[:-7], refs[-7:]
    for part, ref in enumerate((q_ref, k_ref, v_ref)):
        ref[...] = total_of(ins, slice(part * rows, (part + 1) * rows))
    tail = total_of(ins, slice(3 * rows, 3 * rows + 8))[0:1]
    for r in range(2):
        gain_ref[r : r + 1, :] = tail[:, r * rows : (r + 1) * rows]
        shift_ref[r : r + 1, :] = tail[:, (2 + r) * rows : (3 + r) * rows]
    bo_ref[...] = tail[:, 4 * rows : 5 * rows]
    bi_ref[...] = tail[:, 128 : 128 + bi_ref.shape[1]]


def remote_plan(lengths, group_order, position, devices, length):
    count = lengths.shape[1]
    lower = np.tril(np.ones((count, count), np.int32))
    seq_ends = jnp.sum(lengths[:, None, :] * lower[None], axis=2)
    device_ids = np.arange(devices, dtype=np.int32)
    group_id = jnp.sum(jnp.where(device_ids == position, group_order, 0), axis=1)[:, None]
    level_s = np.repeat(np.arange(4, dtype=np.int32), [1, 2, 4, 8])
    index_s = np.concatenate([np.arange(1 << level, dtype=np.int32) for level in range(4)])
    siblings = (((group_id >> level_s) ^ 1) << level_s) + index_s
    owner = jnp.sum(jnp.where(group_order[:, None, :] == siblings[:, :, None], device_ids, 0), axis=2)
    level_q = np.full((32,), -1, np.int32)
    start_q = np.zeros((32,), np.int32)
    row = 0
    for level in range(4):
        for i in range(length // (32 << level)):
            level_q[row] = level
            start_q[row] = i * (32 << level)
            row += 1
    level_k = np.tile(np.repeat(np.arange(4, dtype=np.int32), BLOCK), 2)
    start_k = np.tile(np.arange(BLOCK, dtype=np.int32), 8) * (32 << level_k)
    first_k = (((group_id >> level_k) ^ 1) << level_k) * length
    starts = np.concatenate([start_q, np.array([0, length // 2], np.int32)])
    places = jnp.concatenate([first_k + start_k, group_id * length + starts], axis=1)
    seq = jnp.sum((places[:, :, None] >= seq_ends[:, None, :]).astype(jnp.int32), axis=2)
    same = (seq[:, 128:160, None] == seq[:, None, :128]) & (level_q[:, None] == level_k[None, :])
    bias = jnp.where(same, (level_k + 5).astype(np.float32), OFF)
    apart = (seq[:, 160] != seq[:, 161]).astype(jnp.int32)
    ints = jnp.concatenate([jnp.reshape(position, (1,)), (owner ^ position).reshape(-1), apart]).astype(jnp.int32)
    return ints, bias


def exchange_order(stack, position, devices):
    rest = stack.shape[1:]
    for bit in range(devices.bit_length() - 1):
        cut = stack.reshape((devices >> (bit + 1), 2, 1 << bit) + rest)
        stack = jnp.where((position >> bit) & 1 > 0, cut[:, ::-1], cut).reshape((devices,) + rest)
    return stack


def reordered(stack, order):
    return jnp.concatenate([stack[int(i) : int(i) + 1] for i in order], axis=0)


def natural(pieces, position, devices):
    order = [s for _, sl in pieces for s in sl]
    stack = jnp.concatenate([p for p, _ in pieces], axis=0)
    return exchange_order(reordered(stack, np.argsort(np.array(order))), position, devices)


def picked(pieces, ints, micro_n):
    order = [s for _, sl in pieces for s in sl]
    stack = reordered(jnp.concatenate([p for p, _ in pieces], axis=0), np.argsort(np.array(order)))
    blocks = []
    for m in range(micro_n):
        for b in range(SIBS):
            block = lax.dynamic_slice_in_dim(stack, ints[1 + m * SIBS + b], 1, axis=0)
            blocks.append(block[:, m * BLOCK : (m + 1) * BLOCK])
    return jnp.concatenate(blocks, axis=0)


def on_device(
    layer_in,
    out_grad,
    lengths,
    group_order,
    w_query,
    w_key,
    w_value,
    w_out,
    w_in,
    w_back,
    norm_gain,
    norm_shift,
    ffn_bias_in,
    ffn_bias_out,
):
    devices = lax.axis_size("fsdp")
    position = lax.axis_index("fsdp")
    micro_n, length, width = layer_in.shape
    hidden_n = w_in.shape[1]
    tokens = micro_n * length
    rows = w_query.shape[0]
    half = devices // 2
    direct = rows % 16 == 0
    x = layer_in.reshape(tokens, width)
    top = out_grad.reshape(tokens, width)

    small_rows = -(-3 * rows // 8) * 8
    biases = (ffn_bias_in.reshape(1, -1), ffn_bias_out.reshape(1, -1))
    if direct:
        shards = (w_query, w_key, w_value, w_out, w_in, w_back, norm_gain, norm_shift, *biases)
        packed, packed_w = pl.pallas_call(
            lambda *refs: pack_kernel(rows, *refs),
            grid=(1,),
            in_specs=[pl.BlockSpec(a.shape, lambda i: (0, 0)) for a in shards],
            out_specs=[pl.BlockSpec(memory_space=pltpu.VMEM)] * 2,
            out_shape=[shape_of((3 * rows + 8, width), BF), shape_of((9 * rows, width), BF)],
            name="pack",
        )(*shards)
    else:
        tail = jnp.concatenate(
            [
                norm_gain.reshape(-1),
                norm_shift.reshape(-1),
                ffn_bias_out,
                jnp.zeros((128 - 5 * rows,), BF),
                ffn_bias_in,
                jnp.zeros((384 - ffn_bias_in.shape[0],), BF),
            ]
        )
        packed = jnp.concatenate(
            [
                w_query,
                w_key,
                w_value,
                jnp.zeros((small_rows - 3 * rows, width), BF),
                jnp.broadcast_to(tail[None, :], (8, width)),
            ],
            axis=0,
        )
        packed_w = jnp.concatenate(
            [w_back, w_out] + [w_in[:, c * width : (c + 1) * width] for c in range(hidden_n // width)], axis=0
        )
    marks_q, marks_w = [], []
    pieces_q = core_gather(staged_gather(packed, devices, marks=marks_q), devices)
    lengths, group_order = follow((lengths, group_order), marks_q[0])
    pieces_bo, pieces_in = crossed_gather(packed_w, 5 * rows, devices, marks_w, [])
    ints, remote_bias = remote_plan(lengths, group_order, position, devices, length)

    layout = {
        "rows": rows,
        "devices": devices,
        "direct": direct,
        "small": small_rows,
        "slots": [sl for _, sl in pieces_q],
        "first_slot": 1,
        "order": scatter_order(devices),
    }
    flag_at = 1 + micro_n * SIBS
    arrays_q = [p for p, _ in pieces_q]
    if not direct:
        nat = natural(pieces_q, position, devices)
        arrays_q.append(
            jnp.concatenate([nat[:, part * rows : (part + 1) * rows].reshape(width, width) for part in range(3)], axis=1)
        )
    me = jnp.reshape(position, (1,)).astype(jnp.int32)
    qkv, w_qkv, vectors, bias_row, coarse_kv = call(
        lambda *refs: first_kernel(layout, *refs),
        "norm_qkv",
        [
            ((tokens, 3 * width), BF),
            ((width, 3 * width), BF),
            ((8, width), F32),
            ((8, hidden_n), F32),
            ((micro_n * BLOCK, 2 * width), BF),
        ],
        (ints, x, *arrays_q),
        scalars=1,
        mib=12,
        us=5.0,
    )

    local = [
        call(
            lambda *refs, m=m: local_kernel(m, flag_at, *refs),
            f"local_forward_{m}",
            [
                ((length, width), F32),
                ((length, width), F32),
                ((length, 3 * width), BF),
                ((8, 128, 256 * PAIRS), BF),
                ((8, width), F32),
            ],
            (ints, qkv),
            scalars=1,
            scratch=[
                ((length, width), BF),
                ((length, width), F32),
                ((length, width), F32),
                ((256, WIDE), BF),
                ((length, length), BF),
                ((4, 128, 256), F32),
            ],
            mib=12,
            us=4.0,
            after=marks_w if m == 0 else (),
        )
        for m in range(micro_n)
    ]

    pieces_kv = staged_gather(coarse_kv, devices, [(local[0][4], *marks_w), (local[1][4],)])
    pieces_kv = core_gather(pieces_kv, devices)
    arrays_kv = [p for p, _ in pieces_kv] if direct else [picked(pieces_kv, ints, micro_n)]
    if direct:
        weights_in = [p for p, _ in pieces_bo + pieces_in]
    else:
        nat_bo, nat_in = natural(pieces_bo, position, devices), natural(pieces_in, position, devices)
        weights_in = [
            nat_bo[:, 4 * rows :].reshape(width, width),
            jnp.concatenate([nat_in[:, c * rows : (c + 1) * rows].reshape(width, width) for c in range(4)], axis=1),
            nat_bo[:, : 4 * rows].reshape(hidden_n, width),
        ]
    layout_m = dict(
        layout,
        slots=[sl for _, sl in pieces_kv][: len(arrays_kv)],
        wslots=[sl for _, sl in pieces_bo + pieces_in],
        n_weights=len(weights_in),
    )
    per_local = [a for num, den, coarse, _, vbar in local for a in (num, den, vbar, coarse)]
    (hidden, g_pre, normed_two, attended, gt, g_mixed, ghat, dots_h, dots_l, payload, far_kv, far_w,
     small_sums, bias_sums) = call(
        lambda *refs: middle_kernel(layout_m, *refs),
        "middle",
        [
            ((tokens, hidden_n), BF),
            ((tokens, hidden_n), BF),
            ((tokens, width), BF),
            ((tokens, width), BF),
            ((tokens, width), BF),
            ((tokens, width), F32),
            ((tokens, width), BF),
            ((tokens, 128), BF),
            ((tokens, 128), BF),
            ((micro_n * BLOCK, 2 * width + 128), BF),
            ((micro_n * 64, 2 * width), BF),
            ((micro_n * 32, width), BF),
            ((micro_n, 8, width), F32),
            ((micro_n, 8, hidden_n), F32),
        ],
        (ints, x, top, remote_bias, vectors, bias_row, *per_local, *arrays_kv, *weights_in),
        scalars=1,
        scratch=[((devices, micro_n * BLOCK, 2 * width), BF)] * direct
        + [
            ((256, 2 * width), BF),
            ((width, width), BF),
            ((width, hidden_n), BF),
            ((hidden_n, width), BF),
            ((32, width), F32),
            ((32, width), F32),
        ],
        mib=30,
        us=20.0,
    )

    order = np.array(layout["order"], np.int32)
    stages = bit_groups(devices)[::-1]

    def halves(stack):
        stack = exchange_order(stack, position, devices)
        return reordered(stack, order), reordered(stack, order ^ 1)

    def wide_grads(body, name, ins, plain, count, after):
        blocks = [((half, count, width), BF)] * 2
        return call(
            lambda *refs: body(layout, *refs),
            name,
            blocks if direct else plain,
            ins,
            scalars=1,
            scratch=plain if direct else (),
            mib=12,
            us=3.0,
            after=after,
        )

    begun = first_sends(payload, devices)
    grads_a = wide_grads(
        wide_in_kernel,
        "wide_in",
        (me, g_pre, normed_two, attended, gt),
        [((width, hidden_n), BF), ((width, width), BF)],
        5 * rows,
        (begun[1],),
    )
    grads_b = wide_grads(
        wide_back_kernel, "wide_back", (me, hidden, top), [((hidden_n, width), BF)], 4 * rows, (begun[1],)
    )
    pieces_g = staged_gather(payload, devices, [(grads_a[0], grads_b[0])], begun=begun)
    if direct:
        keeps, sents = (grads_a[0], grads_b[0]), (grads_a[1], grads_b[1])
    else:
        g_in, g_out = grads_a
        stack = [g_in[:, c * width : (c + 1) * width].reshape(devices, rows, width) for c in range(4)]
        stack = jnp.concatenate(stack + [g_out.reshape(devices, rows, width)], axis=1)
        keeps, sents = zip(halves(stack), halves(grads_b[0].reshape(devices, 4 * rows, width)))
    arrived = [send(a, 1, devices) for a in sents]

    def local_backward(m, after):
        return call(
            lambda *refs: back_kernel(m, *refs),
            f"local_backward_{m}",
            [((length, 3 * width), F32)],
            (qkv, local[m][2], local[m][3], ghat, dots_h, dots_l, local[m][4], far_w, far_kv),
            scratch=[
                ((length, width), BF),
                ((length, width), BF),
                ((length, 128), BF),
                ((length, 128), BF),
                ((length, 3 * width), BF),
                ((length, length), BF),
                ((PAIRS, 256, 128), BF),
            ],
            mib=12,
            us=8.0,
            after=after,
        )[0]

    grads = [local_backward(0, tuple(sents))]
    held_w, received_w = scatter_step(keeps, [arrived], stages[0], devices, "add_wide_0", (grads[0],))
    pieces_g = core_gather(pieces_g, devices, held_w)
    arrivals = [p for p, _ in pieces_g]
    grads.append(local_backward(1, (*held_w, *arrivals)))

    arrays_g = [p for p, _ in pieces_g] if direct else [picked(pieces_g, ints, micro_n)]
    layout_l = dict(layout, slots=[sl for _, sl in pieces_g][: len(arrays_g)])
    per_local = [a for m in range(micro_n) for a in (grads[m], local[m][2], local[m][4])]
    last_in = (ints, x, g_mixed, w_qkv, vectors, remote_bias, small_sums, bias_sums, *per_local, *arrays_g)
    scratch = [((devices, micro_n * BLOCK, 2 * width + 128), BF)] * direct + [
        ((256, 2 * width + 128), BF),
        ((tokens, 3 * width), BF),
    ]
    mib = 20
    if direct:
        in_grad, *blocks = call(
            lambda *refs: last_kernel(layout_l, *refs),
            "qkv_grads",
            [((tokens, width), F32)] + [((half, 2 * rows, width), BF), ((half, rows + 8, width), BF)] * 2,
            last_in,
            scalars=1,
            scratch=scratch + [((width, 3 * width), BF)],
            mib=mib,
            us=10.0,
        )
    else:
        in_grad, g_qkv, tails = call(
            lambda *refs: last_kernel(layout_l, *refs),
            "qkv_grads",
            [((tokens, width), F32), ((width, 3 * width), BF), ((devices, 256), F32)],
            last_in,
            scalars=1,
            scratch=scratch,
            mib=mib,
            us=10.0,
        )
        stack = jnp.concatenate(
            [g_qkv[:, c * width : (c + 1) * width].reshape(devices, rows, width) for c in range(3)]
            + [jnp.broadcast_to(jnp.pad(tails, ((0, 0), (0, 256)))[:, None, :], (devices, 8, width)).astype(BF)],
            axis=1,
        )
        blocks = [a[:, cut] for a in halves(stack) for cut in (slice(0, 2 * rows), slice(2 * rows, None))]
    keep_q, sent_q = blocks[:2], blocks[2:]
    given = [p for p, _ in pieces_bo] if direct else [weights_in[0], weights_in[2]]
    layer_out, mark = call(
        lambda *refs: output_kernel(layout_m, *refs),
        "layer_out",
        [((tokens, width), BF), ((8, 128), F32)],
        (me, hidden, attended, x, vectors, *given),
        scalars=1,
        scratch=[((width, width), BF), ((hidden_n, width), BF)],
        mib=12,
        us=3.0,
        after=(keep_q[0],),
    )
    received_q = [[send(a, 1, devices) for a in sent_q]]
    held_q = keep_q
    for stage, group in enumerate(stages):
        if stage + 1 < len(stages):
            late = (mark,) if stage == 0 else held_q
            held_w, received_w = scatter_step(held_w, received_w, stages[stage + 1], devices, f"add_wide_{stage + 1}", late)
        held_q, received_q = scatter_step(held_q, received_q, group, devices, f"add_qkv_{stage}", held_w if stage == 0 else ())
    g_back, g_in, g_out = call(
        lambda *refs: finish_wide_kernel(rows, *refs),
        "finish_wide",
        [((4 * rows, width), F32), ((rows, hidden_n), F32), ((rows, width), F32)],
        (*held_w, *(r for (r,) in received_w)),
        mib=4,
        us=1.0,
    )
    g_query, g_key, g_value, g_gain, g_shift, g_bias_in, g_bias_out = call(
        lambda *refs: finish_qkv_kernel(rows, *refs),
        "finish_qkv",
        [((rows, width), F32)] * 3
        + [((2, rows), F32)] * 2
        + [((1, hidden_n // devices), F32), ((1, rows), F32)],
        (*held_q, *(r for (r,) in received_q)),
        mib=4,
        us=1.0,
    )
    return (
        layer_out.reshape(micro_n, length, width),
        in_grad.reshape(micro_n, length, width),
        g_query,
        g_key,
        g_value,
        g_out,
        g_in,
        g_back,
        g_gain,
        g_shift,
        g_bias_in.reshape(-1),
        g_bias_out.reshape(-1),
    )


def solution(mesh):
    placed = (
        P(None, "fsdp", None),
        P(None, "fsdp", None),
        P(),
        P(),
        P("fsdp", None),
        P("fsdp", None),
        P("fsdp", None),
        P("fsdp", None),
        P("fsdp", None),
        P("fsdp", None),
        P(None, "fsdp"),
        P(None, "fsdp"),
        P("fsdp"),
        P("fsdp"),
    )
    return jax.shard_map(
        on_device,
        mesh=mesh,
        in_specs=placed,
        out_specs=(
            P(None, "fsdp", None),
            P(None, "fsdp", None),
            P("fsdp", None),
            P("fsdp", None),
            P("fsdp", None),
            P("fsdp", None),
            P("fsdp", None),
            P("fsdp", None),
            P(None, "fsdp"),
            P(None, "fsdp"),
            P("fsdp"),
            P("fsdp"),
        ),
        check_vma=False,
    )
```
